512 devices in a mesh: bus: 8 (over y), line: 8 (over x, core), scen: 8 (over z).
Axes of the slice: x: 4, y: 8, z: 8, core: 2. Of those that a mesh axis runs over, the one named last changes fastest.
Arguments:
- shift_factors: bfloat16 [12288, 8192], P('line', 'bus'), may hold values from -0.0625 to 0.0625
- net_load: bfloat16 [512, 8, 8192], P('scen', None, 'bus'), may hold values from -6 to 6
- dispatch_level: float32 [512, 8], P('scen'), may hold values from 0.3 to 1.5
- scenario_weight: float32 [512], P('scen'), may hold values from 0.5 to 2
- cluster_id: int32 [512, 1], P('scen'), may hold values from 0 to 63
- commitment: int32 [8, 4096], P(None, 'bus'), may hold values 0 or 1
- unit_capacity: float32 [4096], P('bus'), may hold values from 0.5 to 4
- unit_bus: int32 [4096], P('bus'), may hold values from 0 to 8191
- line_limit: float32 [12288], P('line'), may hold values from 0.3 to 1.5
- multipliers: float32 [64, 12288], P('scen', 'line'), may hold values from 0 to 1
- penalty_target: float32 [64], P('scen'), may hold values from 1 to 16
Outputs:
- new_multipliers: float32 [64, 12288], P('scen', 'line')
- cut_slopes: float32 [64, 8, 8192], P(('line', 'scen'), None, 'bus')
The draws below stay inside these ranges and needn't reach their ends.
All inputs are finite; a program needn't handle non-finite values. No bound on the sum of `commitment` on one device may be relied on, other than what follows from the above.
Results may differ from the reference program's by a relative error of at most 0.0011.
Values may be sent and summed in bfloat16 or wider, within the bound.
No kernel may reach another device: no remote copies, remote signals or barrier semaphores. Data moves between devices by JAX's collectives and lax.ppermute only.
A program may use at most 64 MiB of HBM per device.

```python
import math
import jax
import jax.numpy as jnp
from jax import lax

BUSES = 8192
LINES = 12288
GENS = 4096
CLUSTERS = 64
HOURS = 8
SCEN = 512


def with_ends(entries, stream_key, least, largest):
    shape = entries.shape
    spot = [jax.random.randint(jax.random.fold_in(stream_key, axis), (), 0, shape[axis]) for axis in range(len(shape))]
    entries = entries.at[tuple(spot)].set(least)
    longest = shape.index(max(shape))
    spot[longest] = (spot[longest] + 1) % shape[longest]
    return entries.at[tuple(spot)].set(largest)


def level_of(own_key, dims, shards, least, largest):
    factor_of, own = 1.0, jax.random.fold_in(own_key, 6)
    for axis_at, parts in shards:
        draws = jnp.exp(jax.random.uniform(jax.random.fold_in(own, axis_at), (parts,), jnp.float32, least / len(shards), largest / len(shards)))
        factor_of = factor_of * jnp.repeat(draws, dims[axis_at] // parts).reshape([-1 if axis == axis_at else 1 for axis in range(len(dims))])
    return factor_of


def different_ones(key, rows, amount, top, lift):
    order = jax.random.permutation(jax.random.fold_in(key, 1), amount)
    favour = order
    for power in range(3):
        favour = favour * favour // amount
    favour = favour * lift // amount
    chance = jax.random.randint(jax.random.fold_in(key, 2), (rows, amount), 0, 4096) + favour
    fixed_rows = jax.random.permutation(jax.random.fold_in(key, 3), rows)[jnp.arange(amount) % rows]
    chance = jnp.where(jnp.arange(rows)[:, None] == fixed_rows[None, :], 1 << 14, chance)
    priority = chance * amount + jnp.arange(amount)
    return lax.top_k(priority.astype(jnp.int32), top)[1].astype(jnp.int32)


def gaussian(key, dims, spread, limit, pieces=(), kind=jnp.bfloat16):
    entries = jax.random.normal(key, dims, jnp.float32) * spread
    if len(pieces) > 0:
        entries = level_of(key, dims, pieces, -0.22, 0.18) * entries
    return jnp.clip(entries, min=-limit, max=limit).astype(kind)


def setup_inputs(seed: int = 0) -> dict:
    keys = jax.random.split(jax.random.key(seed), 12)
    return {
        "shift_factors": gaussian(keys[0], (LINES, BUSES), BUSES ** -0.5, 0.0625, ((0, 8), (1, 8))),
        "net_load": gaussian(keys[1], (SCEN, HOURS, BUSES), 1.0, 6.0, ((0, 8), (2, 8))),
        "dispatch_level": jnp.clip(jnp.exp(math.log(1.5) - 1.60943787 * jax.random.uniform(keys[2], (SCEN, HOURS), jnp.float32) ** level_of(keys[2], (SCEN, HOURS), ((0, 8),), -0.2, 0.2)), 0.3, 1.5),
        "scenario_weight": jnp.clip(jnp.exp(math.log(2.0) - 1.3862944 * jax.random.uniform(keys[3], (SCEN,), jnp.float32) ** level_of(keys[3], (SCEN,), ((0, 8),), -0.2, 0.2)), 0.5, 2.0),
        "cluster_id": different_ones(keys[4], SCEN, CLUSTERS, 1, 256),
        "commitment": with_ends((jax.random.randint(keys[5], (HOURS, GENS), 0, 4) < 3).astype(jnp.int32), jax.random.fold_in(keys[5], 1), 0, 1),
        "unit_capacity": jnp.clip(jnp.exp(math.log(4.0) - 2.0794415 * jax.random.uniform(keys[6], (GENS,), jnp.float32) ** level_of(keys[6], (GENS,), ((0, 8),), -0.2, 0.2)), 0.5, 4.0),
        "unit_bus": with_ends(jax.random.randint(keys[7], (GENS,), 0, BUSES), jax.random.fold_in(keys[7], 1), 0, BUSES - 1).astype(jnp.int32),
        "line_limit": jnp.clip(0.3 + 1.2 * jax.random.uniform(keys[8], (LINES,), jnp.float32) ** level_of(keys[8], (LINES,), ((0, 8),), -0.2, 0.2), 0.3, 1.5),
        "multipliers": jnp.clip(1.0 * jax.random.uniform(keys[9], (CLUSTERS, LINES), jnp.float32) ** level_of(keys[9], (CLUSTERS, LINES), ((0, 8), (1, 8)), -0.2, 0.2), 0.0, 1.0),
        "penalty_target": jnp.clip(jnp.exp(math.log(16.0) - 2.7725887 * jax.random.uniform(keys[10], (CLUSTERS,), jnp.float32) ** level_of(keys[10], (CLUSTERS,), ((0, 8),), -0.2, 0.2)), 1.0, 16.0),
    }


step_size = 0.1


def reference(shift_factors, net_load, dispatch_level, scenario_weight, cluster_id, commitment, unit_capacity, unit_bus, line_limit, multipliers, penalty_target):
    highest = lax.Precision.HIGHEST
    values = commitment.astype(jnp.float32) * unit_capacity[None, :]
    capacity = jax.ops.segment_sum(values.T, unit_bus, num_segments=BUSES).T
    injection = (capacity[None, :, :] * dispatch_level[:, :, None] - net_load.astype(jnp.float32)).astype(jnp.bfloat16)
    factors = shift_factors.astype(jnp.float32)
    inject_flat = injection.reshape(SCEN * HOURS, BUSES).astype(jnp.float32)
    flow = lax.dot_general(factors, inject_flat, (((1,), (1,)), ((), ())), precision=highest)
    flow_cube = flow.reshape(LINES, SCEN, HOURS)
    bounds = line_limit[:, None, None]
    excess = flow_cube - jnp.clip(flow_cube, -bounds, bounds)
    penalty = 0.5 * jnp.sum(excess * excess, axis=2) * scenario_weight[None, :]
    member = (cluster_id[:, 0:1] == jnp.arange(CLUSTERS).astype(jnp.int32)[None, :]).astype(jnp.float32)
    pooled = jnp.dot(member.T, penalty.T, precision=highest)
    new_multipliers = jnp.maximum(multipliers + step_size * (pooled - penalty_target[:, None]), 0.0)
    chosen = jnp.dot(member, new_multipliers, precision=highest)
    push = (excess * (chosen.T * scenario_weight[None, :])[:, :, None]).astype(jnp.bfloat16)
    push_flat = push.reshape(LINES, SCEN * HOURS).astype(jnp.float32)
    sensitivity = lax.dot_general(push_flat, factors, (((0,), (0,)), ((), ())), precision=highest)
    scaled = (sensitivity.reshape(SCEN, HOURS, BUSES) * dispatch_level[:, :, None]).reshape(SCEN, HOURS * BUSES)
    cut_slopes = jnp.dot(member.T, scaled, precision=highest).reshape(CLUSTERS, HOURS, BUSES)
    return new_multipliers, cut_slopes
```

```python
import jax
import jax.numpy as jnp
from jax import lax
from jax.experimental import pallas as pl
from jax.experimental.pallas import tpu as pltpu
from jax.sharding import PartitionSpec as P


BUS_AXIS = 8
LINE_AXIS = 8
SCEN_AXIS = 8
LINES = 1536
SHARE = LINES // BUS_AXIS
BUSES = 1024
SCEN = 64
HOURS = 8
COLS = SCEN * HOURS
UNITS = 4096
OWNED = 8
ROWS = OWNED * HOURS
STEP = 0.1
CODE = 32000.0
VMEM = 56 * 1024 * 1024

F32 = jnp.float32
BF16 = jnp.bfloat16


def dot_nt(a, b):
    return lax.dot_general(a, b, (((1,), (1,)), ((), ())), preferred_element_type=F32)


def dot_nn(a, b):
    return lax.dot_general(a, b, (((1,), (0,)), ((), ())), preferred_element_type=F32)


def split2(x):
    high = x.astype(BF16)
    return high, (x - high.astype(F32)).astype(BF16)


def split3(x):
    high = x.astype(BF16)
    rest = x - high.astype(F32)
    mid = rest.astype(BF16)
    return high, mid, (rest - mid.astype(F32)).astype(BF16)


def net_flow_kernel(factors, load, net):
    net[...] = dot_nt(factors[...], load[...])


def net_flow(factors, load):
    return pl.pallas_call(
        net_flow_kernel,
        grid=(4,),
        in_specs=[
            pl.BlockSpec((LINES // 4, BUSES), lambda j: (j, 0)),
            pl.BlockSpec((COLS, BUSES), lambda j: (0, 0)),
        ],
        out_specs=pl.BlockSpec((LINES // 4, COLS), lambda j: (j, 0)),
        out_shape=jax.ShapeDtypeStruct((LINES, COLS), F32),
        compiler_params=pltpu.CompilerParams(vmem_limit_bytes=VMEM),
        name="net_flow",
    )(factors, load)


def hour_places():
    column = lax.broadcasted_iota(jnp.int32, (HOURS, COLS), 1)
    row = lax.broadcasted_iota(jnp.int32, (HOURS, COLS), 0)
    return (jnp.bitwise_and(column, HOURS - 1) == row).astype(F32).astype(BF16)


def flow_kernel(first, units, factors, net, level, coded, work, capacity):
    @pl.when(pl.program_id(0) == 0)
    def _():
        local = units[:, 8, :] - first[0].astype(F32)
        high = jnp.floor(local * (1.0 / 128.0))
        low = local - high * 128.0
        for src in range(BUS_AXIS):
            values = units[src, 0:8, :]
            row_high = high[src : src + 1, :]
            for block in range(8):
                work[block * 8 : block * 8 + 8, src * 512 : src * 512 + 512] = jnp.where(
                    row_high == float(block), values, 0.0
                )
        lows = lax.broadcasted_iota(jnp.int32, (128, 512), 0).astype(F32)
        total = jnp.zeros((192, 128), F32)
        for src in range(BUS_AXIS):
            match = jnp.where(lows == low[src : src + 1, :], 1.0, 0.0).astype(BF16)
            pieces = jnp.concatenate(split3(work[:, src * 512 : src * 512 + 512]), axis=0)
            total = total + dot_nt(pieces, match)
        total = total[0:64] + total[64:128] + total[128:192]
        for block in range(8):
            parts = split3(total[8 * block : 8 * block + 8])
            for index in range(3):
                capacity[8 * index : 8 * index + 8, 128 * block : 128 * block + 128] = parts[index].astype(F32)

    block = factors[...]
    given = dot_nt(block, capacity[...].astype(BF16))
    place = hour_places()
    place = jnp.concatenate([place, place, place], axis=0)
    g0, g1, g2 = split3(given)
    fixed = dot_nn(g0, place) + dot_nn(g1, place) + dot_nn(g2, place)
    part = fixed * level[0:1, :] - net[...]
    top = jnp.maximum(jnp.max(jnp.abs(part), axis=1, keepdims=True), 1e-30)
    power = jnp.ceil(jnp.log2(top) * 8.0)
    unit = jnp.exp2(power * -0.125) * CODE
    coded[0, 0:SHARE, :] = jnp.round(part * unit).astype(jnp.int32).astype(jnp.int16)
    across = jnp.transpose(jnp.broadcast_to(power, (SHARE, 128)))[0:8]
    across = jnp.concatenate([across, jnp.zeros((8, COLS - SHARE), F32)], axis=1)
    coded[0, SHARE : SHARE + 8, :] = across.astype(jnp.int32).astype(jnp.int16)


def coded_flow(first, units, factors, net, level):
    return pl.pallas_call(
        flow_kernel,
        grid=(BUS_AXIS,),
        in_specs=[
            pl.BlockSpec(memory_space=pltpu.SMEM),
            pl.BlockSpec(memory_space=pltpu.VMEM),
            pl.BlockSpec((SHARE, BUSES), lambda j: (j, 0)),
            pl.BlockSpec((SHARE, COLS), lambda j: (j, 0)),
            pl.BlockSpec((3, COLS), lambda j: (0, 0)),
        ],
        out_specs=pl.BlockSpec((1, SHARE + 8, COLS), lambda j: (j, 0, 0)),
        out_shape=jax.ShapeDtypeStruct((BUS_AXIS, SHARE + 8, COLS), jnp.int16),
        scratch_shapes=[pltpu.VMEM((64, UNITS), F32), pltpu.VMEM((24, BUSES), F32)],
        compiler_params=pltpu.CompilerParams(vmem_limit_bytes=VMEM),
        name="coded_flow",
    )(first, near(units), factors, net, level)


def excess_kernel(coded, limit, rows, out):
    level = rows[0:1, :]
    weight = rows[1:2, :]
    cluster = rows[2:3, :]
    column = lax.broadcasted_iota(jnp.int32, (1, COLS), 1)
    hour = jnp.bitwise_and(column, HOURS - 1)
    power = [coded[src, SHARE : SHARE + 8, 0:SHARE].astype(jnp.int32).astype(F32)[0:1] for src in range(BUS_AXIS)]
    unit = jnp.exp2(jnp.transpose(jnp.concatenate(power, axis=0)) * 0.125) * (1.0 / CODE)
    flow = coded[0, 0:SHARE, :].astype(jnp.int32).astype(F32) * unit[:, 0:1]
    for src in range(1, BUS_AXIS):
        flow = flow + coded[src, 0:SHARE, :].astype(jnp.int32).astype(F32) * unit[:, src : src + 1]
    edge = limit[:, 0:1]
    excess = flow - jnp.clip(flow, -edge, edge)
    p0, p1 = split2(excess * (level * weight))
    e0, e1 = split2(excess * excess * (0.5 * weight))
    key = cluster * float(HOURS) + hour.astype(F32)
    for dest in range(SCEN_AXIS):
        row = lax.broadcasted_iota(jnp.int32, (ROWS, COLS), 0)
        mine = ((row // HOURS) * SCEN_AXIS + dest) * HOURS + jnp.bitwise_and(row, HOURS - 1)
        pick = jnp.where(mine.astype(F32) == key, 1.0, 0.0).astype(BF16)
        pushed = dot_nt(pick, p0) + dot_nt(pick, p1)
        row = lax.broadcasted_iota(jnp.int32, (16, COLS), 0)
        mine = jnp.where(row < 8, row * SCEN_AXIS + dest, dest * OWNED + row - 8)
        pick = jnp.where(mine.astype(F32) == cluster, 1.0, 0.0).astype(BF16)
        pooled = dot_nt(pick, e0) + dot_nt(pick, e1)
        both = jnp.concatenate([pushed, pooled], axis=0)
        out[dest, 0:80, :] = both[:, 0:128]
        out[dest, 80:120, :] = jnp.concatenate([both[0:40, 128:192], both[40:80, 128:192]], axis=1)


def excess_sums(coded, limit, rows):
    return pl.pallas_call(
        excess_kernel,
        in_specs=[pl.BlockSpec(memory_space=pltpu.VMEM)] * 3,
        out_specs=pl.BlockSpec(memory_space=pltpu.VMEM),
        out_shape=jax.ShapeDtypeStruct((SCEN_AXIS, 120, 128), F32),
        compiler_params=pltpu.CompilerParams(vmem_limit_bytes=VMEM),
        name="excess_sums",
    )(near(coded), near(limit), near(rows))


def update_kernel(mine, sums, gathered, current, target, out):
    total = sums[0]
    for src in range(1, SCEN_AXIS):
        total = total + sums[src]
    spread = jnp.concatenate(
        [gathered[pl.ds(8 * i + mine[0], 1), :] for i in range(OWNED)], axis=0
    )
    tail = jnp.concatenate([total[80:120, 0:64], total[80:120, 64:128]], axis=0)
    for part, lo, hi in ((total[0:80], 0, 128), (tail, 128, 192)):
        chosen = jnp.maximum(
            spread[:, lo:hi] + STEP * (part[64:72] - spread[:, SHARE : SHARE + 1]), 0.0
        )
        owned = jnp.maximum(current[:, lo:hi] + STEP * (part[72:80] - target[:, 0:1]), 0.0)
        wide = jnp.concatenate(
            [part[8 * i : 8 * i + 8] * chosen[i : i + 1] for i in range(OWNED)] + [owned], axis=0
        )
        if lo == 0:
            for dest in range(BUS_AXIS):
                out[dest, 0:72, :] = wide
        else:
            folded = jnp.concatenate([wide[0:40], jnp.concatenate([wide[40:72], wide[64:72]], axis=0)], axis=1)
            for dest in range(BUS_AXIS):
                out[dest, 72:112, :] = folded


def updated(mine, sums, gathered, current, target):
    return pl.pallas_call(
        update_kernel,
        in_specs=[pl.BlockSpec(memory_space=pltpu.SMEM)] + [pl.BlockSpec(memory_space=pltpu.VMEM)] * 4,
        out_specs=pl.BlockSpec(memory_space=pltpu.VMEM),
        out_shape=jax.ShapeDtypeStruct((BUS_AXIS, 112, 128), F32),
        compiler_params=pltpu.CompilerParams(vmem_limit_bytes=VMEM),
        name="update",
    )(mine, near(sums), near(gathered), near(current), near(target))


def slopes_kernel(packed, factors, slopes, duals):
    step = pl.program_id(0)
    head = packed[0, 0:72, :]
    tail = packed[0, 72:112, :]
    tail = jnp.concatenate([tail[:, 0:64], tail[0:32, 64:128]], axis=0)
    wide = jnp.concatenate([head, tail], axis=1)
    duals[0] = wide[64:72]
    high, low = split2(wide[0:64])
    both = dot_nn(jnp.concatenate([high, low], axis=0), factors[...])
    part = both[0:64] + both[64:128]

    @pl.when(step == 0)
    def _():
        slopes[...] = part

    @pl.when(step > 0)
    def _():
        slopes[...] = slopes[...] + part


def slopes_of(packed, factors):
    return pl.pallas_call(
        slopes_kernel,
        grid=(BUS_AXIS,),
        in_specs=[
            pl.BlockSpec((1, 112, 128), lambda j: (j, 0, 0)),
            pl.BlockSpec((SHARE, BUSES), lambda j: (j, 0)),
        ],
        out_specs=[
            pl.BlockSpec((ROWS, BUSES), lambda j: (0, 0)),
            pl.BlockSpec((1, 8, SHARE), lambda j: (j, 0, 0)),
        ],
        out_shape=[
            jax.ShapeDtypeStruct((ROWS, BUSES), F32),
            jax.ShapeDtypeStruct((BUS_AXIS, 8, SHARE), F32),
        ],
        compiler_params=pltpu.CompilerParams(vmem_limit_bytes=VMEM),
        name="slopes",
    )(packed, factors)


def exchange(tiles, axis):
    return lax.all_to_all(tiles, axis, 0, 0, tiled=True)


def near(x):
    return pltpu.with_memory_space_constraint(x, pltpu.VMEM)


def per_device(
    shift_factors,
    net_load,
    dispatch_level,
    scenario_weight,
    cluster_id,
    commitment,
    unit_capacity,
    unit_bus,
    line_limit,
    multipliers,
    penalty_target,
):
    place = lax.axis_index("bus")
    values = commitment.astype(F32) * unit_capacity[None, :]
    units = jnp.concatenate([values, unit_bus.astype(F32)[None, :]], axis=0)
    units = exchange(jnp.broadcast_to(units[None], (BUS_AXIS, 9, 512)), "bus")

    net = net_flow(shift_factors, net_load.reshape(COLS, BUSES))
    rows = jnp.stack(
        [
            dispatch_level.reshape(COLS),
            jnp.repeat(scenario_weight, HOURS),
            jnp.repeat(cluster_id[:, 0].astype(F32), HOURS),
        ],
        axis=0,
    )
    coded = coded_flow((place * BUSES).reshape(1), units, shift_factors, net, rows)
    received = exchange(coded, "bus")

    limit = lax.dynamic_slice_in_dim(line_limit, place * SHARE, SHARE, 0).reshape(SHARE, 1)
    current = lax.dynamic_slice_in_dim(multipliers, place * SHARE, SHARE, 1)
    target = penalty_target.reshape(OWNED, 1)
    gathered = jnp.concatenate([current, jnp.broadcast_to(target, (OWNED, 64))], axis=1)
    gathered = lax.all_gather(gathered, "scen", axis=0, tiled=True)

    sums = exchange(excess_sums(received, limit, rows), "scen")
    mine = lax.axis_index("scen").reshape(1)
    packed = exchange(updated(mine, sums, gathered, current, target), "bus")
    slopes, duals = slopes_of(packed, shift_factors)
    slopes = exchange(slopes.reshape(LINE_AXIS, HOURS, BUSES), "line")
    dual_out = jnp.moveaxis(duals, 0, 1).reshape(OWNED, LINES)
    return dual_out, jnp.sum(slopes, axis=0, keepdims=True)


def solution(mesh):
    placed = (
        P("line", "bus"),
        P("scen", None, "bus"),
        P("scen", None),
        P("scen"),
        P("scen", None),
        P(None, "bus"),
        P("bus"),
        P("bus"),
        P("line"),
        P("scen", "line"),
        P("scen"),
    )

    return jax.shard_map(
        per_device,
        mesh=mesh,
        in_specs=placed,
        out_specs=(P("scen", "line"), P(("line", "scen"), None, "bus")),
        check_vma=False,
    )
```

```python
import jax
import jax.numpy as jnp
from jax import lax
from jax.experimental import pallas as pl
from jax.experimental.pallas import tpu as pltpu
from jax.sharding import PartitionSpec as P


BUS_AXIS = 8
LINE_AXIS = 8
SCEN_AXIS = 8
LINES = 1536
SHARE = LINES // BUS_AXIS
BUSES = 1024
SCEN = 64
HOURS = 8
COLS = SCEN * HOURS
OWNED = 8
ROWS = OWNED * HOURS
STEP = 0.1
CODE = 32000.0
VMEM = 20 * 1024 * 1024
WIDE = 56 * 1024 * 1024

F32 = jnp.float32
BF16 = jnp.bfloat16


def dot_nt(a, b):
    return lax.dot_general(a, b, (((1,), (1,)), ((), ())), preferred_element_type=F32)


def dot_nn(a, b):
    return lax.dot_general(a, b, (((1,), (0,)), ((), ())), preferred_element_type=F32)


def split2(x):
    high = x.astype(BF16)
    return high, (x - high.astype(F32)).astype(BF16)


def split3(x):
    high = x.astype(BF16)
    rest = x - high.astype(F32)
    mid = rest.astype(BF16)
    return high, mid, (rest - mid.astype(F32)).astype(BF16)


def net_flow_kernel(factors, load, net):
    net[...] = dot_nt(factors[...], load[...])


def net_flow(factors, load):
    return pl.pallas_call(
        net_flow_kernel,
        grid=(4,),
        in_specs=[
            pl.BlockSpec((LINES // 4, BUSES), lambda j: (j, 0)),
            pl.BlockSpec((COLS, BUSES), lambda j: (0, 0)),
        ],
        out_specs=pl.BlockSpec((LINES // 4, COLS), lambda j: (j, 0)),
        out_shape=jax.ShapeDtypeStruct((LINES, COLS), F32),
        compiler_params=pltpu.CompilerParams(vmem_limit_bytes=WIDE),
        name="net_flow",
    )(factors, load)


def hour_places():
    column = lax.broadcasted_iota(jnp.int32, (HOURS, COLS), 1)
    row = lax.broadcasted_iota(jnp.int32, (HOURS, COLS), 0)
    return (jnp.bitwise_and(column, HOURS - 1) == row).astype(F32).astype(BF16)


def flow_kernel(first, units, factors, net, level, coded, store):
    @pl.when(pl.program_id(0) == 0)
    def _():
        local = units[:, 8, :] - first[0].astype(F32)
        high = jnp.floor(local * (1.0 / 128.0))
        low = local - high * 128.0
        lows = lax.broadcasted_iota(jnp.int32, (128, 512), 0).astype(F32)
        total = jnp.zeros((192, 128), F32)
        for src in range(BUS_AXIS):
            values = units[src, 0:8, :]
            row_high = high[src : src + 1, :]
            work = jnp.concatenate([jnp.where(row_high == float(block), values, 0.0) for block in range(8)], axis=0)
            match = jnp.where(lows == low[src : src + 1, :], 1.0, 0.0).astype(BF16)
            total = total + dot_nt(jnp.concatenate(split3(work), axis=0), match)
        total = total[0:64] + total[64:128] + total[128:192]
        capacity = jnp.concatenate([total[8 * block : 8 * block + 8] for block in range(8)], axis=1)
        for index, piece in enumerate(split3(capacity)):
            store[8 * index : 8 * index + 8, :] = piece.astype(F32)

    capacity = store[...].astype(BF16)
    place = hour_places()
    place = jnp.concatenate([place, place, place], axis=0)
    first_row = pl.program_id(0) * (2 * SHARE)
    for half in range(2):
        rows = pl.ds(pl.multiple_of(first_row + half * SHARE, SHARE), SHARE)
        given = dot_nt(factors[rows, :], capacity)
        g0, g1, g2 = split3(given)
        fixed = dot_nn(g0, place) + dot_nn(g1, place) + dot_nn(g2, place)
        part = fixed * level[0:1, :] - net[half * SHARE : half * SHARE + SHARE, :]
        top = jnp.maximum(jnp.max(jnp.abs(part), axis=1, keepdims=True), 1e-30)
        power = jnp.ceil(jnp.log2(top) * 8.0)
        unit = jnp.exp2(power * -0.125) * CODE
        coded[half, 0:SHARE, :] = jnp.round(part * unit).astype(jnp.int32).astype(jnp.int16)
        across = jnp.transpose(jnp.broadcast_to(power, (SHARE, 128)))[0:8]
        across = jnp.concatenate([across, jnp.zeros((8, COLS - SHARE), F32)], axis=1)
        coded[half, SHARE : SHARE + 8, :] = across.astype(jnp.int32).astype(jnp.int16)


def coded_flow(first, units, factors, net, level):
    whole = pl.BlockSpec(memory_space=pltpu.VMEM)
    return pl.pallas_call(
        flow_kernel,
        grid=(BUS_AXIS // 2,),
        in_specs=[
            pl.BlockSpec(memory_space=pltpu.SMEM),
            whole,
            whole,
            pl.BlockSpec((2 * SHARE, COLS), lambda j: (j, 0)),
            whole,
        ],
        out_specs=pl.BlockSpec((2, SHARE + 8, COLS), lambda j: (j, 0, 0)),
        out_shape=jax.ShapeDtypeStruct((BUS_AXIS, SHARE + 8, COLS), jnp.int16),
        scratch_shapes=[pltpu.VMEM((24, BUSES), F32)],
        compiler_params=pltpu.CompilerParams(vmem_limit_bytes=WIDE),
        name="coded_flow",
    )(first, near(units), factors, net, near(level))


def excess_kernel(coded, limit, rows, current, target, out):
    level = rows[0:1, :]
    weight = rows[1:2, :]
    cluster = rows[2:3, :]
    column = lax.broadcasted_iota(jnp.int32, (1, COLS), 1)
    hour = jnp.bitwise_and(column, HOURS - 1)
    power = [coded[src, SHARE : SHARE + 8, 0:SHARE].astype(jnp.int32).astype(F32)[0:1] for src in range(BUS_AXIS)]
    unit = jnp.exp2(jnp.transpose(jnp.concatenate(power, axis=0)) * 0.125) * (1.0 / CODE)
    flow = coded[0, 0:SHARE, :].astype(jnp.int32).astype(F32) * unit[:, 0:1]
    for src in range(1, BUS_AXIS):
        flow = flow + coded[src, 0:SHARE, :].astype(jnp.int32).astype(F32) * unit[:, src : src + 1]
    edge = limit[:, 0:1]
    excess = flow - jnp.clip(flow, -edge, edge)
    p0, p1 = split2(excess * (level * weight))
    e0, e1 = split2(excess * excess * (0.5 * weight))
    key = cluster * float(HOURS) + hour.astype(F32)
    row = lax.broadcasted_iota(jnp.int32, (COLS, COLS), 0)
    inner = jnp.bitwise_and(row, ROWS - 1)
    owner = jnp.right_shift(row, 6)
    mine = (jnp.right_shift(inner, 3) * SCEN_AXIS + owner) * HOURS + jnp.bitwise_and(inner, HOURS - 1)
    pick = jnp.where(mine.astype(F32) == key, 1.0, 0.0).astype(BF16)
    pushed = dot_nt(pick, p0) + dot_nt(pick, p1)
    row = lax.broadcasted_iota(jnp.int32, (128, COLS), 0)
    inner = jnp.bitwise_and(row, 15)
    owner = jnp.right_shift(row, 4)
    mine = jnp.where(inner < 8, inner * SCEN_AXIS + owner, owner * OWNED + inner - 8)
    pick = jnp.where(mine.astype(F32) == cluster, 1.0, 0.0).astype(BF16)
    pooled = dot_nt(pick, e0) + dot_nt(pick, e1)
    last = lax.broadcasted_iota(jnp.int32, (8, SHARE), 0)
    for dest in range(SCEN_AXIS):
        given = jnp.where(last == 0, current[dest : dest + 1, :], target[dest : dest + 1, 0:1])
        both = jnp.concatenate(
            [pushed[dest * ROWS : dest * ROWS + ROWS], pooled[dest * 16 : dest * 16 + 16], given], axis=0
        )
        out[dest, 0:88, :] = both[:, 0:128]
        right = jnp.concatenate([both[48:88, 128:192], both[80:88, 128:192]], axis=0)
        out[dest, 88:136, :] = jnp.concatenate([both[0:48, 128:192], right], axis=1)


def excess_sums(coded, limit, rows, current, target):
    return pl.pallas_call(
        excess_kernel,
        in_specs=[pl.BlockSpec(memory_space=pltpu.VMEM)] * 5,
        out_specs=pl.BlockSpec(memory_space=pltpu.VMEM),
        out_shape=pltpu.VMEM((SCEN_AXIS, 136, 128), F32),
        compiler_params=pltpu.CompilerParams(vmem_limit_bytes=VMEM),
        name="excess_sums",
    )(near(coded), near(limit), near(rows), near(current), near(target))


def update_kernel(sums, current, target, out):
    total = sums[0]
    for src in range(1, SCEN_AXIS):
        total = total + sums[src]
    tail = jnp.concatenate([total[88:136, 0:64], total[88:128, 64:128]], axis=0)
    spread = jnp.concatenate(
        [jnp.concatenate([sums[src, 80:81, :], sums[src, 120:121, 64:128]], axis=1) for src in range(OWNED)], axis=0
    )
    spread_target = jnp.concatenate([sums[src, 81:82, 0:1] for src in range(OWNED)], axis=0)
    for part, lo, hi in ((total[0:80], 0, 128), (tail, 128, 192)):
        chosen = jnp.maximum(
            spread[:, lo:hi] + STEP * (part[64:72] - spread_target), 0.0
        )
        owned = jnp.maximum(current[:, lo:hi] + STEP * (part[72:80] - target[:, 0:1]), 0.0)
        wide = jnp.concatenate(
            [part[8 * i : 8 * i + 8] * chosen[i : i + 1] for i in range(OWNED)] + [owned], axis=0
        )
        if lo == 0:
            for dest in range(BUS_AXIS):
                out[dest, 0:72, :] = wide
        else:
            folded = jnp.concatenate([wide[0:40], jnp.concatenate([wide[40:72], wide[64:72]], axis=0)], axis=1)
            for dest in range(BUS_AXIS):
                out[dest, 72:112, :] = folded


def updated(sums, current, target):
    return pl.pallas_call(
        update_kernel,
        in_specs=[pl.BlockSpec(memory_space=pltpu.VMEM)] * 3,
        out_specs=pl.BlockSpec(memory_space=pltpu.VMEM),
        out_shape=jax.ShapeDtypeStruct((BUS_AXIS, 112, 128), F32),
        compiler_params=pltpu.CompilerParams(vmem_limit_bytes=VMEM),
        name="update",
    )(near(sums), near(current), near(target))


def slopes_kernel(packed, factors, slopes, duals):
    total = jnp.zeros((2 * ROWS, BUSES), F32)
    for src in range(BUS_AXIS):
        tail = packed[src, 72:112, :]
        tail = jnp.concatenate([tail[:, 0:64], tail[0:32, 64:128]], axis=0)
        wide = jnp.concatenate([packed[src, 0:72, :], tail], axis=1)
        duals[src] = wide[64:72]
        pieces = jnp.concatenate(split2(wide[0:64]), axis=0)
        total = total + dot_nn(pieces, factors[src * SHARE : src * SHARE + SHARE, :])
    slopes[...] = total[0:ROWS] + total[ROWS:]


def slopes_of(packed, factors):
    return pl.pallas_call(
        slopes_kernel,
        in_specs=[pl.BlockSpec(memory_space=pltpu.VMEM)] * 2,
        out_specs=[pl.BlockSpec(memory_space=pltpu.VMEM)] * 2,
        out_shape=[
            jax.ShapeDtypeStruct((ROWS, BUSES), F32),
            jax.ShapeDtypeStruct((BUS_AXIS, 8, SHARE), F32),
        ],
        compiler_params=pltpu.CompilerParams(vmem_limit_bytes=VMEM),
        name="slopes",
    )(near(packed), factors)


def exchange(tiles, axis):
    return lax.all_to_all(tiles, axis, 0, 0, tiled=True)


def near(x):
    return pltpu.with_memory_space_constraint(x, pltpu.VMEM)


def per_device(
    shift_factors,
    net_load,
    dispatch_level,
    scenario_weight,
    cluster_id,
    commitment,
    unit_capacity,
    unit_bus,
    line_limit,
    multipliers,
    penalty_target,
):
    place = lax.axis_index("bus")
    factors = near(shift_factors)
    values = commitment.astype(F32) * unit_capacity[None, :]
    units = jnp.concatenate([values, unit_bus.astype(F32)[None, :]], axis=0)
    units = exchange(jnp.broadcast_to(units[None], (BUS_AXIS, 9, 512)), "bus")

    net = net_flow(shift_factors, net_load.reshape(COLS, BUSES))
    rows = jnp.stack(
        [
            dispatch_level.reshape(COLS),
            jnp.repeat(scenario_weight, HOURS),
            jnp.repeat(cluster_id[:, 0].astype(F32), HOURS),
        ],
        axis=0,
    )
    coded = coded_flow((place * BUSES).reshape(1), units, factors, net, rows)
    received = exchange(coded, "bus")

    limit = lax.dynamic_slice_in_dim(line_limit, place * SHARE, SHARE, 0).reshape(SHARE, 1)
    current = lax.dynamic_slice_in_dim(multipliers, place * SHARE, SHARE, 1)
    target = penalty_target.reshape(OWNED, 1)
    sums = exchange(excess_sums(received, limit, rows, current, target), "scen")
    packed = exchange(updated(sums, current, target), "bus")
    slopes, duals = slopes_of(packed, factors)
    slopes = exchange(slopes.reshape(LINE_AXIS, HOURS, BUSES), "line")
    dual_out = jnp.moveaxis(duals, 0, 1).reshape(OWNED, LINES)
    return dual_out, jnp.sum(slopes, axis=0, keepdims=True)


def solution(mesh):
    placed = (
        P("line", "bus"),
        P("scen", None, "bus"),
        P("scen", None),
        P("scen"),
        P("scen", None),
        P(None, "bus"),
        P("bus"),
        P("bus"),
        P("line"),
        P("scen", "line"),
        P("scen"),
    )

    return jax.shard_map(
        per_device,
        mesh=mesh,
        in_specs=placed,
        out_specs=(P("scen", "line"), P(("line", "scen"), None, "bus")),
        check_vma=False,
    )
```

```python
import jax
import jax.numpy as jnp
from jax import lax
from jax.experimental import pallas as pl
from jax.experimental.pallas import tpu as pltpu
from jax.sharding import PartitionSpec as P


BUS_AXIS = 8
LINE_AXIS = 8
SCEN_AXIS = 8
LINES = 1536
SHARE = LINES // BUS_AXIS
HALF = SHARE // 2
PAIRS = BUS_AXIS // 2
BUSES = 1024
SCEN = 64
HOURS = 8
COLS = SCEN * HOURS
OWNED = 8
ROWS = OWNED * HOURS
STEP = 0.1
CODE = 32000.0
VMEM = 20 * 1024 * 1024
WIDE = 56 * 1024 * 1024

F32 = jnp.float32
BF16 = jnp.bfloat16


def dot_nt(a, b):
    return lax.dot_general(a, b, (((1,), (1,)), ((), ())), preferred_element_type=F32)


def dot_nn(a, b):
    return lax.dot_general(a, b, (((1,), (0,)), ((), ())), preferred_element_type=F32)


def split2(x):
    high = x.astype(BF16)
    return high, (x - high.astype(F32)).astype(BF16)


def split3(x):
    high = x.astype(BF16)
    rest = x - high.astype(F32)
    mid = rest.astype(BF16)
    return high, mid, (rest - mid.astype(F32)).astype(BF16)


def powers_of(part):
    top = jnp.maximum(jnp.max(jnp.abs(part), axis=1, keepdims=True), 1e-30)
    return jnp.ceil(jnp.log2(top) * 8.0)


def to_code(part, power):
    return jnp.round(part * (jnp.exp2(power * -0.125) * CODE)).astype(jnp.int32).astype(jnp.int16)


def from_code(code):
    return code.astype(jnp.int32).astype(F32)


def unit_of(power):
    return jnp.exp2(power * 0.125) * (1.0 / CODE)


def as_row(column):
    return jnp.transpose(jnp.broadcast_to(column, (column.shape[0], 128)))[0:1]


def as_column(row):
    return jnp.transpose(jnp.broadcast_to(row, (128, row.shape[1])))[:, 0:1]


def net_flow_kernel(parity, factors, load, keep, send_a, send_b, work, powers):
    step = pl.program_id(0)
    work[...] = dot_nt(factors[...], load[...])
    keep[...] = work[pl.ds(pl.multiple_of(parity[0] * SHARE, SHARE), SHARE), :]
    other = work[pl.ds(pl.multiple_of((1 - parity[0]) * SHARE, SHARE), SHARE), :]

    @pl.when(step == 0)
    def _():
        powers[...] = jnp.zeros_like(powers)

    for index, out in enumerate((send_a, send_b)):
        part = other[index * HALF : index * HALF + HALF]
        power = powers_of(part)
        out[pl.ds(pl.multiple_of(step * HALF, HALF), HALF), :] = to_code(part, power)
        wide = jnp.concatenate([jnp.broadcast_to(power, (HALF, 128)), jnp.zeros((128 - HALF, 128), F32)], axis=0)
        mine = lax.broadcasted_iota(jnp.int32, (8, 128), 0) == step
        powers[index, :, 0:128] = jnp.where(mine, jnp.transpose(wide)[0:8], powers[index, :, 0:128])

    @pl.when(step == PAIRS - 1)
    def _():
        for index, out in enumerate((send_a, send_b)):
            out[PAIRS * HALF : PAIRS * HALF + 8, :] = powers[index].astype(jnp.int32).astype(jnp.int16)


def net_flow(parity, factors, load):
    sent = jax.ShapeDtypeStruct((PAIRS * HALF + 8, COLS), jnp.int16)
    return pl.pallas_call(
        net_flow_kernel,
        grid=(PAIRS,),
        in_specs=[
            pl.BlockSpec(memory_space=pltpu.SMEM),
            pl.BlockSpec((2 * SHARE, BUSES), lambda j: (j, 0)),
            pl.BlockSpec((COLS, BUSES), lambda j: (0, 0)),
        ],
        out_specs=[
            pl.BlockSpec((SHARE, COLS), lambda j: (j, 0)),
            pl.BlockSpec((PAIRS * HALF + 8, COLS), lambda j: (0, 0)),
            pl.BlockSpec((PAIRS * HALF + 8, COLS), lambda j: (0, 0)),
        ],
        out_shape=[jax.ShapeDtypeStruct((PAIRS * SHARE, COLS), F32), sent, sent],
        scratch_shapes=[pltpu.VMEM((2 * SHARE, COLS), F32), pltpu.VMEM((2, 8, COLS), F32)],
        compiler_params=pltpu.CompilerParams(vmem_limit_bytes=WIDE),
        name="net_flow",
    )(parity, factors, load)


def capacity_kernel(place, units, factors, keep, send):
    local = units[:, 8, :] - (place[0] * BUSES).astype(F32)
    parity = jnp.bitwise_and(place[0], 1)
    high = jnp.floor(local * (1.0 / 128.0))
    low = local - high * 128.0
    lows = lax.broadcasted_iota(jnp.int32, (128, 512), 0).astype(F32)
    total = jnp.zeros((192, 128), F32)
    for src in range(BUS_AXIS):
        values = units[src, 0:8, :]
        row_high = high[src : src + 1, :]
        work = jnp.concatenate([jnp.where(row_high == float(block), values, 0.0) for block in range(8)], axis=0)
        match = jnp.where(lows == low[src : src + 1, :], 1.0, 0.0).astype(BF16)
        total = total + dot_nt(jnp.concatenate(split3(work), axis=0), match)
    total = total[0:64] + total[64:128] + total[128:192]
    capacity = jnp.concatenate([total[8 * block : 8 * block + 8] for block in range(8)], axis=1)
    capacity = jnp.concatenate(split3(capacity), axis=0)
    for pair in range(PAIRS):
        for out, side in ((keep, parity), (send, 1 - parity)):
            first = pl.multiple_of((2 * pair + side) * SHARE, SHARE)
            given = jnp.transpose(dot_nt(factors[pl.ds(first, SHARE), :], capacity))
            out[pair] = given[0:8] + given[8:16] + given[16:24]


def capacity_flow(place, units, factors):
    whole = pl.BlockSpec(memory_space=pltpu.VMEM)
    share = jax.ShapeDtypeStruct((PAIRS, HOURS, SHARE), F32)
    return pl.pallas_call(
        capacity_kernel,
        in_specs=[pl.BlockSpec(memory_space=pltpu.SMEM), whole, whole],
        out_specs=[whole, whole],
        out_shape=[share, share],
        compiler_params=pltpu.CompilerParams(vmem_limit_bytes=VMEM),
        name="capacity_flow",
    )(place, near(units), factors)


def hour_places():
    column = lax.broadcasted_iota(jnp.int32, (HOURS, COLS), 1)
    row = lax.broadcasted_iota(jnp.int32, (HOURS, COLS), 0)
    return (jnp.bitwise_and(column, HOURS - 1) == row).astype(F32).astype(BF16)


def pair_kernel(net, code_a, code_b, power_a, power_b, given, given_a, given_b, level, coded):
    step = pl.program_id(0)
    place = hour_places()
    here = lax.broadcasted_iota(jnp.int32, (8, 128), 0) == step
    halves = []
    for index, (code, power) in enumerate(((code_a, power_a), (code_b, power_b))):
        row = jnp.sum(jnp.where(here, from_code(power[:, 0:128]), 0.0), axis=0, keepdims=True)
        unit = unit_of(as_column(row))[0:HALF]
        halves.append(net[index * HALF : index * HALF + HALF, :] + from_code(code[...]) * unit)
    lane = lax.broadcasted_iota(jnp.int32, (HOURS, SHARE), 1)
    total = given[0] + jnp.where(lane < HALF, given_a[0], given_b[0])
    g0, g1, g2 = split3(jnp.transpose(total))
    fixed = dot_nn(g0, place) + dot_nn(g1, place) + dot_nn(g2, place)
    part = fixed * level[0:1, :] - jnp.concatenate(halves, axis=0)
    power = powers_of(part)
    coded[0, 0:SHARE, :] = to_code(part, power)
    across = jnp.broadcast_to(as_row(power), (8, SHARE))
    across = jnp.concatenate([across, jnp.zeros((8, COLS - SHARE), F32)], axis=1)
    coded[0, SHARE : SHARE + 8, :] = across.astype(jnp.int32).astype(jnp.int16)


def pair_flow(net, code_a, code_b, given, given_a, given_b, level):
    lines = pl.BlockSpec((HALF, COLS), lambda j: (j, 0))
    tail = pl.BlockSpec((8, COLS), lambda j: (PAIRS * HALF // 8, 0))
    hours = pl.BlockSpec((1, HOURS, SHARE), lambda j: (j, 0, 0))
    return pl.pallas_call(
        pair_kernel,
        grid=(PAIRS,),
        in_specs=[
            pl.BlockSpec((SHARE, COLS), lambda j: (j, 0)),
            lines,
            lines,
            tail,
            tail,
            hours,
            hours,
            hours,
            pl.BlockSpec((3, COLS), lambda j: (0, 0)),
        ],
        out_specs=pl.BlockSpec((1, SHARE + 8, COLS), lambda j: (j, 0, 0)),
        out_shape=jax.ShapeDtypeStruct((PAIRS, SHARE + 8, COLS), jnp.int16),
        compiler_params=pltpu.CompilerParams(vmem_limit_bytes=WIDE),
        name="pair_flow",
    )(net, code_a, code_b, code_a, code_b, given, given_a, given_b, level)


def excess_kernel(coded, limit, rows, current, target, out):
    level = rows[0:1, :]
    weight = rows[1:2, :]
    cluster = rows[2:3, :]
    column = lax.broadcasted_iota(jnp.int32, (1, COLS), 1)
    hour = jnp.bitwise_and(column, HOURS - 1)
    power = jnp.concatenate([from_code(coded[src, SHARE : SHARE + 8, 0:SHARE])[0:1] for src in range(PAIRS)] * 2, axis=0)
    unit = unit_of(jnp.transpose(power))
    flow = from_code(coded[0, 0:SHARE, :]) * unit[:, 0:1]
    for src in range(1, PAIRS):
        flow = flow + from_code(coded[src, 0:SHARE, :]) * unit[:, src : src + 1]
    edge = limit[:, 0:1]
    excess = flow - jnp.clip(flow, -edge, edge)
    p0, p1 = split2(excess * (level * weight))
    e0, e1 = split2(excess * excess * (0.5 * weight))
    key = cluster * float(HOURS) + hour.astype(F32)
    row = lax.broadcasted_iota(jnp.int32, (COLS, COLS), 0)
    inner = jnp.bitwise_and(row, ROWS - 1)
    owner = jnp.right_shift(row, 6)
    mine = (jnp.right_shift(inner, 3) * SCEN_AXIS + owner) * HOURS + jnp.bitwise_and(inner, HOURS - 1)
    pick = jnp.where(mine.astype(F32) == key, 1.0, 0.0).astype(BF16)
    pushed = dot_nt(pick, p0) + dot_nt(pick, p1)
    row = lax.broadcasted_iota(jnp.int32, (128, COLS), 0)
    inner = jnp.bitwise_and(row, 15)
    owner = jnp.right_shift(row, 4)
    mine = jnp.where(inner < 8, inner * SCEN_AXIS + owner, owner * OWNED + inner - 8)
    pick = jnp.where(mine.astype(F32) == cluster, 1.0, 0.0).astype(BF16)
    pooled = dot_nt(pick, e0) + dot_nt(pick, e1)
    last = lax.broadcasted_iota(jnp.int32, (8, SHARE), 0)
    for dest in range(SCEN_AXIS):
        given = jnp.where(last == 0, current[dest : dest + 1, :], target[dest : dest + 1, 0:1])
        both = jnp.concatenate(
            [pushed[dest * ROWS : dest * ROWS + ROWS], pooled[dest * 16 : dest * 16 + 16], given], axis=0
        )
        out[dest, 0:88, :] = both[:, 0:128]
        right = jnp.concatenate([both[48:88, 128:192], both[80:88, 128:192]], axis=0)
        out[dest, 88:136, :] = jnp.concatenate([both[0:48, 128:192], right], axis=1)


def excess_sums(coded, limit, rows, current, target):
    return pl.pallas_call(
        excess_kernel,
        in_specs=[pl.BlockSpec(memory_space=pltpu.VMEM)] * 5,
        out_specs=pl.BlockSpec(memory_space=pltpu.VMEM),
        out_shape=pltpu.VMEM((SCEN_AXIS, 136, 128), F32),
        compiler_params=pltpu.CompilerParams(vmem_limit_bytes=VMEM),
        name="excess_sums",
    )(near(coded), near(limit), near(rows), near(current), near(target))


def update_kernel(sums, current, target, out):
    total = sums[0]
    for src in range(1, SCEN_AXIS):
        total = total + sums[src]
    tail = jnp.concatenate([total[88:136, 0:64], total[88:128, 64:128]], axis=0)
    spread = jnp.concatenate(
        [jnp.concatenate([sums[src, 80:81, :], sums[src, 120:121, 64:128]], axis=1) for src in range(OWNED)], axis=0
    )
    spread_target = jnp.concatenate([sums[src, 81:82, 0:1] for src in range(OWNED)], axis=0)
    for part, lo, hi in ((total[0:80], 0, 128), (tail, 128, 192)):
        chosen = jnp.maximum(
            spread[:, lo:hi] + STEP * (part[64:72] - spread_target), 0.0
        )
        owned = jnp.maximum(current[:, lo:hi] + STEP * (part[72:80] - target[:, 0:1]), 0.0)
        wide = jnp.concatenate(
            [part[8 * i : 8 * i + 8] * chosen[i : i + 1] for i in range(OWNED)] + [owned], axis=0
        )
        if lo == 0:
            for dest in range(BUS_AXIS):
                out[dest, 0:72, :] = wide
        else:
            folded = jnp.concatenate([wide[0:40], jnp.concatenate([wide[40:72], wide[64:72]], axis=0)], axis=1)
            for dest in range(BUS_AXIS):
                out[dest, 72:112, :] = folded


def updated(sums, current, target):
    return pl.pallas_call(
        update_kernel,
        in_specs=[pl.BlockSpec(memory_space=pltpu.VMEM)] * 3,
        out_specs=pl.BlockSpec(memory_space=pltpu.VMEM),
        out_shape=jax.ShapeDtypeStruct((BUS_AXIS, 112, 128), F32),
        compiler_params=pltpu.CompilerParams(vmem_limit_bytes=VMEM),
        name="update",
    )(near(sums), near(current), near(target))


def slopes_kernel(packed, factors, slopes, duals):
    total = jnp.zeros((2 * ROWS, BUSES), F32)
    for src in range(BUS_AXIS):
        tail = packed[src, 72:112, :]
        tail = jnp.concatenate([tail[:, 0:64], tail[0:32, 64:128]], axis=0)
        wide = jnp.concatenate([packed[src, 0:72, :], tail], axis=1)
        duals[src] = wide[64:72]
        pieces = jnp.concatenate(split2(wide[0:64]), axis=0)
        total = total + dot_nn(pieces, factors[src * SHARE : src * SHARE + SHARE, :])
    slopes[...] = total[0:ROWS] + total[ROWS:]


def slopes_of(packed, factors):
    return pl.pallas_call(
        slopes_kernel,
        in_specs=[pl.BlockSpec(memory_space=pltpu.VMEM)] * 2,
        out_specs=[pl.BlockSpec(memory_space=pltpu.VMEM)] * 2,
        out_shape=[
            jax.ShapeDtypeStruct((ROWS, BUSES), F32),
            jax.ShapeDtypeStruct((BUS_AXIS, 8, SHARE), F32),
        ],
        compiler_params=pltpu.CompilerParams(vmem_limit_bytes=VMEM),
        name="slopes",
    )(near(packed), factors)


NEAR_A = [(i, i ^ 1) for i in range(BUS_AXIS)]
NEAR_B = [(i, (i + 1 if i % 2 else i - 1) % BUS_AXIS) for i in range(BUS_AXIS)]
SAME_PARITY = [list(range(0, BUS_AXIS, 2)), list(range(1, BUS_AXIS, 2))]


def exchange(tiles, axis):
    return lax.all_to_all(tiles, axis, 0, 0, tiled=True)


def near(x):
    return pltpu.with_memory_space_constraint(x, pltpu.VMEM)


def per_device(
    shift_factors,
    net_load,
    dispatch_level,
    scenario_weight,
    cluster_id,
    commitment,
    unit_capacity,
    unit_bus,
    line_limit,
    multipliers,
    penalty_target,
):
    place = lax.axis_index("bus")
    factors = near(shift_factors)
    values = commitment.astype(F32) * unit_capacity[None, :]
    units = jnp.concatenate([values, unit_bus.astype(F32)[None, :]], axis=0)
    units = exchange(jnp.broadcast_to(units[None], (BUS_AXIS, 9, 512)), "bus")

    parity = jnp.bitwise_and(place, 1)
    keep, send_a, send_b = net_flow(parity.reshape(1), shift_factors, net_load.reshape(COLS, BUSES))
    code_a = lax.ppermute(send_a, "bus", NEAR_A)
    code_b = lax.ppermute(send_b, "bus", NEAR_B)
    keep, dispatch_level, scenario_weight, cluster_id = lax.optimization_barrier(
        (keep, dispatch_level, scenario_weight, cluster_id)
    )
    rows = jnp.stack(
        [
            dispatch_level.reshape(COLS),
            jnp.repeat(scenario_weight, HOURS),
            jnp.repeat(cluster_id[:, 0].astype(F32), HOURS),
        ],
        axis=0,
    )
    given, send = capacity_flow(place.reshape(1), units, factors)
    given_a = lax.ppermute(send, "bus", NEAR_A)
    given_b = lax.ppermute(send, "bus", NEAR_B)
    coded = pair_flow(keep, code_a, code_b, given, given_a, given_b, rows)
    received = lax.all_to_all(coded, "bus", 0, 0, axis_index_groups=SAME_PARITY, tiled=True)

    limit = lax.dynamic_slice_in_dim(line_limit, place * SHARE, SHARE, 0).reshape(SHARE, 1)
    current = lax.dynamic_slice_in_dim(multipliers, place * SHARE, SHARE, 1)
    target = penalty_target.reshape(OWNED, 1)
    sums = exchange(excess_sums(received, limit, rows, current, target), "scen")
    packed = exchange(updated(sums, current, target), "bus")
    slopes, duals = slopes_of(packed, factors)
    slopes = exchange(slopes.reshape(LINE_AXIS, HOURS, BUSES), "line")
    dual_out = jnp.moveaxis(duals, 0, 1).reshape(OWNED, LINES)
    return dual_out, jnp.sum(slopes, axis=0, keepdims=True)


def solution(mesh):
    placed = (
        P("line", "bus"),
        P("scen", None, "bus"),
        P("scen", None),
        P("scen"),
        P("scen", None),
        P(None, "bus"),
        P("bus"),
        P("bus"),
        P("line"),
        P("scen", "line"),
        P("scen"),
    )

    return jax.shard_map(
        per_device,
        mesh=mesh,
        in_specs=placed,
        out_specs=(P("scen", "line"), P(("line", "scen"), None, "bus")),
        check_vma=False,
    )
```

```python
import jax
import jax.numpy as jnp
from jax import lax
from jax.experimental import pallas as pl
from jax.experimental.pallas import tpu as pltpu
from jax.sharding import PartitionSpec as P


BUS_AXIS = 8
LINE_AXIS = 8
SCEN_AXIS = 8
LINES = 1536
SHARE = LINES // BUS_AXIS
HALF = SHARE // 2
PAIRS = BUS_AXIS // 2
BUSES = 1024
SCEN = 64
HOURS = 8
COLS = SCEN * HOURS
OWNED = 8
ROWS = OWNED * HOURS
STEP = 0.1
CODE = 32000.0
VMEM = 20 * 1024 * 1024
WIDE = 56 * 1024 * 1024

F32 = jnp.float32
BF16 = jnp.bfloat16


def dot_nt(a, b):
    return lax.dot_general(a, b, (((1,), (1,)), ((), ())), preferred_element_type=F32)


def dot_nn(a, b):
    return lax.dot_general(a, b, (((1,), (0,)), ((), ())), preferred_element_type=F32)


def split2(x):
    high = x.astype(BF16)
    return high, (x - high.astype(F32)).astype(BF16)


def split3(x):
    high = x.astype(BF16)
    rest = x - high.astype(F32)
    mid = rest.astype(BF16)
    return high, mid, (rest - mid.astype(F32)).astype(BF16)


def powers_of(part):
    top = jnp.maximum(jnp.max(jnp.abs(part), axis=1, keepdims=True), 1e-30)
    return jnp.ceil(jnp.log2(top) * 8.0)


def to_code(part, power):
    return jnp.round(part * (jnp.exp2(power * -0.125) * CODE)).astype(jnp.int32).astype(jnp.int16)


def from_code(code):
    return code.astype(jnp.int32).astype(F32)


def unit_of(power):
    return jnp.exp2(power * 0.125) * (1.0 / CODE)


def as_row(column):
    return jnp.transpose(jnp.broadcast_to(column, (column.shape[0], 128)))[0:1]


def as_column(row):
    return jnp.transpose(jnp.broadcast_to(row, (128, row.shape[1])))[:, 0:1]


def units_kernel(commitment, capacity, bus, out):
    values = commitment[...].astype(F32) * capacity[...]
    where = bus[...].astype(F32)
    blank = jnp.zeros((8, 128), F32)
    row = lax.broadcasted_iota(jnp.int32, (8, 128), 0)
    for part in range(4):
        blank = jnp.where(row == part, where[:, 128 * part : 128 * part + 128], blank)
    for dest in range(BUS_AXIS):
        for part in range(4):
            out[dest, 8 * part : 8 * part + 8, :] = values[:, 128 * part : 128 * part + 128]
        out[dest, 32:40, :] = blank


def packed_units(commitment, capacity, bus):
    return pl.pallas_call(
        units_kernel,
        out_shape=jax.ShapeDtypeStruct((BUS_AXIS, 40, 128), F32),
        compiler_params=pltpu.CompilerParams(vmem_limit_bytes=WIDE),
        name="units",
    )(commitment, capacity.reshape(1, 512), bus.reshape(1, 512))


def net_flow_kernel(parity, factors, load, keep, other, work):
    work[...] = dot_nt(factors[...], load[...])
    keep[...] = work[pl.ds(pl.multiple_of(parity[0] * SHARE, SHARE), SHARE), :]
    other[...] = work[pl.ds(pl.multiple_of((1 - parity[0]) * SHARE, SHARE), SHARE), :]


def net_flow(parity, factors, load):
    half = jax.ShapeDtypeStruct((PAIRS * SHARE, COLS), F32)
    return pl.pallas_call(
        net_flow_kernel,
        grid=(PAIRS,),
        in_specs=[
            pl.BlockSpec(memory_space=pltpu.SMEM),
            pl.BlockSpec((2 * SHARE, BUSES), lambda j: (j, 0)),
            pl.BlockSpec((COLS, BUSES), lambda j: (0, 0)),
        ],
        out_specs=[pl.BlockSpec((SHARE, COLS), lambda j: (j, 0))] * 2,
        out_shape=[half, half],
        scratch_shapes=[pltpu.VMEM((2 * SHARE, COLS), F32)],
        compiler_params=pltpu.CompilerParams(vmem_limit_bytes=WIDE),
        name="net_flow",
    )(parity, factors, load)


def hour_places():
    column = lax.broadcasted_iota(jnp.int32, (3 * HOURS, COLS), 1)
    row = lax.broadcasted_iota(jnp.int32, (3 * HOURS, COLS), 0)
    return (jnp.bitwise_and(column, HOURS - 1) == jnp.bitwise_and(row, HOURS - 1)).astype(F32).astype(BF16)


def over_columns(given, place):
    pieces = jnp.concatenate([piece.astype(F32) for piece in split3(given)], axis=0)
    return dot_nn(jnp.transpose(pieces).astype(BF16), place)


def send_kernel(place, units, factors, level, other, given, send_a, send_b, stage, powers, semaphore):
    load = pltpu.make_async_copy(other, stage, semaphore)
    load.start()
    parity = jnp.bitwise_and(place[0], 1)
    first = (place[0] * BUSES).astype(F32)
    lows = lax.broadcasted_iota(jnp.int32, (128, 512), 0).astype(F32)
    total = jnp.zeros((192, 128), F32)
    for src in range(BUS_AXIS):
        values = jnp.concatenate([units[src, 8 * part : 8 * part + 8, :] for part in range(4)], axis=1)
        local = jnp.concatenate([units[src, 32 + part : 33 + part, :] for part in range(4)], axis=1) - first
        high = jnp.floor(local * (1.0 / 128.0))
        low = local - high * 128.0
        work = jnp.concatenate([jnp.where(high == float(block), values, 0.0) for block in range(8)], axis=0)
        match = jnp.where(lows == low, 1.0, 0.0).astype(BF16)
        total = total + dot_nt(jnp.concatenate(split3(work), axis=0), match)
    total = total[0:64] + total[64:128] + total[128:192]
    capacity = jnp.concatenate([total[8 * block : 8 * block + 8] for block in range(8)], axis=1)
    capacity = jnp.concatenate(split3(capacity), axis=0)
    spread = hour_places()
    powers[...] = jnp.zeros_like(powers)
    load.wait()
    for pair in range(PAIRS):
        halves = []
        for side in (parity, 1 - parity):
            row = pl.multiple_of((2 * pair + side) * SHARE, SHARE)
            part = jnp.transpose(dot_nt(factors[pl.ds(row, SHARE), :], capacity))
            halves.append(part[0:8] + part[8:16] + part[16:24])
        given[pair] = halves[0]
        part = over_columns(halves[1], spread) * level[0:1, :] - stage[pair * SHARE : pair * SHARE + SHARE, :]
        power = powers_of(part)
        code = to_code(part, power)
        across = as_row(power)
        for index, out in enumerate((send_a, send_b)):
            out[pair * HALF : pair * HALF + HALF, :] = code[index * HALF : index * HALF + HALF]
        powers[pair : pair + 1, 0:SHARE] = across
    for out in (send_a, send_b):
        out[PAIRS * HALF : PAIRS * HALF + 8, :] = powers[...].astype(jnp.int32).astype(jnp.int16)


def sent_flow(place, units, factors, level, other):
    whole = pl.BlockSpec(memory_space=pltpu.VMEM)
    sent = jax.ShapeDtypeStruct((PAIRS * HALF + 8, COLS), jnp.int16)
    return pl.pallas_call(
        send_kernel,
        in_specs=[
            pl.BlockSpec(memory_space=pltpu.SMEM),
            whole,
            whole,
            whole,
            pl.BlockSpec(memory_space=pl.ANY),
        ],
        out_specs=[whole, whole, whole],
        out_shape=[jax.ShapeDtypeStruct((PAIRS, HOURS, SHARE), F32), sent, sent],
        scratch_shapes=[
            pltpu.VMEM((PAIRS * SHARE, COLS), F32),
            pltpu.VMEM((8, COLS), F32),
            pltpu.SemaphoreType.DMA(()),
        ],
        compiler_params=pltpu.CompilerParams(vmem_limit_bytes=WIDE),
        name="sent_flow",
    )(place, near(units), factors, near(level), other)


def pair_kernel(net, code_a, code_b, power_a, power_b, given, level, coded):
    here = lax.broadcasted_iota(jnp.int32, (8, 256), 0) == pl.program_id(0)
    lane = lax.broadcasted_iota(jnp.int32, (1, 256), 1)
    rows = [
        jnp.sum(jnp.where(here, from_code(power[:, 0:256]), 0.0), axis=0, keepdims=True) for power in (power_a, power_b)
    ]
    unit = unit_of(as_column(jnp.where(lane < HALF, rows[0], rows[1])))[0:SHARE]
    code = jnp.concatenate([from_code(code_a[...]), from_code(code_b[...])], axis=0)
    part = over_columns(given[0], hour_places()) * level[0:1, :] - net[...] + code * unit
    power = powers_of(part)
    coded[0, 0:SHARE, :] = to_code(part, power)
    across = jnp.broadcast_to(as_row(power), (8, SHARE))
    across = jnp.concatenate([across, jnp.zeros((8, COLS - SHARE), F32)], axis=1)
    coded[0, SHARE : SHARE + 8, :] = across.astype(jnp.int32).astype(jnp.int16)


def pair_flow(net, code_a, code_b, given, level):
    lines = pl.BlockSpec((HALF, COLS), lambda j: (j, 0))
    tail = pl.BlockSpec((8, COLS), lambda j: (PAIRS * HALF // 8, 0))
    return pl.pallas_call(
        pair_kernel,
        grid=(PAIRS,),
        in_specs=[
            pl.BlockSpec((SHARE, COLS), lambda j: (j, 0)),
            lines,
            lines,
            tail,
            tail,
            pl.BlockSpec((1, HOURS, SHARE), lambda j: (j, 0, 0)),
            pl.BlockSpec((3, COLS), lambda j: (0, 0)),
        ],
        out_specs=pl.BlockSpec((1, SHARE + 8, COLS), lambda j: (j, 0, 0)),
        out_shape=pltpu.HBM((PAIRS, SHARE + 8, COLS), jnp.int16),
        compiler_params=pltpu.CompilerParams(vmem_limit_bytes=VMEM),
        name="pair_flow",
    )(net, code_a, code_b, code_a, code_b, given, level)


def excess_kernel(coded, limit, rows, current, target, out):
    level = rows[0:1, :]
    weight = rows[1:2, :]
    cluster = rows[2:3, :]
    column = lax.broadcasted_iota(jnp.int32, (1, COLS), 1)
    hour = jnp.bitwise_and(column, HOURS - 1)
    power = jnp.concatenate([from_code(coded[src, SHARE : SHARE + 8, 0:SHARE])[0:1] for src in range(PAIRS)] * 2, axis=0)
    unit = unit_of(jnp.transpose(power))
    flow = from_code(coded[0, 0:SHARE, :]) * unit[:, 0:1]
    for src in range(1, PAIRS):
        flow = flow + from_code(coded[src, 0:SHARE, :]) * unit[:, src : src + 1]
    edge = limit[:, 0:1]
    excess = flow - jnp.clip(flow, -edge, edge)
    p0, p1 = split2(excess * (level * weight))
    e0, e1 = split2(excess * excess * (0.5 * weight))
    key = cluster * float(HOURS) + hour.astype(F32)
    row = lax.broadcasted_iota(jnp.int32, (COLS, COLS), 0)
    inner = jnp.bitwise_and(row, ROWS - 1)
    owner = jnp.right_shift(row, 6)
    mine = (jnp.right_shift(inner, 3) * SCEN_AXIS + owner) * HOURS + jnp.bitwise_and(inner, HOURS - 1)
    pick = jnp.where(mine.astype(F32) == key, 1.0, 0.0).astype(BF16)
    pushed = dot_nt(pick, p0) + dot_nt(pick, p1)
    row = lax.broadcasted_iota(jnp.int32, (128, COLS), 0)
    inner = jnp.bitwise_and(row, 15)
    owner = jnp.right_shift(row, 4)
    mine = jnp.where(inner < 8, inner * SCEN_AXIS + owner, owner * OWNED + inner - 8)
    pick = jnp.where(mine.astype(F32) == cluster, 1.0, 0.0).astype(BF16)
    pooled = dot_nt(pick, e0) + dot_nt(pick, e1)
    last = lax.broadcasted_iota(jnp.int32, (8, SHARE), 0)
    for dest in range(SCEN_AXIS):
        given = jnp.where(last == 0, current[dest : dest + 1, :], target[dest : dest + 1, 0:1])
        both = jnp.concatenate(
            [pushed[dest * ROWS : dest * ROWS + ROWS], pooled[dest * 16 : dest * 16 + 16], given], axis=0
        )
        out[dest, 0:88, :] = both[:, 0:128]
        right = jnp.concatenate([both[48:88, 128:192], both[80:88, 128:192]], axis=0)
        out[dest, 88:136, :] = jnp.concatenate([both[0:48, 128:192], right], axis=1)


def excess_sums(coded, limit, rows, current, target):
    return pl.pallas_call(
        excess_kernel,
        in_specs=[pl.BlockSpec(memory_space=pltpu.VMEM)] * 5,
        out_specs=pl.BlockSpec(memory_space=pltpu.VMEM),
        out_shape=pltpu.VMEM((SCEN_AXIS, 136, 128), F32),
        compiler_params=pltpu.CompilerParams(vmem_limit_bytes=VMEM),
        name="excess_sums",
    )(near(coded), near(limit), near(rows), near(current), near(target))


def update_kernel(sums, current, target, out):
    total = sums[0]
    for src in range(1, SCEN_AXIS):
        total = total + sums[src]
    tail = jnp.concatenate([total[88:136, 0:64], total[88:128, 64:128]], axis=0)
    spread = jnp.concatenate(
        [jnp.concatenate([sums[src, 80:81, :], sums[src, 120:121, 64:128]], axis=1) for src in range(OWNED)], axis=0
    )
    spread_target = jnp.concatenate([sums[src, 81:82, 0:1] for src in range(OWNED)], axis=0)
    for part, lo, hi in ((total[0:80], 0, 128), (tail, 128, 192)):
        chosen = jnp.maximum(
            spread[:, lo:hi] + STEP * (part[64:72] - spread_target), 0.0
        )
        owned = jnp.maximum(current[:, lo:hi] + STEP * (part[72:80] - target[:, 0:1]), 0.0)
        wide = jnp.concatenate(
            [part[8 * i : 8 * i + 8] * chosen[i : i + 1] for i in range(OWNED)] + [owned], axis=0
        )
        if lo == 0:
            for dest in range(BUS_AXIS):
                out[dest, 0:72, :] = wide
        else:
            folded = jnp.concatenate([wide[0:40], jnp.concatenate([wide[40:72], wide[64:72]], axis=0)], axis=1)
            for dest in range(BUS_AXIS):
                out[dest, 72:112, :] = folded


def updated(sums, current, target):
    return pl.pallas_call(
        update_kernel,
        in_specs=[pl.BlockSpec(memory_space=pltpu.VMEM)] * 3,
        out_specs=pl.BlockSpec(memory_space=pltpu.VMEM),
        out_shape=jax.ShapeDtypeStruct((BUS_AXIS, 112, 128), F32),
        compiler_params=pltpu.CompilerParams(vmem_limit_bytes=VMEM),
        name="update",
    )(near(sums), near(current), near(target))


def slopes_kernel(packed, factors, slopes, duals):
    total = jnp.zeros((2 * ROWS, BUSES), F32)
    for src in range(BUS_AXIS):
        tail = packed[src, 72:112, :]
        tail = jnp.concatenate([tail[:, 0:64], tail[0:32, 64:128]], axis=0)
        wide = jnp.concatenate([packed[src, 0:72, :], tail], axis=1)
        duals[src] = wide[64:72]
        pieces = jnp.concatenate(split2(wide[0:64]), axis=0)
        total = total + dot_nn(pieces, factors[src * SHARE : src * SHARE + SHARE, :])
    slopes[...] = total[0:ROWS] + total[ROWS:]


def slopes_of(packed, factors):
    return pl.pallas_call(
        slopes_kernel,
        in_specs=[pl.BlockSpec(memory_space=pltpu.VMEM)] * 2,
        out_specs=[pl.BlockSpec(memory_space=pltpu.VMEM)] * 2,
        out_shape=[
            jax.ShapeDtypeStruct((ROWS, BUSES), F32),
            jax.ShapeDtypeStruct((BUS_AXIS, 8, SHARE), F32),
        ],
        compiler_params=pltpu.CompilerParams(vmem_limit_bytes=VMEM),
        name="slopes",
    )(near(packed), factors)


NEAR_A = [(i, i ^ 1) for i in range(BUS_AXIS)]
NEAR_B = [(i, (i + 1 if i % 2 else i - 1) % BUS_AXIS) for i in range(BUS_AXIS)]
SAME_PARITY = [list(range(0, BUS_AXIS, 2)), list(range(1, BUS_AXIS, 2))]


def exchange(tiles, axis):
    return lax.all_to_all(tiles, axis, 0, 0, tiled=True)


def near(x):
    return pltpu.with_memory_space_constraint(x, pltpu.VMEM)


def per_device(
    shift_factors,
    net_load,
    dispatch_level,
    scenario_weight,
    cluster_id,
    commitment,
    unit_capacity,
    unit_bus,
    line_limit,
    multipliers,
    penalty_target,
):
    place = lax.axis_index("bus")
    factors = near(shift_factors)
    units = exchange(packed_units(commitment, unit_capacity, unit_bus), "bus")
    parity = jnp.bitwise_and(place, 1)
    keep, other = net_flow(parity.reshape(1), shift_factors, net_load.reshape(COLS, BUSES))
    keep, dispatch_level, scenario_weight, cluster_id = lax.optimization_barrier(
        (keep, dispatch_level, scenario_weight, cluster_id)
    )
    rows = jnp.stack(
        [
            dispatch_level.reshape(COLS),
            jnp.repeat(scenario_weight, HOURS),
            jnp.repeat(cluster_id[:, 0].astype(F32), HOURS),
        ],
        axis=0,
    )
    given, send_a, send_b = sent_flow(place.reshape(1), units, factors, rows, other)
    code_a = lax.ppermute(send_a, "bus", NEAR_A)
    code_b = lax.ppermute(send_b, "bus", NEAR_B)
    coded = pair_flow(keep, code_a, code_b, given, rows)
    received = lax.all_to_all(coded, "bus", 0, 0, axis_index_groups=SAME_PARITY, tiled=True)

    limit = lax.dynamic_slice_in_dim(line_limit, place * SHARE, SHARE, 0).reshape(SHARE, 1)
    current = lax.dynamic_slice_in_dim(multipliers, place * SHARE, SHARE, 1)
    target = penalty_target.reshape(OWNED, 1)
    sums = exchange(excess_sums(received, limit, rows, current, target), "scen")
    packed = exchange(updated(sums, current, target), "bus")
    slopes, duals = slopes_of(packed, factors)
    slopes = exchange(slopes.reshape(LINE_AXIS, HOURS, BUSES), "line")
    dual_out = jnp.moveaxis(duals, 0, 1).reshape(OWNED, LINES)
    return dual_out, jnp.sum(slopes, axis=0, keepdims=True)


def solution(mesh):
    placed = (
        P("line", "bus"),
        P("scen", None, "bus"),
        P("scen", None),
        P("scen"),
        P("scen", None),
        P(None, "bus"),
        P("bus"),
        P("bus"),
        P("line"),
        P("scen", "line"),
        P("scen"),
    )

    return jax.shard_map(
        per_device,
        mesh=mesh,
        in_specs=placed,
        out_specs=(P("scen", "line"), P(("line", "scen"), None, "bus")),
        check_vma=False,
    )
```

```python
import jax
import jax.numpy as jnp
from jax import lax
from jax.experimental import pallas as pl
from jax.experimental.pallas import tpu as pltpu
from jax.sharding import PartitionSpec as P


BUS_AXIS = 8
LINE_AXIS = 8
SCEN_AXIS = 8
LINES = 1536
SHARE = LINES // BUS_AXIS
HALF = SHARE // 2
PAIRS = BUS_AXIS // 2
BUSES = 1024
SCEN = 64
HOURS = 8
COLS = SCEN * HOURS
OWNED = 8
ROWS = OWNED * HOURS
STEP = 0.1
CODE = 32000.0
FINE = 60000.0
POOLED = 176
UPDATED = 128
VMEM = 20 * 1024 * 1024
WIDE = 56 * 1024 * 1024

F32 = jnp.float32
BF16 = jnp.bfloat16


def dot_nt(a, b):
    return lax.dot_general(a, b, (((1,), (1,)), ((), ())), preferred_element_type=F32)


def dot_nn(a, b):
    return lax.dot_general(a, b, (((1,), (0,)), ((), ())), preferred_element_type=F32)


def split2(x):
    high = x.astype(BF16)
    return high, (x - high.astype(F32)).astype(BF16)


def split3(x):
    high = x.astype(BF16)
    rest = x - high.astype(F32)
    mid = rest.astype(BF16)
    return high, mid, (rest - mid.astype(F32)).astype(BF16)


def powers_of(part):
    top = jnp.maximum(jnp.max(jnp.abs(part), axis=1, keepdims=True), 1e-30)
    return jnp.ceil(jnp.log2(top) * 8.0)


def rounded(x):
    return jnp.floor(x + 0.5)


def to_code(part, power):
    return rounded(part * (jnp.exp2(power * -0.125) * CODE)).astype(jnp.int32).astype(jnp.int16)


def from_code(code):
    return code.astype(jnp.int32).astype(F32)


def unit_of(power):
    return jnp.exp2(power * 0.125) * (1.0 / CODE)


def coded_rows(rough, fine):
    rough_power = powers_of(rough)
    fine_power = powers_of(fine)
    rough = rounded(rough * (jnp.exp2(rough_power * -0.125) * CODE))
    fine = fine * (jnp.exp2(fine_power * -0.125) * CODE)
    high = rounded(fine)
    both = jnp.concatenate([rough, high, rounded((fine - high) * FINE)], axis=0)
    half = both.shape[0] // 2
    tail = jnp.concatenate([both[0:half, 128:SHARE], both[half:, 128:SHARE]], axis=1)
    blank = jnp.zeros((128 - rough_power.shape[0] - fine_power.shape[0], 1), F32)
    return jnp.concatenate([both[:, 0:128], tail], axis=0), jnp.concatenate([rough_power, fine_power, blank], axis=0)


def decoded_rows(block, unit, count):
    rows = ROWS + 2 * count
    tail = block[rows : rows + rows // 2]
    tail = jnp.concatenate([tail[:, 0:64], tail[:, 64:128]], axis=0)
    both = jnp.concatenate([block[0:rows], tail], axis=1)
    fine = both[ROWS : ROWS + count] + both[ROWS + count : rows] * (1.0 / FINE)
    return both[0:ROWS] * unit[0:ROWS], fine * unit[ROWS : ROWS + count]


def as_row(column):
    return jnp.transpose(jnp.broadcast_to(column, (column.shape[0], 128)))[0:1]


def as_column(row):
    return jnp.transpose(jnp.broadcast_to(row, (128, row.shape[1])))[:, 0:1]


def units_kernel(commitment, capacity, bus, out):
    values = commitment[...].astype(F32) * capacity[...]
    where = bus[...].astype(F32)
    blank = jnp.zeros((8, 128), F32)
    row = lax.broadcasted_iota(jnp.int32, (8, 128), 0)
    for part in range(4):
        blank = jnp.where(row == part, where[:, 128 * part : 128 * part + 128], blank)
    for dest in range(BUS_AXIS):
        for part in range(4):
            out[dest, 8 * part : 8 * part + 8, :] = values[:, 128 * part : 128 * part + 128]
        out[dest, 32:40, :] = blank


def packed_units(commitment, capacity, bus):
    return pl.pallas_call(
        units_kernel,
        out_shape=jax.ShapeDtypeStruct((BUS_AXIS, 40, 128), F32),
        compiler_params=pltpu.CompilerParams(vmem_limit_bytes=WIDE),
        name="units",
    )(commitment, capacity.reshape(1, 512), bus.reshape(1, 512))


def net_flow_kernel(parity, factors, load, keep, other, work):
    work[...] = dot_nt(factors[...], load[...])
    keep[...] = work[pl.ds(pl.multiple_of(parity[0] * SHARE, SHARE), SHARE), :]
    other[...] = work[pl.ds(pl.multiple_of((1 - parity[0]) * SHARE, SHARE), SHARE), :]


def net_flow(parity, factors, load):
    half = jax.ShapeDtypeStruct((PAIRS * SHARE, COLS), F32)
    return pl.pallas_call(
        net_flow_kernel,
        grid=(PAIRS,),
        in_specs=[
            pl.BlockSpec(memory_space=pltpu.SMEM),
            pl.BlockSpec((2 * SHARE, BUSES), lambda j: (j, 0)),
            pl.BlockSpec((COLS, BUSES), lambda j: (0, 0)),
        ],
        out_specs=[pl.BlockSpec((SHARE, COLS), lambda j: (j, 0))] * 2,
        out_shape=[half, half],
        scratch_shapes=[pltpu.VMEM((2 * SHARE, COLS), F32)],
        compiler_params=pltpu.CompilerParams(vmem_limit_bytes=WIDE),
        name="net_flow",
    )(parity, factors, load)


def hour_places():
    column = lax.broadcasted_iota(jnp.int32, (3 * HOURS, COLS), 1)
    row = lax.broadcasted_iota(jnp.int32, (3 * HOURS, COLS), 0)
    return (jnp.bitwise_and(column, HOURS - 1) == jnp.bitwise_and(row, HOURS - 1)).astype(F32).astype(BF16)


def over_columns(given, place):
    pieces = jnp.concatenate([piece.astype(F32) for piece in split3(given)], axis=0)
    return dot_nn(jnp.transpose(pieces).astype(BF16), place)


def send_kernel(place, units, factors, level, other, given, send_a, send_b, stage, powers, semaphore):
    load = pltpu.make_async_copy(other, stage, semaphore)
    load.start()
    parity = jnp.bitwise_and(place[0], 1)
    first = (place[0] * BUSES).astype(F32)
    lows = lax.broadcasted_iota(jnp.int32, (128, 512), 0).astype(F32)
    total = jnp.zeros((192, 128), F32)
    for src in range(BUS_AXIS):
        values = jnp.concatenate([units[src, 8 * part : 8 * part + 8, :] for part in range(4)], axis=1)
        local = jnp.concatenate([units[src, 32 + part : 33 + part, :] for part in range(4)], axis=1) - first
        high = jnp.floor(local * (1.0 / 128.0))
        low = local - high * 128.0
        work = jnp.concatenate([jnp.where(high == float(block), values, 0.0) for block in range(8)], axis=0)
        match = jnp.where(lows == low, 1.0, 0.0).astype(BF16)
        total = total + dot_nt(jnp.concatenate(split3(work), axis=0), match)
    total = total[0:64] + total[64:128] + total[128:192]
    capacity = jnp.concatenate([total[8 * block : 8 * block + 8] for block in range(8)], axis=1)
    capacity = jnp.concatenate(split3(capacity), axis=0)
    spread = hour_places()
    powers[...] = jnp.zeros_like(powers)
    load.wait()
    for pair in range(PAIRS):
        halves = []
        for side in (parity, 1 - parity):
            row = pl.multiple_of((2 * pair + side) * SHARE, SHARE)
            part = jnp.transpose(dot_nt(factors[pl.ds(row, SHARE), :], capacity))
            halves.append(part[0:8] + part[8:16] + part[16:24])
        given[pair] = halves[0]
        part = over_columns(halves[1], spread) * level[0:1, :] - stage[pair * SHARE : pair * SHARE + SHARE, :]
        power = powers_of(part)
        code = to_code(part, power)
        across = as_row(power)
        for index, out in enumerate((send_a, send_b)):
            out[pair * HALF : pair * HALF + HALF, :] = code[index * HALF : index * HALF + HALF]
        powers[pair : pair + 1, 0:SHARE] = across
    for out in (send_a, send_b):
        out[PAIRS * HALF : PAIRS * HALF + 8, :] = powers[...].astype(jnp.int32).astype(jnp.int16)


def sent_flow(place, units, factors, level, other):
    whole = pl.BlockSpec(memory_space=pltpu.VMEM)
    sent = jax.ShapeDtypeStruct((PAIRS * HALF + 8, COLS), jnp.int16)
    return pl.pallas_call(
        send_kernel,
        in_specs=[
            pl.BlockSpec(memory_space=pltpu.SMEM),
            whole,
            whole,
            whole,
            pl.BlockSpec(memory_space=pl.ANY),
        ],
        out_specs=[whole, whole, whole],
        out_shape=[jax.ShapeDtypeStruct((PAIRS, HOURS, SHARE), F32), sent, sent],
        scratch_shapes=[
            pltpu.VMEM((PAIRS * SHARE, COLS), F32),
            pltpu.VMEM((8, COLS), F32),
            pltpu.SemaphoreType.DMA(()),
        ],
        compiler_params=pltpu.CompilerParams(vmem_limit_bytes=WIDE),
        name="sent_flow",
    )(place, near(units), factors, near(level), other)


def pair_kernel(net, code_a, code_b, power_a, power_b, given, level, coded):
    here = lax.broadcasted_iota(jnp.int32, (8, 256), 0) == pl.program_id(0)
    lane = lax.broadcasted_iota(jnp.int32, (1, 256), 1)
    rows = [
        jnp.sum(jnp.where(here, from_code(power[:, 0:256]), 0.0), axis=0, keepdims=True) for power in (power_a, power_b)
    ]
    unit = unit_of(as_column(jnp.where(lane < HALF, rows[0], rows[1])))[0:SHARE]
    code = jnp.concatenate([from_code(code_a[...]), from_code(code_b[...])], axis=0)
    part = over_columns(given[0], hour_places()) * level[0:1, :] - net[...] + code * unit
    power = powers_of(part)
    coded[0, 0:SHARE, :] = to_code(part, power)
    across = jnp.broadcast_to(as_row(power), (8, SHARE))
    across = jnp.concatenate([across, jnp.zeros((8, COLS - SHARE), F32)], axis=1)
    coded[0, SHARE : SHARE + 8, :] = across.astype(jnp.int32).astype(jnp.int16)


def pair_flow(net, code_a, code_b, given, level):
    lines = pl.BlockSpec((HALF, COLS), lambda j: (j, 0))
    tail = pl.BlockSpec((8, COLS), lambda j: (PAIRS * HALF // 8, 0))
    return pl.pallas_call(
        pair_kernel,
        grid=(PAIRS,),
        in_specs=[
            pl.BlockSpec((SHARE, COLS), lambda j: (j, 0)),
            lines,
            lines,
            tail,
            tail,
            pl.BlockSpec((1, HOURS, SHARE), lambda j: (j, 0, 0)),
            pl.BlockSpec((3, COLS), lambda j: (0, 0)),
        ],
        out_specs=pl.BlockSpec((1, SHARE + 8, COLS), lambda j: (j, 0, 0)),
        out_shape=pltpu.HBM((PAIRS, SHARE + 8, COLS), jnp.int16),
        compiler_params=pltpu.CompilerParams(vmem_limit_bytes=VMEM),
        name="pair_flow",
    )(net, code_a, code_b, code_a, code_b, given, level)


def excess_kernel(coded, limit, rows, current, target, out):
    level = rows[0:1, :]
    weight = rows[1:2, :]
    cluster = rows[2:3, :]
    column = lax.broadcasted_iota(jnp.int32, (1, COLS), 1)
    hour = jnp.bitwise_and(column, HOURS - 1)
    power = jnp.concatenate([from_code(coded[src, SHARE : SHARE + 8, 0:SHARE])[0:1] for src in range(PAIRS)] * 2, axis=0)
    unit = unit_of(jnp.transpose(power))
    flow = from_code(coded[0, 0:SHARE, :]) * unit[:, 0:1]
    for src in range(1, PAIRS):
        flow = flow + from_code(coded[src, 0:SHARE, :]) * unit[:, src : src + 1]
    edge = limit[:, 0:1]
    excess = flow - jnp.clip(flow, -edge, edge)
    p0, p1 = split2(excess * (level * weight))
    e0, e1 = split2(excess * excess * (0.5 * weight))
    key = cluster * float(HOURS) + hour.astype(F32)
    row = lax.broadcasted_iota(jnp.int32, (COLS, COLS), 0)
    inner = jnp.bitwise_and(row, ROWS - 1)
    owner = jnp.right_shift(row, 6)
    mine = (jnp.right_shift(inner, 3) * SCEN_AXIS + owner) * HOURS + jnp.bitwise_and(inner, HOURS - 1)
    pick = jnp.where(mine.astype(F32) == key, 1.0, 0.0).astype(BF16)
    pushed = dot_nt(pick, p0) + dot_nt(pick, p1)
    row = lax.broadcasted_iota(jnp.int32, (128, COLS), 0)
    inner = jnp.bitwise_and(row, 15)
    owner = jnp.right_shift(row, 4)
    mine = jnp.where(inner < 8, inner * SCEN_AXIS + owner, owner * OWNED + inner - 8)
    pick = jnp.where(mine.astype(F32) == cluster, 1.0, 0.0).astype(BF16)
    pooled = dot_nt(pick, e0) + dot_nt(pick, e1)
    lane = lax.broadcasted_iota(jnp.int32, (128, 128), 1)
    last = lax.broadcasted_iota(jnp.int32, (8, SHARE), 0)
    table = jnp.zeros((128, 128), F32)
    blocks = []
    for dest in range(SCEN_AXIS):
        given = jnp.where(last == 0, current[dest : dest + 1, :], jnp.where(last == 1, target[dest : dest + 1, 0:1], 0.0))
        block, power = coded_rows(
            pushed[dest * ROWS : dest * ROWS + ROWS],
            jnp.concatenate([pooled[dest * 16 : dest * 16 + 16], given], axis=0),
        )
        table = jnp.where(lane == dest, power, table)
        blocks.append(block)
    table = jnp.transpose(table)
    for dest in range(SCEN_AXIS):
        tail = jnp.broadcast_to(table[dest : dest + 1], (8, 128))
        out[dest] = jnp.concatenate([blocks[dest], tail], axis=0).astype(jnp.int32).astype(jnp.int16)


def excess_sums(coded, limit, rows, current, target):
    return pl.pallas_call(
        excess_kernel,
        in_specs=[pl.BlockSpec(memory_space=pltpu.VMEM)] * 5,
        out_specs=pl.BlockSpec(memory_space=pltpu.VMEM),
        out_shape=pltpu.VMEM((SCEN_AXIS, POOLED, 128), jnp.int16),
        compiler_params=pltpu.CompilerParams(vmem_limit_bytes=VMEM),
        name="excess_sums",
    )(near(coded), near(limit), near(rows), near(current), near(target))


def update_kernel(sums, current, target, out):
    tables = jnp.concatenate([from_code(sums[src, POOLED - 16 : POOLED, :])[15:16] for src in range(SCEN_AXIS)], axis=0)
    units = unit_of(jnp.transpose(tables))
    pushed = jnp.zeros((ROWS, SHARE), F32)
    pooled = jnp.zeros((16, SHARE), F32)
    given = []
    for src in range(SCEN_AXIS):
        rough, fine = decoded_rows(from_code(sums[src]), units[:, src : src + 1], 24)
        pushed = pushed + rough
        pooled = pooled + fine[0:16]
        given.append(fine[16:24])
    spread = jnp.concatenate([part[0:1] for part in given], axis=0)
    spread_target = jnp.concatenate([part[1:2, 0:1] for part in given], axis=0)
    chosen = jnp.maximum(spread + STEP * (pooled[0:8] - spread_target), 0.0)
    owned = jnp.maximum(current[...] + STEP * (pooled[8:16] - target[:, 0:1]), 0.0)
    wide = jnp.concatenate([pushed[8 * i : 8 * i + 8] * chosen[i : i + 1] for i in range(OWNED)], axis=0)
    block, power = coded_rows(wide, owned)
    tail = jnp.broadcast_to(as_row(power), (8, 128))
    block = jnp.concatenate([block, tail], axis=0).astype(jnp.int32).astype(jnp.int16)
    for dest in range(BUS_AXIS):
        out[dest] = block


def updated(sums, current, target):
    return pl.pallas_call(
        update_kernel,
        in_specs=[pl.BlockSpec(memory_space=pltpu.VMEM)] * 3,
        out_specs=pl.BlockSpec(memory_space=pltpu.VMEM),
        out_shape=jax.ShapeDtypeStruct((BUS_AXIS, UPDATED, 128), jnp.int16),
        compiler_params=pltpu.CompilerParams(vmem_limit_bytes=VMEM),
        name="update",
    )(near(sums), near(current), near(target))


def slopes_kernel(packed, factors, slopes, duals):
    tables = jnp.concatenate([from_code(packed[src, UPDATED - 16 : UPDATED, :])[15:16] for src in range(BUS_AXIS)], axis=0)
    units = unit_of(jnp.transpose(tables))
    total = jnp.zeros((2 * ROWS, BUSES), F32)
    for src in range(BUS_AXIS):
        wide, duals[src] = decoded_rows(from_code(packed[src]), units[:, src : src + 1], 8)
        pieces = jnp.concatenate(split2(wide), axis=0)
        total = total + dot_nn(pieces, factors[src * SHARE : src * SHARE + SHARE, :])
    slopes[...] = total[0:ROWS] + total[ROWS:]


def slopes_of(packed, factors):
    return pl.pallas_call(
        slopes_kernel,
        in_specs=[pl.BlockSpec(memory_space=pltpu.VMEM)] * 2,
        out_specs=[pl.BlockSpec(memory_space=pltpu.VMEM)] * 2,
        out_shape=[
            jax.ShapeDtypeStruct((ROWS, BUSES), F32),
            jax.ShapeDtypeStruct((BUS_AXIS, 8, SHARE), F32),
        ],
        compiler_params=pltpu.CompilerParams(vmem_limit_bytes=VMEM),
        name="slopes",
    )(near(packed), factors)


NEAR_A = [(i, i ^ 1) for i in range(BUS_AXIS)]
NEAR_B = [(i, (i + 1 if i % 2 else i - 1) % BUS_AXIS) for i in range(BUS_AXIS)]
SAME_PARITY = [list(range(0, BUS_AXIS, 2)), list(range(1, BUS_AXIS, 2))]


def exchange(tiles, axis):
    return lax.all_to_all(tiles, axis, 0, 0, tiled=True)


def near(x):
    return pltpu.with_memory_space_constraint(x, pltpu.VMEM)


def per_device(
    shift_factors,
    net_load,
    dispatch_level,
    scenario_weight,
    cluster_id,
    commitment,
    unit_capacity,
    unit_bus,
    line_limit,
    multipliers,
    penalty_target,
):
    place = lax.axis_index("bus")
    factors = near(shift_factors)
    units = exchange(packed_units(commitment, unit_capacity, unit_bus), "bus")
    parity = jnp.bitwise_and(place, 1)
    keep, other = net_flow(parity.reshape(1), shift_factors, net_load.reshape(COLS, BUSES))
    keep, dispatch_level, scenario_weight, cluster_id = lax.optimization_barrier(
        (keep, dispatch_level, scenario_weight, cluster_id)
    )
    rows = jnp.stack(
        [
            dispatch_level.reshape(COLS),
            jnp.repeat(scenario_weight, HOURS),
            jnp.repeat(cluster_id[:, 0].astype(F32), HOURS),
        ],
        axis=0,
    )
    given, send_a, send_b = sent_flow(place.reshape(1), units, factors, rows, other)
    code_a = lax.ppermute(send_a, "bus", NEAR_A)
    code_b = lax.ppermute(send_b, "bus", NEAR_B)
    coded = pair_flow(keep, code_a, code_b, given, rows)
    received = lax.all_to_all(coded, "bus", 0, 0, axis_index_groups=SAME_PARITY, tiled=True)

    limit = lax.dynamic_slice_in_dim(line_limit, place * SHARE, SHARE, 0).reshape(SHARE, 1)
    current = lax.dynamic_slice_in_dim(multipliers, place * SHARE, SHARE, 1)
    target = penalty_target.reshape(OWNED, 1)
    sums = exchange(excess_sums(received, limit, rows, current, target), "scen")
    packed = exchange(updated(sums, current, target), "bus")
    slopes, duals = slopes_of(packed, factors)
    slopes = exchange(slopes.reshape(LINE_AXIS, HOURS, BUSES), "line")
    dual_out = jnp.moveaxis(duals, 0, 1).reshape(OWNED, LINES)
    return dual_out, jnp.sum(slopes, axis=0, keepdims=True)


def solution(mesh):
    placed = (
        P("line", "bus"),
        P("scen", None, "bus"),
        P("scen", None),
        P("scen"),
        P("scen", None),
        P(None, "bus"),
        P("bus"),
        P("bus"),
        P("line"),
        P("scen", "line"),
        P("scen"),
    )

    return jax.shard_map(
        per_device,
        mesh=mesh,
        in_specs=placed,
        out_specs=(P("scen", "line"), P(("line", "scen"), None, "bus")),
        check_vma=False,
    )
```

```python
import jax
import jax.numpy as jnp
from jax import lax
from jax.experimental import pallas as pl
from jax.experimental.pallas import tpu as pltpu
from jax.sharding import PartitionSpec as P


BUS_AXIS = 8
LINE_AXIS = 8
SCEN_AXIS = 8
LINES = 1536
SHARE = LINES // BUS_AXIS
HALF = SHARE // 2
PAIRS = BUS_AXIS // 2
BUSES = 1024
SCEN = 64
HOURS = 8
COLS = SCEN * HOURS
OWNED = 8
ROWS = OWNED * HOURS
STEP = 0.1
CODE = 32000.0
FINE = 60000.0
POOLED = 176
UPDATED = 128
VMEM = 20 * 1024 * 1024
WIDE = 56 * 1024 * 1024

F32 = jnp.float32
BF16 = jnp.bfloat16


def dot_nt(a, b):
    return lax.dot_general(a, b, (((1,), (1,)), ((), ())), preferred_element_type=F32)


def dot_nn(a, b):
    return lax.dot_general(a, b, (((1,), (0,)), ((), ())), preferred_element_type=F32)


def split2(x):
    high = x.astype(BF16)
    return high, (x - high.astype(F32)).astype(BF16)


def split3(x):
    high = x.astype(BF16)
    rest = x - high.astype(F32)
    mid = rest.astype(BF16)
    return high, mid, (rest - mid.astype(F32)).astype(BF16)


def power_of(top):
    return jnp.ceil(jnp.log2(jnp.maximum(top, 1e-30)) * 8.0)


def powers_of(part):
    return power_of(jnp.max(jnp.abs(part), axis=1, keepdims=True))


def rounded(x):
    return jnp.floor(x + 0.5)


def to_code(part, power):
    return rounded(part * (jnp.exp2(power * -0.125) * CODE)).astype(jnp.int32).astype(jnp.int16)


def from_code(code):
    return code.astype(jnp.int32).astype(F32)


def unit_of(power):
    return jnp.exp2(power * 0.125) * (1.0 / CODE)


def coded_rows(rough, fine):
    rough_power = powers_of(rough)
    fine_power = powers_of(fine)
    rough = rounded(rough * (jnp.exp2(rough_power * -0.125) * CODE))
    fine = fine * (jnp.exp2(fine_power * -0.125) * CODE)
    high = rounded(fine)
    both = jnp.concatenate([rough, high, rounded((fine - high) * FINE)], axis=0)
    half = both.shape[0] // 2
    tail = jnp.concatenate([both[0:half, 128:SHARE], both[half:, 128:SHARE]], axis=1)
    blank = jnp.zeros((128 - rough_power.shape[0] - fine_power.shape[0], 1), F32)
    return jnp.concatenate([both[:, 0:128], tail], axis=0), jnp.concatenate([rough_power, fine_power, blank], axis=0)


def decoded_rows(block, unit, count):
    rows = ROWS + 2 * count
    tail = block[rows : rows + rows // 2]
    tail = jnp.concatenate([tail[:, 0:64], tail[:, 64:128]], axis=0)
    both = jnp.concatenate([block[0:rows], tail], axis=1)
    fine = both[ROWS : ROWS + count] + both[ROWS + count : rows] * (1.0 / FINE)
    return both[0:ROWS] * unit[0:ROWS], fine * unit[ROWS : ROWS + count]


def as_row(column):
    return jnp.transpose(jnp.broadcast_to(column, (column.shape[0], 128)))[0:1]


def as_column(row):
    return jnp.transpose(jnp.broadcast_to(row, (128, row.shape[1])))[:, 0:1]


def units_kernel(commitment, capacity, bus, out):
    values = commitment[...].astype(F32) * capacity[...]
    where = bus[...].astype(F32)
    blank = jnp.zeros((8, 128), F32)
    row = lax.broadcasted_iota(jnp.int32, (8, 128), 0)
    for part in range(4):
        blank = jnp.where(row == part, where[:, 128 * part : 128 * part + 128], blank)
    for dest in range(BUS_AXIS):
        for part in range(4):
            out[dest, 8 * part : 8 * part + 8, :] = values[:, 128 * part : 128 * part + 128]
        out[dest, 32:40, :] = blank


def packed_units(commitment, capacity, bus):
    return pl.pallas_call(
        units_kernel,
        out_shape=jax.ShapeDtypeStruct((BUS_AXIS, 40, 128), F32),
        compiler_params=pltpu.CompilerParams(vmem_limit_bytes=WIDE),
        name="units",
    )(commitment, capacity.reshape(1, 512), bus.reshape(1, 512))


def net_flow_kernel(parity, factors, load, keep, other, top, work):
    work[...] = dot_nt(factors[...], load[...])
    keep[...] = work[pl.ds(pl.multiple_of(parity[0] * SHARE, SHARE), SHARE), :]
    part = work[pl.ds(pl.multiple_of((1 - parity[0]) * SHARE, SHARE), SHARE), :]
    other[...] = part
    top[...] = jnp.broadcast_to(jnp.max(jnp.abs(part), axis=1, keepdims=True), (SHARE, 128))


def net_flow(parity, factors, load):
    half = jax.ShapeDtypeStruct((PAIRS * SHARE, COLS), F32)
    return pl.pallas_call(
        net_flow_kernel,
        grid=(PAIRS,),
        in_specs=[
            pl.BlockSpec(memory_space=pltpu.SMEM),
            pl.BlockSpec((2 * SHARE, BUSES), lambda j: (j, 0)),
            pl.BlockSpec((COLS, BUSES), lambda j: (0, 0)),
        ],
        out_specs=[pl.BlockSpec((SHARE, COLS), lambda j: (j, 0))] * 2 + [pl.BlockSpec((SHARE, 128), lambda j: (j, 0))],
        out_shape=[half, half, jax.ShapeDtypeStruct((PAIRS * SHARE, 128), F32)],
        scratch_shapes=[pltpu.VMEM((2 * SHARE, COLS), F32)],
        compiler_params=pltpu.CompilerParams(vmem_limit_bytes=WIDE),
        name="net_flow",
    )(parity, factors, load)


def hour_places():
    column = lax.broadcasted_iota(jnp.int32, (3 * HOURS, COLS), 1)
    row = lax.broadcasted_iota(jnp.int32, (3 * HOURS, COLS), 0)
    return (jnp.bitwise_and(column, HOURS - 1) == jnp.bitwise_and(row, HOURS - 1)).astype(F32).astype(BF16)


def capacity_part(factors, capacity, place):
    given = jnp.transpose(dot_nt(factors, capacity))
    given = given[0:8] + given[8:16] + given[16:24]
    largest = jnp.broadcast_to(jnp.max(jnp.abs(given), axis=0, keepdims=True), (8, SHARE))
    pieces = jnp.concatenate([piece.astype(F32) for piece in split3(given)] + [largest], axis=0)
    pieces = jnp.transpose(pieces)
    return dot_nn(pieces[:, 0:24].astype(BF16), place), pieces[:, 24:25]


def send_kernel(place, units, factors, level, other, top, capacity_out, send_a, send_b, stage, tops, powers, semaphores):
    loads = (
        pltpu.make_async_copy(other, stage, semaphores.at[0]),
        pltpu.make_async_copy(top, tops, semaphores.at[1]),
    )
    for load in loads:
        load.start()
    parity = jnp.bitwise_and(place[0], 1)
    first = (place[0] * BUSES).astype(F32)
    lows = lax.broadcasted_iota(jnp.int32, (128, 512), 0).astype(F32)
    total = jnp.zeros((192, 128), F32)
    for src in range(BUS_AXIS):
        values = jnp.concatenate([units[src, 8 * part : 8 * part + 8, :] for part in range(4)], axis=1)
        local = jnp.concatenate([units[src, 32 + part : 33 + part, :] for part in range(4)], axis=1) - first
        high = jnp.floor(local * (1.0 / 128.0))
        low = local - high * 128.0
        pieces = [piece.astype(F32) for piece in split3(values)]
        work = [jnp.where(high == float(block), piece, 0.0) for piece in pieces for block in range(8)]
        match = jnp.where(lows == low, 1.0, 0.0).astype(BF16)
        total = total + dot_nt(jnp.concatenate(work, axis=0).astype(BF16), match)
    total = total[0:64] + total[64:128] + total[128:192]
    capacity = jnp.concatenate([total[8 * block : 8 * block + 8] for block in range(8)], axis=1)
    capacity = jnp.concatenate(split3(capacity), axis=0)
    capacity_out[...] = capacity.astype(F32)
    spread = hour_places()
    most = jnp.max(jnp.abs(level[0:1, :]), axis=1, keepdims=True)
    powers[...] = jnp.zeros_like(powers)
    for load in loads:
        load.wait()
    for pair in range(PAIRS):
        row = pl.multiple_of((2 * pair + 1 - parity) * SHARE, SHARE)
        fixed, largest = capacity_part(factors[pl.ds(row, SHARE), :], capacity, spread)
        rows = slice(pair * SHARE, pair * SHARE + SHARE)
        power = power_of(tops[rows, 0:1] + largest * most)
        code = to_code(fixed * level[0:1, :] - stage[rows, :], power)
        for index, out in enumerate((send_a, send_b)):
            out[pair * HALF : pair * HALF + HALF, :] = code[index * HALF : index * HALF + HALF]
        powers[pair : pair + 1, 0:SHARE] = as_row(power)
    for out in (send_a, send_b):
        out[PAIRS * HALF : PAIRS * HALF + 8, :] = powers[...].astype(jnp.int32).astype(jnp.int16)


def sent_flow(place, units, factors, level, other, top):
    whole = pl.BlockSpec(memory_space=pltpu.VMEM)
    anywhere = pl.BlockSpec(memory_space=pl.ANY)
    sent = jax.ShapeDtypeStruct((PAIRS * HALF + 8, COLS), jnp.int16)
    return pl.pallas_call(
        send_kernel,
        in_specs=[pl.BlockSpec(memory_space=pltpu.SMEM), whole, whole, whole, anywhere, anywhere],
        out_specs=[whole, whole, whole],
        out_shape=[pltpu.VMEM((3 * HOURS, BUSES), F32), sent, sent],
        scratch_shapes=[
            pltpu.VMEM((PAIRS * SHARE, COLS), F32),
            pltpu.VMEM((PAIRS * SHARE, 128), F32),
            pltpu.VMEM((8, COLS), F32),
            pltpu.SemaphoreType.DMA((2,)),
        ],
        compiler_params=pltpu.CompilerParams(vmem_limit_bytes=WIDE),
        name="sent_flow",
    )(place, near(units), factors, near(level), other, top)


def kept_kernel(place, capacity, factors, net, level, out, top):
    side = 2 * pl.program_id(0) + jnp.bitwise_and(place[0], 1)
    rows = pl.ds(pl.multiple_of(side * SHARE, SHARE), SHARE)
    fixed, _ = capacity_part(factors[rows, :], capacity[...].astype(BF16), hour_places())
    part = fixed * level[0:1, :] - net[...]
    out[...] = part
    top[...] = jnp.broadcast_to(jnp.max(jnp.abs(part), axis=1, keepdims=True), (SHARE, 128))


def kept_flow(place, capacity, factors, net, level):
    whole = pl.BlockSpec(memory_space=pltpu.VMEM)
    return pl.pallas_call(
        kept_kernel,
        grid=(PAIRS,),
        in_specs=[
            pl.BlockSpec(memory_space=pltpu.SMEM),
            whole,
            whole,
            pl.BlockSpec((SHARE, COLS), lambda j: (j, 0)),
            whole,
        ],
        out_specs=[pl.BlockSpec((SHARE, COLS), lambda j: (j, 0)), pl.BlockSpec((SHARE, 128), lambda j: (j, 0))],
        out_shape=[
            pltpu.VMEM((PAIRS * SHARE, COLS), F32),
            pltpu.VMEM((PAIRS * SHARE, 128), F32),
        ],
        compiler_params=pltpu.CompilerParams(vmem_limit_bytes=VMEM),
        name="kept_flow",
    )(place, near(capacity), factors, net, near(level))


def pair_kernel(part, top, code_a, code_b, power_a, power_b, coded):
    here = lax.broadcasted_iota(jnp.int32, (8, 256), 0) == pl.program_id(0)
    lane = lax.broadcasted_iota(jnp.int32, (1, 256), 1)
    rows = [
        jnp.sum(jnp.where(here, from_code(power[:, 0:256]), 0.0), axis=0, keepdims=True) for power in (power_a, power_b)
    ]
    unit = unit_of(as_column(jnp.where(lane < HALF, rows[0], rows[1])))[0:SHARE]
    power = power_of(top[:, 0:1] + unit * CODE)
    code = jnp.concatenate([from_code(code_a[...]), from_code(code_b[...])], axis=0)
    coded[0, 0:SHARE, :] = to_code(part[...] + code * unit, power)
    across = jnp.broadcast_to(as_row(power), (8, SHARE))
    across = jnp.concatenate([across, jnp.zeros((8, COLS - SHARE), F32)], axis=1)
    coded[0, SHARE : SHARE + 8, :] = across.astype(jnp.int32).astype(jnp.int16)


def pair_flow(part, top, code_a, code_b):
    lines = pl.BlockSpec((HALF, COLS), lambda j: (j, 0))
    tail = pl.BlockSpec((8, COLS), lambda j: (PAIRS * HALF // 8, 0))
    return pl.pallas_call(
        pair_kernel,
        grid=(PAIRS,),
        in_specs=[
            pl.BlockSpec((SHARE, COLS), lambda j: (j, 0)),
            pl.BlockSpec((SHARE, 128), lambda j: (j, 0)),
            lines,
            lines,
            tail,
            tail,
        ],
        out_specs=pl.BlockSpec((1, SHARE + 8, COLS), lambda j: (j, 0, 0)),
        out_shape=pltpu.HBM((PAIRS, SHARE + 8, COLS), jnp.int16),
        compiler_params=pltpu.CompilerParams(vmem_limit_bytes=VMEM),
        name="pair_flow",
    )(part, top, code_a, code_b, code_a, code_b)


def excess_kernel(coded, limit, rows, current, target, out):
    level = rows[0:1, :]
    weight = rows[1:2, :]
    cluster = rows[2:3, :]
    column = lax.broadcasted_iota(jnp.int32, (1, COLS), 1)
    hour = jnp.bitwise_and(column, HOURS - 1)
    power = jnp.concatenate([from_code(coded[src, SHARE : SHARE + 8, 0:SHARE])[0:1] for src in range(PAIRS)] * 2, axis=0)
    unit = unit_of(jnp.transpose(power))
    flow = from_code(coded[0, 0:SHARE, :]) * unit[:, 0:1]
    for src in range(1, PAIRS):
        flow = flow + from_code(coded[src, 0:SHARE, :]) * unit[:, src : src + 1]
    edge = limit[:, 0:1]
    excess = flow - jnp.clip(flow, -edge, edge)
    p0, p1 = split2(excess * (level * weight))
    e0, e1 = split2(excess * excess * (0.5 * weight))
    key = cluster * float(HOURS) + hour.astype(F32)
    row = lax.broadcasted_iota(jnp.int32, (COLS, COLS), 0)
    inner = jnp.bitwise_and(row, ROWS - 1)
    owner = jnp.right_shift(row, 6)
    mine = (jnp.right_shift(inner, 3) * SCEN_AXIS + owner) * HOURS + jnp.bitwise_and(inner, HOURS - 1)
    pick = jnp.where(mine.astype(F32) == key, 1.0, 0.0).astype(BF16)
    pushed = dot_nt(pick, p0) + dot_nt(pick, p1)
    row = lax.broadcasted_iota(jnp.int32, (128, COLS), 0)
    inner = jnp.bitwise_and(row, 15)
    owner = jnp.right_shift(row, 4)
    mine = jnp.where(inner < 8, inner * SCEN_AXIS + owner, owner * OWNED + inner - 8)
    pick = jnp.where(mine.astype(F32) == cluster, 1.0, 0.0).astype(BF16)
    pooled = dot_nt(pick, e0) + dot_nt(pick, e1)
    lane = lax.broadcasted_iota(jnp.int32, (128, 128), 1)
    last = lax.broadcasted_iota(jnp.int32, (8, SHARE), 0)
    table = jnp.zeros((128, 128), F32)
    blocks = []
    for dest in range(SCEN_AXIS):
        given = jnp.where(last == 0, current[dest : dest + 1, :], jnp.where(last == 1, target[dest : dest + 1, 0:1], 0.0))
        block, power = coded_rows(
            pushed[dest * ROWS : dest * ROWS + ROWS],
            jnp.concatenate([pooled[dest * 16 : dest * 16 + 16], given], axis=0),
        )
        table = jnp.where(lane == dest, power, table)
        blocks.append(block)
    table = jnp.transpose(table)
    for dest in range(SCEN_AXIS):
        tail = jnp.broadcast_to(table[dest : dest + 1], (8, 128))
        out[dest] = jnp.concatenate([blocks[dest], tail], axis=0).astype(jnp.int32).astype(jnp.int16)


def excess_sums(coded, limit, rows, current, target):
    return pl.pallas_call(
        excess_kernel,
        in_specs=[pl.BlockSpec(memory_space=pltpu.VMEM)] * 5,
        out_specs=pl.BlockSpec(memory_space=pltpu.VMEM),
        out_shape=pltpu.VMEM((SCEN_AXIS, POOLED, 128), jnp.int16),
        compiler_params=pltpu.CompilerParams(vmem_limit_bytes=VMEM),
        name="excess_sums",
    )(near(coded), near(limit), near(rows), near(current), near(target))


def update_kernel(sums, current, target, out):
    tables = jnp.concatenate([from_code(sums[src, POOLED - 16 : POOLED, :])[15:16] for src in range(SCEN_AXIS)], axis=0)
    units = unit_of(jnp.transpose(tables))
    pushed = jnp.zeros((ROWS, SHARE), F32)
    pooled = jnp.zeros((16, SHARE), F32)
    given = []
    for src in range(SCEN_AXIS):
        rough, fine = decoded_rows(from_code(sums[src]), units[:, src : src + 1], 24)
        pushed = pushed + rough
        pooled = pooled + fine[0:16]
        given.append(fine[16:24])
    spread = jnp.concatenate([part[0:1] for part in given], axis=0)
    spread_target = jnp.concatenate([part[1:2, 0:1] for part in given], axis=0)
    chosen = jnp.maximum(spread + STEP * (pooled[0:8] - spread_target), 0.0)
    owned = jnp.maximum(current[...] + STEP * (pooled[8:16] - target[:, 0:1]), 0.0)
    wide = jnp.concatenate([pushed[8 * i : 8 * i + 8] * chosen[i : i + 1] for i in range(OWNED)], axis=0)
    block, power = coded_rows(wide, owned)
    tail = jnp.broadcast_to(as_row(power), (8, 128))
    block = jnp.concatenate([block, tail], axis=0).astype(jnp.int32).astype(jnp.int16)
    for dest in range(BUS_AXIS):
        out[dest] = block


def updated(sums, current, target):
    return pl.pallas_call(
        update_kernel,
        in_specs=[pl.BlockSpec(memory_space=pltpu.VMEM)] * 3,
        out_specs=pl.BlockSpec(memory_space=pltpu.VMEM),
        out_shape=jax.ShapeDtypeStruct((BUS_AXIS, UPDATED, 128), jnp.int16),
        compiler_params=pltpu.CompilerParams(vmem_limit_bytes=VMEM),
        name="update",
    )(near(sums), near(current), near(target))


def slopes_kernel(packed, factors, slopes, duals):
    tables = jnp.concatenate([from_code(packed[src, UPDATED - 16 : UPDATED, :])[15:16] for src in range(BUS_AXIS)], axis=0)
    units = unit_of(jnp.transpose(tables))
    total = jnp.zeros((2 * ROWS, BUSES), F32)
    for src in range(BUS_AXIS):
        wide, duals[src] = decoded_rows(from_code(packed[src]), units[:, src : src + 1], 8)
        pieces = jnp.concatenate(split2(wide), axis=0)
        total = total + dot_nn(pieces, factors[src * SHARE : src * SHARE + SHARE, :])
    slopes[...] = total[0:ROWS] + total[ROWS:]


def slopes_of(packed, factors):
    return pl.pallas_call(
        slopes_kernel,
        in_specs=[pl.BlockSpec(memory_space=pltpu.VMEM)] * 2,
        out_specs=[pl.BlockSpec(memory_space=pltpu.VMEM)] * 2,
        out_shape=[
            jax.ShapeDtypeStruct((ROWS, BUSES), F32),
            jax.ShapeDtypeStruct((BUS_AXIS, 8, SHARE), F32),
        ],
        compiler_params=pltpu.CompilerParams(vmem_limit_bytes=VMEM),
        name="slopes",
    )(near(packed), factors)


NEAR_A = [(i, i ^ 1) for i in range(BUS_AXIS)]
NEAR_B = [(i, (i + 1 if i % 2 else i - 1) % BUS_AXIS) for i in range(BUS_AXIS)]
SAME_PARITY = [list(range(0, BUS_AXIS, 2)), list(range(1, BUS_AXIS, 2))]


def exchange(tiles, axis):
    return lax.all_to_all(tiles, axis, 0, 0, tiled=True)


def near(x):
    return pltpu.with_memory_space_constraint(x, pltpu.VMEM)


def per_device(
    shift_factors,
    net_load,
    dispatch_level,
    scenario_weight,
    cluster_id,
    commitment,
    unit_capacity,
    unit_bus,
    line_limit,
    multipliers,
    penalty_target,
):
    place = lax.axis_index("bus")
    factors = near(shift_factors)
    units = exchange(packed_units(commitment, unit_capacity, unit_bus), "bus")
    parity = jnp.bitwise_and(place, 1)
    keep, other, top = net_flow(parity.reshape(1), shift_factors, net_load.reshape(COLS, BUSES))
    keep, dispatch_level, scenario_weight, cluster_id = lax.optimization_barrier(
        (keep, dispatch_level, scenario_weight, cluster_id)
    )
    rows = jnp.stack(
        [
            dispatch_level.reshape(COLS),
            jnp.repeat(scenario_weight, HOURS),
            jnp.repeat(cluster_id[:, 0].astype(F32), HOURS),
        ],
        axis=0,
    )
    capacity, send_a, send_b = sent_flow(place.reshape(1), units, factors, rows, other, top)
    code_a = lax.ppermute(send_a, "bus", NEAR_A)
    code_b = lax.ppermute(send_b, "bus", NEAR_B)
    part, top = kept_flow(place.reshape(1), capacity, factors, keep, rows)
    coded = pair_flow(part, top, code_a, code_b)
    received = lax.all_to_all(coded, "bus", 0, 0, axis_index_groups=SAME_PARITY, tiled=True)

    limit = lax.dynamic_slice_in_dim(line_limit, place * SHARE, SHARE, 0).reshape(SHARE, 1)
    current = lax.dynamic_slice_in_dim(multipliers, place * SHARE, SHARE, 1)
    target = penalty_target.reshape(OWNED, 1)
    sums = exchange(excess_sums(received, limit, rows, current, target), "scen")
    packed = exchange(updated(sums, current, target), "bus")
    slopes, duals = slopes_of(packed, factors)
    slopes = exchange(slopes.reshape(LINE_AXIS, HOURS, BUSES), "line")
    dual_out = jnp.moveaxis(duals, 0, 1).reshape(OWNED, LINES)
    return dual_out, jnp.sum(slopes, axis=0, keepdims=True)


def solution(mesh):
    placed = (
        P("line", "bus"),
        P("scen", None, "bus"),
        P("scen", None),
        P("scen"),
        P("scen", None),
        P(None, "bus"),
        P("bus"),
        P("bus"),
        P("line"),
        P("scen", "line"),
        P("scen"),
    )

    return jax.shard_map(
        per_device,
        mesh=mesh,
        in_specs=placed,
        out_specs=(P("scen", "line"), P(("line", "scen"), None, "bus")),
        check_vma=False,
    )
```

```python
import jax
import jax.numpy as jnp
from jax import lax
from jax.experimental import pallas as pl
from jax.experimental.pallas import tpu as pltpu
from jax.sharding import PartitionSpec as P


BUS_AXIS = 8
LINE_AXIS = 8
SCEN_AXIS = 8
LINES = 1536
SHARE = LINES // BUS_AXIS
HALF = SHARE // 2
PAIRS = BUS_AXIS // 2
BUSES = 1024
SCEN = 64
HOURS = 8
COLS = SCEN * HOURS
OWNED = 8
ROWS = OWNED * HOURS
STEP = 0.1
CODE = 32000.0
FINE = 60000.0
OFFSET = 65536.5
POOLED = 176
UPDATED = 128
VMEM = 20 * 1024 * 1024
WIDE = 56 * 1024 * 1024

F32 = jnp.float32
BF16 = jnp.bfloat16


def dot_nt(a, b):
    return lax.dot_general(a, b, (((1,), (1,)), ((), ())), preferred_element_type=F32)


def dot_nn(a, b):
    return lax.dot_general(a, b, (((1,), (0,)), ((), ())), preferred_element_type=F32)


def split2(x):
    high = x.astype(BF16)
    return high, (x - high.astype(F32)).astype(BF16)


def power_of(top):
    return jnp.ceil(jnp.log2(jnp.maximum(top, 1e-30)) * 8.0)


def powers_of(part):
    return power_of(jnp.max(jnp.abs(part), axis=1, keepdims=True))


def rounded(x):
    return jnp.floor(x + 0.5)


def wrapped(x):
    return x.astype(jnp.int32).astype(jnp.int16)


def from_code(code):
    return code.astype(jnp.int32).astype(F32)


def unit_of(power):
    return jnp.exp2(power * 0.125) * (1.0 / CODE)


def coded_rows(rough, fine):
    rough_power = powers_of(rough)
    fine_power = powers_of(fine)
    rough = rounded(rough * (jnp.exp2(rough_power * -0.125) * CODE))
    fine = fine * (jnp.exp2(fine_power * -0.125) * CODE)
    high = rounded(fine)
    both = jnp.concatenate([rough, high, rounded((fine - high) * FINE)], axis=0)
    half = both.shape[0] // 2
    tail = jnp.concatenate([both[0:half, 128:SHARE], both[half:, 128:SHARE]], axis=1)
    blank = jnp.zeros((128 - rough_power.shape[0] - fine_power.shape[0], 1), F32)
    return jnp.concatenate([both[:, 0:128], tail], axis=0), jnp.concatenate([rough_power, fine_power, blank], axis=0)


def decoded_rows(block, unit, count):
    rows = ROWS + 2 * count
    tail = block[rows : rows + rows // 2]
    tail = jnp.concatenate([tail[:, 0:64], tail[:, 64:128]], axis=0)
    both = jnp.concatenate([block[0:rows], tail], axis=1)
    fine = both[ROWS : ROWS + count] + both[ROWS + count : rows] * (1.0 / FINE)
    return both[0:ROWS] * unit[0:ROWS], fine * unit[ROWS : ROWS + count]


def as_row(column):
    return jnp.transpose(jnp.broadcast_to(column, (column.shape[0], 128)))[0:1]


def units_kernel(commitment, capacity, bus, out):
    values = commitment[...].astype(F32) * capacity[...]
    where = bus[...].astype(F32)
    blank = jnp.zeros((8, 128), F32)
    row = lax.broadcasted_iota(jnp.int32, (8, 128), 0)
    for part in range(4):
        blank = jnp.where(row == part, where[:, 128 * part : 128 * part + 128], blank)
    for dest in range(BUS_AXIS):
        for part in range(4):
            out[dest, 8 * part : 8 * part + 8, :] = values[:, 128 * part : 128 * part + 128]
        out[dest, 32:40, :] = blank


def packed_units(commitment, capacity, bus):
    return pl.pallas_call(
        units_kernel,
        out_shape=jax.ShapeDtypeStruct((BUS_AXIS, 40, 128), F32),
        compiler_params=pltpu.CompilerParams(vmem_limit_bytes=WIDE),
        name="units",
    )(commitment, capacity.reshape(1, 512), bus.reshape(1, 512))


def net_flow_kernel(parity, factors, load, keep, other, top, work):
    work[...] = dot_nt(factors[...], load[...])
    keep[...] = work[pl.ds(pl.multiple_of(parity[0] * SHARE, SHARE), SHARE), :]
    part = work[pl.ds(pl.multiple_of((1 - parity[0]) * SHARE, SHARE), SHARE), :]
    other[...] = part
    top[0] = jnp.broadcast_to(as_row(jnp.max(jnp.abs(part), axis=1, keepdims=True)), (8, SHARE))


def net_flow(parity, factors, load):
    half = jax.ShapeDtypeStruct((PAIRS * SHARE, COLS), F32)
    return pl.pallas_call(
        net_flow_kernel,
        grid=(PAIRS,),
        in_specs=[
            pl.BlockSpec(memory_space=pltpu.SMEM),
            pl.BlockSpec((2 * SHARE, BUSES), lambda j: (j, 0)),
            pl.BlockSpec((COLS, BUSES), lambda j: (0, 0)),
        ],
        out_specs=[pl.BlockSpec((SHARE, COLS), lambda j: (j, 0))] * 2 + [pl.BlockSpec((1, 8, SHARE), lambda j: (j, 0, 0))],
        out_shape=[half, half, jax.ShapeDtypeStruct((PAIRS, 8, SHARE), F32)],
        scratch_shapes=[pltpu.VMEM((2 * SHARE, COLS), F32)],
        compiler_params=pltpu.CompilerParams(vmem_limit_bytes=WIDE),
        name="net_flow",
    )(parity, factors, load)


def hour_levels(level):
    column = lax.broadcasted_iota(jnp.int32, (HOURS, COLS), 1)
    row = lax.broadcasted_iota(jnp.int32, (HOURS, COLS), 0)
    here = jnp.bitwise_and(column, HOURS - 1) == row
    first, second = [jnp.where(here, piece.astype(F32), 0.0) for piece in split2(level)]
    ones = jnp.where(row < 2, 1.0, 0.0)
    return jnp.concatenate([first, second, first, ones], axis=0).astype(BF16)


def capacity_part(factors, capacity):
    half = BUSES // 2
    given = jnp.transpose(dot_nt(factors[:, 0:half], capacity[:, 0:half]) + dot_nt(factors[:, half:], capacity[:, half:]))
    return given[0:8] + given[8:16]


def left_side(given, high, low, value):
    first, second = [piece.astype(F32) for piece in split2(given)]
    row = lax.broadcasted_iota(jnp.int32, (8, SHARE), 0)
    constant = jnp.where(row == 0, high, jnp.where(row == 1, low, 0.0))
    both = jnp.transpose(jnp.concatenate([first, first, second, constant, jnp.broadcast_to(value, (8, SHARE))], axis=0))
    return both[:, 0:32].astype(BF16), both[:, 32:33]


def send_kernel(place, units, factors, level, other, top, capacity_out, send_a, send_b, stage, tops, powers, semaphores):
    loads = (
        pltpu.make_async_copy(other, stage, semaphores.at[0]),
        pltpu.make_async_copy(top, tops, semaphores.at[1]),
    )
    for load in loads:
        load.start()
    parity = jnp.bitwise_and(place[0], 1)
    first = (place[0] * BUSES).astype(F32)
    lows = lax.broadcasted_iota(jnp.int32, (128, 512), 0).astype(F32)
    totals = [jnp.zeros((128, 128), F32), jnp.zeros((128, 128), F32)]
    for src in range(BUS_AXIS):
        values = jnp.concatenate([units[src, 8 * part : 8 * part + 8, :] for part in range(4)], axis=1)
        local = jnp.concatenate([units[src, 32 + part : 33 + part, :] for part in range(4)], axis=1) - first
        high = jnp.floor(local * (1.0 / 128.0))
        low = local - high * 128.0
        pieces = [piece.astype(F32) for piece in split2(values)]
        work = [jnp.where(high == float(block), piece, 0.0) for piece in pieces for block in range(8)]
        match = jnp.where(lows == low, 1.0, 0.0).astype(BF16)
        totals[src % 2] = totals[src % 2] + dot_nt(jnp.concatenate(work, axis=0).astype(BF16), match)
    total = totals[0] + totals[1]
    total = total[0:64] + total[64:128]
    capacity = jnp.concatenate([total[8 * block : 8 * block + 8] for block in range(8)], axis=1)
    capacity = jnp.concatenate(split2(capacity), axis=0)
    capacity_out[...] = capacity.astype(F32)
    right = hour_levels(level[0:1, :])
    most = jnp.max(jnp.abs(level[0:1, :]), axis=1, keepdims=True)
    powers[...] = jnp.zeros_like(powers)
    for load in loads:
        load.wait()
    for pair in range(PAIRS):
        row = pl.multiple_of((2 * pair + 1 - parity) * SHARE, SHARE)
        given = capacity_part(factors[pl.ds(row, SHARE), :], capacity)
        power = power_of(tops[pair, 0:1, :] + jnp.max(jnp.abs(given), axis=0, keepdims=True) * most)
        powers[pair : pair + 1, 0:SHARE] = power
        unit = jnp.exp2(power * -0.125) * CODE
        left, unit = left_side(given * unit, OFFSET - 0.5, 0.5, unit)
        for index, out in enumerate((send_a, send_b)):
            for start in range(0, HALF, 32):
                some = slice(index * HALF + start, index * HALF + start + 32)
                rows = slice(pair * SHARE + some.start, pair * SHARE + some.stop)
                code = wrapped(dot_nn(left[some], right) - stage[rows, :] * unit[some])
                out[pair * HALF + start : pair * HALF + start + 32, :] = code
    for out in (send_a, send_b):
        out[PAIRS * HALF : PAIRS * HALF + 8, :] = powers[...].astype(jnp.int32).astype(jnp.int16)


def sent_flow(place, units, factors, level, other, top):
    whole = pl.BlockSpec(memory_space=pltpu.VMEM)
    anywhere = pl.BlockSpec(memory_space=pl.ANY)
    sent = jax.ShapeDtypeStruct((PAIRS * HALF + 8, COLS), jnp.int16)
    return pl.pallas_call(
        send_kernel,
        in_specs=[pl.BlockSpec(memory_space=pltpu.SMEM), whole, whole, whole, anywhere, anywhere],
        out_specs=[whole, whole, whole],
        out_shape=[pltpu.VMEM((2 * HOURS, BUSES), F32), sent, sent],
        scratch_shapes=[
            pltpu.VMEM((PAIRS * SHARE, COLS), F32),
            pltpu.VMEM((PAIRS, 8, SHARE), F32),
            pltpu.VMEM((8, COLS), F32),
            pltpu.SemaphoreType.DMA((2,)),
        ],
        compiler_params=pltpu.CompilerParams(vmem_limit_bytes=WIDE),
        name="sent_flow",
    )(place, near(units), factors, near(level), other, top)


def kept_kernel(place, capacity, factors, net, level, out, top):
    side = 2 * pl.program_id(0) + jnp.bitwise_and(place[0], 1)
    rows = pl.ds(pl.multiple_of(side * SHARE, SHARE), SHARE)
    given = capacity_part(factors[rows, :], capacity[...].astype(BF16))
    left, _ = left_side(given, 0.0, 0.0, given[0:1])
    part = dot_nn(left, hour_levels(level[0:1, :])) - net[...]
    out[...] = part
    top[0] = jnp.broadcast_to(as_row(jnp.max(jnp.abs(part), axis=1, keepdims=True)), (8, SHARE))


def kept_flow(place, capacity, factors, net, level):
    whole = pl.BlockSpec(memory_space=pltpu.VMEM)
    return pl.pallas_call(
        kept_kernel,
        grid=(PAIRS,),
        in_specs=[
            pl.BlockSpec(memory_space=pltpu.SMEM),
            whole,
            whole,
            pl.BlockSpec((SHARE, COLS), lambda j: (j, 0)),
            whole,
        ],
        out_specs=[pl.BlockSpec((SHARE, COLS), lambda j: (j, 0)), pl.BlockSpec((1, 8, SHARE), lambda j: (j, 0, 0))],
        out_shape=[
            pltpu.VMEM((PAIRS * SHARE, COLS), F32),
            pltpu.VMEM((PAIRS, 8, SHARE), F32),
        ],
        compiler_params=pltpu.CompilerParams(vmem_limit_bytes=VMEM),
        name="kept_flow",
    )(place, near(capacity), factors, net, near(level))


def pair_kernel(part, top, code_a, code_b, power_a, power_b, coded):
    here = lax.broadcasted_iota(jnp.int32, (8, 256), 0) == pl.program_id(0)
    lane = lax.broadcasted_iota(jnp.int32, (1, 256), 1)
    rows = [
        jnp.sum(jnp.where(here, from_code(power[:, 0:256]), 0.0), axis=0, keepdims=True) for power in (power_a, power_b)
    ]
    unit = unit_of(jnp.where(lane < HALF, rows[0], rows[1]))[:, 0:SHARE]
    power = power_of(top[0, 0:1, :] + unit * CODE)
    again = jnp.exp2(power * -0.125) * CODE
    scales = [jnp.broadcast_to(scale, (8, SHARE)) for scale in (unit * again, again)]
    scales = jnp.transpose(jnp.concatenate(scales, axis=0))
    for index, code in enumerate((code_a, code_b)):
        for start in range(0, HALF, 32):
            some = slice(index * HALF + start, index * HALF + start + 32)
            value = part[some, :] * scales[some, 8:9] + OFFSET
            coded[0, some, :] = wrapped(value + from_code(code[start : start + 32, :]) * scales[some, 0:1])
    across = jnp.concatenate([jnp.broadcast_to(power, (8, SHARE)), jnp.zeros((8, COLS - SHARE), F32)], axis=1)
    coded[0, SHARE : SHARE + 8, :] = across.astype(jnp.int32).astype(jnp.int16)


def pair_flow(part, top, code_a, code_b):
    lines = pl.BlockSpec((HALF, COLS), lambda j: (j, 0))
    tail = pl.BlockSpec((8, COLS), lambda j: (PAIRS * HALF // 8, 0))
    return pl.pallas_call(
        pair_kernel,
        grid=(PAIRS,),
        in_specs=[
            pl.BlockSpec((SHARE, COLS), lambda j: (j, 0)),
            pl.BlockSpec((1, 8, SHARE), lambda j: (j, 0, 0)),
            lines,
            lines,
            tail,
            tail,
        ],
        out_specs=pl.BlockSpec((1, SHARE + 8, COLS), lambda j: (j, 0, 0)),
        out_shape=pltpu.HBM((PAIRS, SHARE + 8, COLS), jnp.int16),
        compiler_params=pltpu.CompilerParams(vmem_limit_bytes=VMEM),
        name="pair_flow",
    )(part, top, code_a, code_b, code_a, code_b)


def excess_kernel(coded, limit, rows, current, target, out):
    level = rows[0:1, :]
    weight = rows[1:2, :]
    cluster = rows[2:3, :]
    column = lax.broadcasted_iota(jnp.int32, (1, COLS), 1)
    hour = jnp.bitwise_and(column, HOURS - 1)
    power = jnp.concatenate([from_code(coded[src, SHARE : SHARE + 8, 0:SHARE])[0:1] for src in range(PAIRS)] * 2, axis=0)
    unit = unit_of(jnp.transpose(power))
    flow = from_code(coded[0, 0:SHARE, :]) * unit[:, 0:1]
    for src in range(1, PAIRS):
        flow = flow + from_code(coded[src, 0:SHARE, :]) * unit[:, src : src + 1]
    edge = limit[:, 0:1]
    excess = flow - jnp.clip(flow, -edge, edge)
    p0, p1 = split2(excess * (level * weight))
    e0, e1 = split2(excess * excess * (0.5 * weight))
    key = cluster * float(HOURS) + hour.astype(F32)
    row = lax.broadcasted_iota(jnp.int32, (COLS, COLS), 0)
    inner = jnp.bitwise_and(row, ROWS - 1)
    owner = jnp.right_shift(row, 6)
    mine = (jnp.right_shift(inner, 3) * SCEN_AXIS + owner) * HOURS + jnp.bitwise_and(inner, HOURS - 1)
    pick = jnp.where(mine.astype(F32) == key, 1.0, 0.0).astype(BF16)
    pushed = dot_nt(pick, p0) + dot_nt(pick, p1)
    row = lax.broadcasted_iota(jnp.int32, (128, COLS), 0)
    inner = jnp.bitwise_and(row, 15)
    owner = jnp.right_shift(row, 4)
    mine = jnp.where(inner < 8, inner * SCEN_AXIS + owner, owner * OWNED + inner - 8)
    pick = jnp.where(mine.astype(F32) == cluster, 1.0, 0.0).astype(BF16)
    pooled = dot_nt(pick, e0) + dot_nt(pick, e1)
    lane = lax.broadcasted_iota(jnp.int32, (128, 128), 1)
    last = lax.broadcasted_iota(jnp.int32, (8, SHARE), 0)
    table = jnp.zeros((128, 128), F32)
    blocks = []
    for dest in range(SCEN_AXIS):
        given = jnp.where(last == 0, current[dest : dest + 1, :], jnp.where(last == 1, target[dest : dest + 1, 0:1], 0.0))
        block, power = coded_rows(
            pushed[dest * ROWS : dest * ROWS + ROWS],
            jnp.concatenate([pooled[dest * 16 : dest * 16 + 16], given], axis=0),
        )
        table = jnp.where(lane == dest, power, table)
        blocks.append(block)
    table = jnp.transpose(table)
    for dest in range(SCEN_AXIS):
        tail = jnp.broadcast_to(table[dest : dest + 1], (8, 128))
        out[dest] = jnp.concatenate([blocks[dest], tail], axis=0).astype(jnp.int32).astype(jnp.int16)


def excess_sums(coded, limit, rows, current, target):
    return pl.pallas_call(
        excess_kernel,
        in_specs=[pl.BlockSpec(memory_space=pltpu.VMEM)] * 5,
        out_specs=pl.BlockSpec(memory_space=pltpu.VMEM),
        out_shape=pltpu.VMEM((SCEN_AXIS, POOLED, 128), jnp.int16),
        compiler_params=pltpu.CompilerParams(vmem_limit_bytes=VMEM),
        name="excess_sums",
    )(near(coded), near(limit), near(rows), near(current), near(target))


def update_kernel(sums, current, target, out):
    tables = jnp.concatenate([from_code(sums[src, POOLED - 16 : POOLED, :])[15:16] for src in range(SCEN_AXIS)], axis=0)
    units = unit_of(jnp.transpose(tables))
    pushed = jnp.zeros((ROWS, SHARE), F32)
    pooled = jnp.zeros((16, SHARE), F32)
    given = []
    for src in range(SCEN_AXIS):
        rough, fine = decoded_rows(from_code(sums[src]), units[:, src : src + 1], 24)
        pushed = pushed + rough
        pooled = pooled + fine[0:16]
        given.append(fine[16:24])
    spread = jnp.concatenate([part[0:1] for part in given], axis=0)
    spread_target = jnp.concatenate([part[1:2, 0:1] for part in given], axis=0)
    chosen = jnp.maximum(spread + STEP * (pooled[0:8] - spread_target), 0.0)
    owned = jnp.maximum(current[...] + STEP * (pooled[8:16] - target[:, 0:1]), 0.0)
    wide = jnp.concatenate([pushed[8 * i : 8 * i + 8] * chosen[i : i + 1] for i in range(OWNED)], axis=0)
    block, power = coded_rows(wide, owned)
    tail = jnp.broadcast_to(as_row(power), (8, 128))
    block = jnp.concatenate([block, tail], axis=0).astype(jnp.int32).astype(jnp.int16)
    for dest in range(BUS_AXIS):
        out[dest] = block


def updated(sums, current, target):
    return pl.pallas_call(
        update_kernel,
        in_specs=[pl.BlockSpec(memory_space=pltpu.VMEM)] * 3,
        out_specs=pl.BlockSpec(memory_space=pltpu.VMEM),
        out_shape=jax.ShapeDtypeStruct((BUS_AXIS, UPDATED, 128), jnp.int16),
        compiler_params=pltpu.CompilerParams(vmem_limit_bytes=VMEM),
        name="update",
    )(near(sums), near(current), near(target))


def slopes_kernel(packed, factors, slopes, duals):
    tables = jnp.concatenate([from_code(packed[src, UPDATED - 16 : UPDATED, :])[15:16] for src in range(BUS_AXIS)], axis=0)
    units = unit_of(jnp.transpose(tables))
    total = jnp.zeros((2 * ROWS, BUSES), F32)
    for src in range(BUS_AXIS):
        wide, duals[src] = decoded_rows(from_code(packed[src]), units[:, src : src + 1], 8)
        pieces = jnp.concatenate(split2(wide), axis=0)
        total = total + dot_nn(pieces, factors[src * SHARE : src * SHARE + SHARE, :])
    slopes[...] = total[0:ROWS] + total[ROWS:]


def slopes_of(packed, factors):
    return pl.pallas_call(
        slopes_kernel,
        in_specs=[pl.BlockSpec(memory_space=pltpu.VMEM)] * 2,
        out_specs=[pl.BlockSpec(memory_space=pltpu.VMEM)] * 2,
        out_shape=[
            jax.ShapeDtypeStruct((ROWS, BUSES), F32),
            jax.ShapeDtypeStruct((BUS_AXIS, 8, SHARE), F32),
        ],
        compiler_params=pltpu.CompilerParams(vmem_limit_bytes=VMEM),
        name="slopes",
    )(near(packed), factors)


NEAR_A = [(i, i ^ 1) for i in range(BUS_AXIS)]
NEAR_B = [(i, (i + 1 if i % 2 else i - 1) % BUS_AXIS) for i in range(BUS_AXIS)]
SAME_PARITY = [list(range(0, BUS_AXIS, 2)), list(range(1, BUS_AXIS, 2))]


def exchange(tiles, axis):
    return lax.all_to_all(tiles, axis, 0, 0, tiled=True)


def near(x):
    return pltpu.with_memory_space_constraint(x, pltpu.VMEM)


def per_device(
    shift_factors,
    net_load,
    dispatch_level,
    scenario_weight,
    cluster_id,
    commitment,
    unit_capacity,
    unit_bus,
    line_limit,
    multipliers,
    penalty_target,
):
    place = lax.axis_index("bus")
    factors = near(shift_factors)
    units = exchange(packed_units(commitment, unit_capacity, unit_bus), "bus")
    parity = jnp.bitwise_and(place, 1)
    keep, other, top = net_flow(parity.reshape(1), shift_factors, net_load.reshape(COLS, BUSES))
    keep, dispatch_level, scenario_weight, cluster_id = lax.optimization_barrier(
        (keep, dispatch_level, scenario_weight, cluster_id)
    )
    rows = jnp.stack(
        [
            dispatch_level.reshape(COLS),
            jnp.repeat(scenario_weight, HOURS),
            jnp.repeat(cluster_id[:, 0].astype(F32), HOURS),
        ],
        axis=0,
    )
    capacity, send_a, send_b = sent_flow(place.reshape(1), units, factors, rows, other, top)
    code_a = lax.ppermute(send_a, "bus", NEAR_A)
    code_b = lax.ppermute(send_b, "bus", NEAR_B)
    part, top = kept_flow(place.reshape(1), capacity, factors, keep, rows)
    coded = pair_flow(part, top, code_a, code_b)
    received = lax.all_to_all(coded, "bus", 0, 0, axis_index_groups=SAME_PARITY, tiled=True)

    limit = lax.dynamic_slice_in_dim(line_limit, place * SHARE, SHARE, 0).reshape(SHARE, 1)
    current = lax.dynamic_slice_in_dim(multipliers, place * SHARE, SHARE, 1)
    target = penalty_target.reshape(OWNED, 1)
    sums = exchange(excess_sums(received, limit, rows, current, target), "scen")
    packed = exchange(updated(sums, current, target), "bus")
    slopes, duals = slopes_of(packed, factors)
    slopes = exchange(slopes.reshape(LINE_AXIS, HOURS, BUSES), "line")
    dual_out = jnp.moveaxis(duals, 0, 1).reshape(OWNED, LINES)
    return dual_out, jnp.sum(slopes, axis=0, keepdims=True)


def solution(mesh):
    placed = (
        P("line", "bus"),
        P("scen", None, "bus"),
        P("scen", None),
        P("scen"),
        P("scen", None),
        P(None, "bus"),
        P("bus"),
        P("bus"),
        P("line"),
        P("scen", "line"),
        P("scen"),
    )

    return jax.shard_map(
        per_device,
        mesh=mesh,
        in_specs=placed,
        out_specs=(P("scen", "line"), P(("line", "scen"), None, "bus")),
        check_vma=False,
    )
```

```python
import jax
import jax.numpy as jnp
from jax import lax
from jax.experimental import pallas as pl
from jax.experimental.pallas import tpu as pltpu
from jax.sharding import PartitionSpec as P


BUS_AXIS = 8
LINE_AXIS = 8
SCEN_AXIS = 8
LINES = 1536
SHARE = LINES // BUS_AXIS
HALF = SHARE // 2
PAIRS = BUS_AXIS // 2
BUSES = 1024
SCEN = 64
HOURS = 8
COLS = SCEN * HOURS
OWNED = 8
ROWS = OWNED * HOURS
STEP = 0.1
CODE = 32000.0
FINE = 60000.0
OFFSET = 65536.5
POOLED = 176
UPDATED = 128
VMEM = 20 * 1024 * 1024
WIDE = 56 * 1024 * 1024
MIDDLE = 50 * 1024 * 1024

F32 = jnp.float32
BF16 = jnp.bfloat16


def dot_nt(a, b):
    return lax.dot_general(a, b, (((1,), (1,)), ((), ())), preferred_element_type=F32)


def dot_nn(a, b):
    return lax.dot_general(a, b, (((1,), (0,)), ((), ())), preferred_element_type=F32)


def split2(x):
    high = x.astype(BF16)
    return high, (x - high.astype(F32)).astype(BF16)


def power_of(top):
    return jnp.ceil(jnp.log2(jnp.maximum(top, 1e-30)) * 8.0)


def powers_of(part):
    return power_of(jnp.max(jnp.abs(part), axis=1, keepdims=True))


def rounded(x):
    return jnp.floor(x + 0.5)


def wrapped(x):
    return x.astype(jnp.int32).astype(jnp.int16)


def from_code(code):
    return code.astype(jnp.int32).astype(F32)


def unit_of(power):
    return jnp.exp2(power * 0.125) * (1.0 / CODE)


def coded_rows(rough, fine):
    rough_power = powers_of(rough)
    fine_power = powers_of(fine)
    rough = rounded(rough * (jnp.exp2(rough_power * -0.125) * CODE))
    fine = fine * (jnp.exp2(fine_power * -0.125) * CODE)
    high = rounded(fine)
    both = jnp.concatenate([rough, high, rounded((fine - high) * FINE)], axis=0)
    half = both.shape[0] // 2
    tail = jnp.concatenate([both[0:half, 128:SHARE], both[half:, 128:SHARE]], axis=1)
    blank = jnp.zeros((128 - rough_power.shape[0] - fine_power.shape[0], 1), F32)
    return jnp.concatenate([both[:, 0:128], tail], axis=0), jnp.concatenate([rough_power, fine_power, blank], axis=0)


def decoded_rows(block, unit, count):
    rows = ROWS + 2 * count
    tail = block[rows : rows + rows // 2]
    tail = jnp.concatenate([tail[:, 0:64], tail[:, 64:128]], axis=0)
    both = jnp.concatenate([block[0:rows], tail], axis=1)
    fine = both[ROWS : ROWS + count] + both[ROWS + count : rows] * (1.0 / FINE)
    return both[0:ROWS] * unit[0:ROWS], fine * unit[ROWS : ROWS + count]


def as_row(column):
    return jnp.transpose(jnp.broadcast_to(column, (column.shape[0], 128)))[0:1]


def units_kernel(commitment, capacity, bus, out):
    values = commitment[...].astype(F32) * capacity[...]
    where = bus[...].astype(F32)
    blank = jnp.zeros((8, 128), F32)
    row = lax.broadcasted_iota(jnp.int32, (8, 128), 0)
    for part in range(4):
        blank = jnp.where(row == part, where[:, 128 * part : 128 * part + 128], blank)
    for dest in range(BUS_AXIS):
        for part in range(4):
            out[dest, 8 * part : 8 * part + 8, :] = values[:, 128 * part : 128 * part + 128]
        out[dest, 32:40, :] = blank


def packed_units(commitment, capacity, bus):
    return pl.pallas_call(
        units_kernel,
        out_shape=jax.ShapeDtypeStruct((BUS_AXIS, 40, 128), F32),
        compiler_params=pltpu.CompilerParams(vmem_limit_bytes=WIDE),
        name="units",
    )(commitment, capacity.reshape(1, 512), bus.reshape(1, 512))


def net_flow_kernel(parity, factors, load, keep, other, top, work):
    work[...] = dot_nt(factors[...], load[...])
    keep[...] = work[pl.ds(pl.multiple_of(parity[0] * SHARE, SHARE), SHARE), :]
    part = work[pl.ds(pl.multiple_of((1 - parity[0]) * SHARE, SHARE), SHARE), :]
    other[...] = part
    top[0] = jnp.broadcast_to(as_row(jnp.max(jnp.abs(part), axis=1, keepdims=True)), (8, SHARE))


def net_flow(parity, factors, load):
    half = pltpu.HBM((PAIRS * SHARE, COLS), F32)
    return pl.pallas_call(
        net_flow_kernel,
        grid=(PAIRS,),
        in_specs=[
            pl.BlockSpec(memory_space=pltpu.SMEM),
            pl.BlockSpec((2 * SHARE, BUSES), lambda j: (j, 0)),
            pl.BlockSpec((COLS, BUSES), lambda j: (0, 0)),
        ],
        out_specs=[pl.BlockSpec((SHARE, COLS), lambda j: (j, 0))] * 2 + [pl.BlockSpec((1, 8, SHARE), lambda j: (j, 0, 0))],
        out_shape=[half, half, pltpu.HBM((PAIRS, 8, SHARE), F32)],
        scratch_shapes=[pltpu.VMEM((2 * SHARE, COLS), F32)],
        compiler_params=pltpu.CompilerParams(vmem_limit_bytes=WIDE),
        name="net_flow",
    )(parity, factors, load)


def hour_levels(level):
    column = lax.broadcasted_iota(jnp.int32, (HOURS, COLS), 1)
    row = lax.broadcasted_iota(jnp.int32, (HOURS, COLS), 0)
    here = jnp.bitwise_and(column, HOURS - 1) == row
    first, second = [jnp.where(here, piece.astype(F32), 0.0) for piece in split2(level)]
    ones = jnp.where(row < 2, 1.0, 0.0)
    return jnp.concatenate([first, second, first, ones], axis=0).astype(BF16)


def capacity_part(factors, capacity):
    half = BUSES // 2
    given = jnp.transpose(dot_nt(factors[:, 0:half], capacity[:, 0:half]) + dot_nt(factors[:, half:], capacity[:, half:]))
    return given[0:8] + given[8:16]


def left_side(given, high, low, value):
    first, second = [piece.astype(F32) for piece in split2(given)]
    row = lax.broadcasted_iota(jnp.int32, (8, SHARE), 0)
    constant = jnp.where(row == 0, high, jnp.where(row == 1, low, 0.0))
    both = jnp.transpose(jnp.concatenate([first, first, second, constant, jnp.broadcast_to(value, (8, SHARE))], axis=0))
    return both[:, 0:32].astype(BF16), both[:, 32:33]


def send_kernel(place, units, factors, level, other, top, capacity_out, send_a, send_b, stage, tops, powers, semaphores):
    loads = (
        pltpu.make_async_copy(other, stage, semaphores.at[0]),
        pltpu.make_async_copy(top, tops, semaphores.at[1]),
    )
    for load in loads:
        load.start()
    parity = jnp.bitwise_and(place[0], 1)
    first = (place[0] * BUSES).astype(F32)
    lows = lax.broadcasted_iota(jnp.int32, (128, 512), 0).astype(F32)
    totals = [jnp.zeros((128, 128), F32), jnp.zeros((128, 128), F32)]
    for src in range(BUS_AXIS):
        values = jnp.concatenate([units[src, 8 * part : 8 * part + 8, :] for part in range(4)], axis=1)
        local = jnp.concatenate([units[src, 32 + part : 33 + part, :] for part in range(4)], axis=1) - first
        high = jnp.floor(local * (1.0 / 128.0))
        low = local - high * 128.0
        pieces = [piece.astype(F32) for piece in split2(values)]
        work = [jnp.where(high == float(block), piece, 0.0) for piece in pieces for block in range(8)]
        match = jnp.where(lows == low, 1.0, 0.0).astype(BF16)
        totals[src % 2] = totals[src % 2] + dot_nt(jnp.concatenate(work, axis=0).astype(BF16), match)
    total = totals[0] + totals[1]
    total = total[0:64] + total[64:128]
    capacity = jnp.concatenate([total[8 * block : 8 * block + 8] for block in range(8)], axis=1)
    capacity = jnp.concatenate(split2(capacity), axis=0)
    capacity_out[...] = capacity.astype(F32)
    right = hour_levels(level[0:1, :])
    most = jnp.max(jnp.abs(level[0:1, :]), axis=1, keepdims=True)
    powers[...] = jnp.zeros_like(powers)
    for load in loads:
        load.wait()
    for pair in range(PAIRS):
        row = pl.multiple_of((2 * pair + 1 - parity) * SHARE, SHARE)
        given = capacity_part(factors[pl.ds(row, SHARE), :], capacity)
        power = power_of(tops[pair, 0:1, :] + jnp.max(jnp.abs(given), axis=0, keepdims=True) * most)
        powers[pair : pair + 1, 0:SHARE] = power
        unit = jnp.exp2(power * -0.125) * CODE
        left, unit = left_side(given * unit, OFFSET - 0.5, 0.5, unit)
        for index, out in enumerate((send_a, send_b)):
            for start in range(0, HALF, 32):
                some = slice(index * HALF + start, index * HALF + start + 32)
                rows = slice(pair * SHARE + some.start, pair * SHARE + some.stop)
                code = wrapped(dot_nn(left[some], right) - stage[rows, :] * unit[some])
                out[pair * HALF + start : pair * HALF + start + 32, :] = code
    for out in (send_a, send_b):
        out[PAIRS * HALF : PAIRS * HALF + 8, :] = powers[...].astype(jnp.int32).astype(jnp.int16)


def sent_flow(place, units, factors, level, other, top):
    whole = pl.BlockSpec(memory_space=pltpu.VMEM)
    anywhere = pl.BlockSpec(memory_space=pltpu.HBM)
    sent = jax.ShapeDtypeStruct((PAIRS * HALF + 8, COLS), jnp.int16)
    return pl.pallas_call(
        send_kernel,
        in_specs=[pl.BlockSpec(memory_space=pltpu.SMEM), whole, whole, whole, anywhere, anywhere],
        out_specs=[whole, whole, whole],
        out_shape=[pltpu.VMEM((2 * HOURS, BUSES), F32), sent, sent],
        scratch_shapes=[
            pltpu.VMEM((PAIRS * SHARE, COLS), F32),
            pltpu.VMEM((PAIRS, 8, SHARE), F32),
            pltpu.VMEM((8, COLS), F32),
            pltpu.SemaphoreType.DMA((2,)),
        ],
        compiler_params=pltpu.CompilerParams(vmem_limit_bytes=VMEM),
        name="sent_flow",
    )(place, near(units), factors, near(level), far(other), far(top))


def kept_kernel(place, capacity, factors, net, level, out, top):
    side = 2 * pl.program_id(0) + jnp.bitwise_and(place[0], 1)
    rows = pl.ds(pl.multiple_of(side * SHARE, SHARE), SHARE)
    given = capacity_part(factors[rows, :], capacity[...].astype(BF16))
    left, _ = left_side(given, 0.0, 0.0, given[0:1])
    part = dot_nn(left, hour_levels(level[0:1, :])) - net[...]
    out[...] = part
    top[0] = jnp.broadcast_to(as_row(jnp.max(jnp.abs(part), axis=1, keepdims=True)), (8, SHARE))


def kept_flow(place, capacity, factors, net, level):
    whole = pl.BlockSpec(memory_space=pltpu.VMEM)
    return pl.pallas_call(
        kept_kernel,
        grid=(PAIRS,),
        in_specs=[
            pl.BlockSpec(memory_space=pltpu.SMEM),
            whole,
            whole,
            pl.BlockSpec((SHARE, COLS), lambda j: (j, 0)),
            whole,
        ],
        out_specs=[pl.BlockSpec((SHARE, COLS), lambda j: (j, 0)), pl.BlockSpec((1, 8, SHARE), lambda j: (j, 0, 0))],
        out_shape=[
            pltpu.VMEM((PAIRS * SHARE, COLS), F32),
            pltpu.VMEM((PAIRS, 8, SHARE), F32),
        ],
        compiler_params=pltpu.CompilerParams(vmem_limit_bytes=MIDDLE),
        name="kept_flow",
    )(place, near(capacity), factors, net, near(level))


def pair_kernel(part, top, code_a, code_b, power_a, power_b, coded):
    here = lax.broadcasted_iota(jnp.int32, (8, 256), 0) == pl.program_id(0)
    lane = lax.broadcasted_iota(jnp.int32, (1, 256), 1)
    rows = [
        jnp.sum(jnp.where(here, from_code(power[:, 0:256]), 0.0), axis=0, keepdims=True) for power in (power_a, power_b)
    ]
    unit = unit_of(jnp.where(lane < HALF, rows[0], rows[1]))[:, 0:SHARE]
    power = power_of(top[0, 0:1, :] + unit * CODE)
    again = jnp.exp2(power * -0.125) * CODE
    scales = [jnp.broadcast_to(scale, (8, SHARE)) for scale in (unit * again, again)]
    scales = jnp.transpose(jnp.concatenate(scales, axis=0))
    for index, code in enumerate((code_a, code_b)):
        for start in range(0, HALF, 32):
            some = slice(index * HALF + start, index * HALF + start + 32)
            value = part[some, :] * scales[some, 8:9] + OFFSET
            coded[0, some, :] = wrapped(value + from_code(code[start : start + 32, :]) * scales[some, 0:1])
    across = jnp.concatenate([jnp.broadcast_to(power, (8, SHARE)), jnp.zeros((8, COLS - SHARE), F32)], axis=1)
    coded[0, SHARE : SHARE + 8, :] = across.astype(jnp.int32).astype(jnp.int16)


def pair_flow(part, top, code_a, code_b):
    lines = pl.BlockSpec((HALF, COLS), lambda j: (j, 0))
    tail = pl.BlockSpec((8, COLS), lambda j: (PAIRS * HALF // 8, 0))
    return pl.pallas_call(
        pair_kernel,
        grid=(PAIRS,),
        in_specs=[
            pl.BlockSpec((SHARE, COLS), lambda j: (j, 0)),
            pl.BlockSpec((1, 8, SHARE), lambda j: (j, 0, 0)),
            lines,
            lines,
            tail,
            tail,
        ],
        out_specs=pl.BlockSpec((1, SHARE + 8, COLS), lambda j: (j, 0, 0)),
        out_shape=pltpu.HBM((PAIRS, SHARE + 8, COLS), jnp.int16),
        compiler_params=pltpu.CompilerParams(vmem_limit_bytes=VMEM),
        name="pair_flow",
    )(part, top, code_a, code_b, code_a, code_b)


def excess_kernel(received, limit, rows, current, target, out, coded, pick, pushes, squares, pushed, semaphores):
    loads = [pltpu.make_async_copy(received.at[src], coded.at[src], semaphores.at[src]) for src in range(PAIRS)]
    for load in loads:
        load.start()
    level = rows[0:1, :]
    weight = rows[1:2, :]
    cluster = rows[2:3, :]
    column = lax.broadcasted_iota(jnp.int32, (1, COLS), 1)
    hour = jnp.bitwise_and(column, HOURS - 1)
    key = cluster * float(HOURS) + hour.astype(F32)
    for owner in range(SCEN_AXIS):
        inner = lax.broadcasted_iota(jnp.int32, (ROWS, COLS), 0)
        mine = (jnp.right_shift(inner, 3) * SCEN_AXIS + owner) * HOURS + jnp.bitwise_and(inner, HOURS - 1)
        pick[owner * ROWS : owner * ROWS + ROWS, :] = jnp.where(mine.astype(F32) == key, 1.0, 0.0).astype(BF16)
    row = lax.broadcasted_iota(jnp.int32, (128, COLS), 0)
    inner = jnp.bitwise_and(row, 15)
    owner = jnp.right_shift(row, 4)
    mine = jnp.where(inner < 8, inner * SCEN_AXIS + owner, owner * OWNED + inner - 8)
    pick[COLS : COLS + 128, :] = jnp.where(mine.astype(F32) == cluster, 1.0, 0.0).astype(BF16)
    scaled = level * weight
    half = 0.5 * weight
    for load in loads:
        load.wait()
    power = jnp.concatenate([from_code(coded[src, SHARE : SHARE + 8, 0:SHARE])[0:1] for src in range(PAIRS)] * 2, axis=0)
    unit = unit_of(jnp.transpose(power))
    for start in range(0, SHARE, 32):
        some = slice(start, start + 32)
        flow = from_code(coded[0, some, :]) * unit[some, 0:1]
        for src in range(1, PAIRS):
            flow = flow + from_code(coded[src, some, :]) * unit[some, src : src + 1]
        edge = limit[some, 0:1]
        excess = flow - jnp.clip(flow, -edge, edge)
        for out_ref, value in ((pushes, excess * scaled), (squares, excess * excess * half)):
            out_ref[some, 0:COLS], out_ref[some, COLS:] = split2(value)
    twice = pick[0:COLS, :]
    pushed[...] = dot_nt(jnp.concatenate([twice, twice], axis=1), pushes[...])
    twice = pick[COLS:, :]
    pooled = dot_nt(jnp.concatenate([twice, twice], axis=1), squares[...])
    lane = lax.broadcasted_iota(jnp.int32, (128, 128), 1)
    last = lax.broadcasted_iota(jnp.int32, (8, SHARE), 0)
    table = jnp.zeros((128, 128), F32)
    blocks = []
    for dest in range(SCEN_AXIS):
        given = jnp.where(last == 0, current[dest : dest + 1, :], jnp.where(last == 1, target[dest : dest + 1, 0:1], 0.0))
        block, power = coded_rows(
            pushed[dest * ROWS : dest * ROWS + ROWS, :],
            jnp.concatenate([pooled[dest * 16 : dest * 16 + 16], given], axis=0),
        )
        table = jnp.where(lane == dest, power, table)
        blocks.append(block)
    table = jnp.transpose(table)
    for dest in range(SCEN_AXIS):
        tail = jnp.broadcast_to(table[dest : dest + 1], (8, 128))
        out[dest] = jnp.concatenate([blocks[dest], tail], axis=0).astype(jnp.int32).astype(jnp.int16)


def excess_sums(received, limit, rows, current, target):
    return pl.pallas_call(
        excess_kernel,
        in_specs=[pl.BlockSpec(memory_space=pltpu.HBM)] + [pl.BlockSpec(memory_space=pltpu.VMEM)] * 4,
        out_specs=pl.BlockSpec(memory_space=pltpu.VMEM),
        out_shape=pltpu.VMEM((SCEN_AXIS, POOLED, 128), jnp.int16),
        scratch_shapes=[
            pltpu.VMEM((PAIRS, SHARE + 8, COLS), jnp.int16),
            pltpu.VMEM((COLS + 128, COLS), BF16),
            pltpu.VMEM((SHARE, 2 * COLS), BF16),
            pltpu.VMEM((SHARE, 2 * COLS), BF16),
            pltpu.VMEM((COLS, SHARE), F32),
            pltpu.SemaphoreType.DMA((PAIRS,)),
        ],
        compiler_params=pltpu.CompilerParams(vmem_limit_bytes=VMEM),
        name="excess_sums",
    )(received, near(limit), near(rows), near(current), near(target))


def update_kernel(sums, current, target, out):
    tables = jnp.concatenate([from_code(sums[src, POOLED - 16 : POOLED, :])[15:16] for src in range(SCEN_AXIS)], axis=0)
    units = unit_of(jnp.transpose(tables))
    pushed = jnp.zeros((ROWS, SHARE), F32)
    pooled = jnp.zeros((16, SHARE), F32)
    given = []
    for src in range(SCEN_AXIS):
        rough, fine = decoded_rows(from_code(sums[src]), units[:, src : src + 1], 24)
        pushed = pushed + rough
        pooled = pooled + fine[0:16]
        given.append(fine[16:24])
    spread = jnp.concatenate([part[0:1] for part in given], axis=0)
    spread_target = jnp.concatenate([part[1:2, 0:1] for part in given], axis=0)
    chosen = jnp.maximum(spread + STEP * (pooled[0:8] - spread_target), 0.0)
    owned = jnp.maximum(current[...] + STEP * (pooled[8:16] - target[:, 0:1]), 0.0)
    wide = jnp.concatenate([pushed[8 * i : 8 * i + 8] * chosen[i : i + 1] for i in range(OWNED)], axis=0)
    block, power = coded_rows(wide, owned)
    tail = jnp.broadcast_to(as_row(power), (8, 128))
    block = jnp.concatenate([block, tail], axis=0).astype(jnp.int32).astype(jnp.int16)
    for dest in range(BUS_AXIS):
        out[dest] = block


def updated(sums, current, target):
    return pl.pallas_call(
        update_kernel,
        in_specs=[pl.BlockSpec(memory_space=pltpu.VMEM)] * 3,
        out_specs=pl.BlockSpec(memory_space=pltpu.VMEM),
        out_shape=jax.ShapeDtypeStruct((BUS_AXIS, UPDATED, 128), jnp.int16),
        compiler_params=pltpu.CompilerParams(vmem_limit_bytes=VMEM),
        name="update",
    )(near(sums), near(current), near(target))


def slopes_kernel(packed, factors, slopes, duals):
    tables = jnp.concatenate([from_code(packed[src, UPDATED - 16 : UPDATED, :])[15:16] for src in range(BUS_AXIS)], axis=0)
    units = unit_of(jnp.transpose(tables))
    total = jnp.zeros((2 * ROWS, BUSES), F32)
    for src in range(BUS_AXIS):
        wide, duals[src] = decoded_rows(from_code(packed[src]), units[:, src : src + 1], 8)
        pieces = jnp.concatenate(split2(wide), axis=0)
        total = total + dot_nn(pieces, factors[src * SHARE : src * SHARE + SHARE, :])
    slopes[...] = total[0:ROWS] + total[ROWS:]


def slopes_of(packed, factors):
    return pl.pallas_call(
        slopes_kernel,
        in_specs=[pl.BlockSpec(memory_space=pltpu.VMEM)] * 2,
        out_specs=[pl.BlockSpec(memory_space=pltpu.VMEM)] * 2,
        out_shape=[
            jax.ShapeDtypeStruct((ROWS, BUSES), F32),
            jax.ShapeDtypeStruct((BUS_AXIS, 8, SHARE), F32),
        ],
        compiler_params=pltpu.CompilerParams(vmem_limit_bytes=VMEM),
        name="slopes",
    )(near(packed), factors)


NEAR_A = [(i, i ^ 1) for i in range(BUS_AXIS)]
NEAR_B = [(i, (i + 1 if i % 2 else i - 1) % BUS_AXIS) for i in range(BUS_AXIS)]
SAME_PARITY = [list(range(0, BUS_AXIS, 2)), list(range(1, BUS_AXIS, 2))]


def exchange(tiles, axis):
    return lax.all_to_all(tiles, axis, 0, 0, tiled=True)


def far(x):
    return pltpu.with_memory_space_constraint(x, pltpu.HBM)


def near(x):
    return pltpu.with_memory_space_constraint(x, pltpu.VMEM)


def per_device(
    shift_factors,
    net_load,
    dispatch_level,
    scenario_weight,
    cluster_id,
    commitment,
    unit_capacity,
    unit_bus,
    line_limit,
    multipliers,
    penalty_target,
):
    place = lax.axis_index("bus")
    factors = near(shift_factors)
    units = exchange(packed_units(commitment, unit_capacity, unit_bus), "bus")
    parity = jnp.bitwise_and(place, 1)
    keep, other, top = net_flow(parity.reshape(1), shift_factors, net_load.reshape(COLS, BUSES))
    keep, dispatch_level, scenario_weight, cluster_id = lax.optimization_barrier(
        (keep, dispatch_level, scenario_weight, cluster_id)
    )
    rows = jnp.stack(
        [
            dispatch_level.reshape(COLS),
            jnp.repeat(scenario_weight, HOURS),
            jnp.repeat(cluster_id[:, 0].astype(F32), HOURS),
        ],
        axis=0,
    )
    capacity, send_a, send_b = sent_flow(place.reshape(1), units, factors, rows, other, top)
    code_a = lax.ppermute(send_a, "bus", NEAR_A)
    code_b = lax.ppermute(send_b, "bus", NEAR_B)
    part, top = kept_flow(place.reshape(1), capacity, factors, keep, rows)
    coded = pair_flow(part, top, code_a, code_b)
    received = lax.all_to_all(coded, "bus", 0, 0, axis_index_groups=SAME_PARITY, tiled=True)

    limit = lax.dynamic_slice_in_dim(line_limit, place * SHARE, SHARE, 0).reshape(SHARE, 1)
    current = lax.dynamic_slice_in_dim(multipliers, place * SHARE, SHARE, 1)
    target = penalty_target.reshape(OWNED, 1)
    sums = exchange(excess_sums(received, limit, rows, current, target), "scen")
    packed = exchange(updated(sums, current, target), "bus")
    slopes, duals = slopes_of(packed, factors)
    slopes = exchange(slopes.reshape(LINE_AXIS, HOURS, BUSES), "line")
    dual_out = jnp.moveaxis(duals, 0, 1).reshape(OWNED, LINES)
    return dual_out, jnp.sum(slopes, axis=0, keepdims=True)


def solution(mesh):
    placed = (
        P("line", "bus"),
        P("scen", None, "bus"),
        P("scen", None),
        P("scen"),
        P("scen", None),
        P(None, "bus"),
        P("bus"),
        P("bus"),
        P("line"),
        P("scen", "line"),
        P("scen"),
    )

    return jax.shard_map(
        per_device,
        mesh=mesh,
        in_specs=placed,
        out_specs=(P("scen", "line"), P(("line", "scen"), None, "bus")),
        check_vma=False,
    )
```

```python
import jax
import jax.numpy as jnp
from jax import lax
from jax.experimental import pallas as pl
from jax.experimental.pallas import tpu as pltpu
from jax.sharding import PartitionSpec as P


BUS_AXIS = 8
LINE_AXIS = 8
SCEN_AXIS = 8
LINES = 1536
SHARE = LINES // BUS_AXIS
HALF = SHARE // 2
PAIRS = BUS_AXIS // 2
BUSES = 1024
SCEN = 64
HOURS = 8
COLS = SCEN * HOURS
OWNED = 8
ROWS = OWNED * HOURS
STEP = 0.1
CODE = 32000.0
FINE = 60000.0
OFFSET = 65536.5
POOLED = 144
UPDATED = 128
VMEM = 20 * 1024 * 1024
WIDE = 56 * 1024 * 1024
MIDDLE = 50 * 1024 * 1024

F32 = jnp.float32
BF16 = jnp.bfloat16


def dot_nt(a, b):
    return lax.dot_general(a, b, (((1,), (1,)), ((), ())), preferred_element_type=F32)


def dot_nn(a, b):
    return lax.dot_general(a, b, (((1,), (0,)), ((), ())), preferred_element_type=F32)


def split2(x):
    high = x.astype(BF16)
    return high, (x - high.astype(F32)).astype(BF16)


def power_of(top):
    return jnp.ceil(jnp.log2(jnp.maximum(top, 1e-30)) * 8.0)


def powers_of(part):
    return power_of(jnp.max(jnp.abs(part), axis=1, keepdims=True))


def rounded(x):
    return jnp.floor(x + 0.5)


def wrapped(x):
    return x.astype(jnp.int32).astype(jnp.int16)


def from_code(code):
    return code.astype(jnp.int32).astype(F32)


def unit_of(power):
    return jnp.exp2(power * 0.125) * (1.0 / CODE)


def coded_rows(rough, fine):
    rough_power = powers_of(rough)
    fine_power = powers_of(fine)
    rough = rounded(rough * (jnp.exp2(rough_power * -0.125) * CODE))
    fine = fine * (jnp.exp2(fine_power * -0.125) * CODE)
    high = rounded(fine)
    both = jnp.concatenate([rough, high, rounded((fine - high) * FINE)], axis=0)
    half = both.shape[0] // 2
    tail = jnp.concatenate([both[0:half, 128:SHARE], both[half:, 128:SHARE]], axis=1)
    blank = jnp.zeros((128 - rough_power.shape[0] - fine_power.shape[0], 1), F32)
    return jnp.concatenate([both[:, 0:128], tail], axis=0), jnp.concatenate([rough_power, fine_power, blank], axis=0)


def coded_pool(rough, fine):
    rough_power = powers_of(rough)
    fine_power = powers_of(fine)
    scaled = [part * (jnp.exp2(power * -0.125) * CODE) for part, power in ((rough, rough_power), (fine, fine_power))]
    both = rounded(jnp.concatenate(scaled, axis=0))
    right = jnp.concatenate([both[48:88, 128:SHARE], jnp.zeros((8, 64), F32)], axis=0)
    tail = jnp.concatenate([both[0:48, 128:SHARE], right], axis=1)
    power = jnp.concatenate([rough_power, fine_power, jnp.zeros((40, 1), F32)], axis=0)
    return jnp.concatenate([both[:, 0:128], tail], axis=0), power


def decoded_pool(block, unit):
    tail = jnp.concatenate([block[88:136, 0:64], block[88:128, 64:128]], axis=0)
    both = jnp.concatenate([block[0:88], tail], axis=1) * unit[0:88]
    return both[0:ROWS], both[ROWS:88]


def decoded_rows(block, unit, count):
    rows = ROWS + 2 * count
    tail = block[rows : rows + rows // 2]
    tail = jnp.concatenate([tail[:, 0:64], tail[:, 64:128]], axis=0)
    both = jnp.concatenate([block[0:rows], tail], axis=1)
    fine = both[ROWS : ROWS + count] + both[ROWS + count : rows] * (1.0 / FINE)
    return both[0:ROWS] * unit[0:ROWS], fine * unit[ROWS : ROWS + count]


def as_row(column):
    return jnp.transpose(jnp.broadcast_to(column, (column.shape[0], 128)))[0:1]


def units_kernel(commitment, capacity, bus, out):
    values = commitment[...].astype(F32) * capacity[...]
    where = bus[...].astype(F32)
    blank = jnp.zeros((8, 128), F32)
    row = lax.broadcasted_iota(jnp.int32, (8, 128), 0)
    for part in range(4):
        blank = jnp.where(row == part, where[:, 128 * part : 128 * part + 128], blank)
    for dest in range(BUS_AXIS):
        for part in range(4):
            out[dest, 8 * part : 8 * part + 8, :] = values[:, 128 * part : 128 * part + 128]
        out[dest, 32:40, :] = blank


def packed_units(commitment, capacity, bus):
    return pl.pallas_call(
        units_kernel,
        out_shape=jax.ShapeDtypeStruct((BUS_AXIS, 40, 128), F32),
        compiler_params=pltpu.CompilerParams(vmem_limit_bytes=WIDE),
        name="units",
    )(commitment, capacity.reshape(1, 512), bus.reshape(1, 512))


def net_flow_kernel(parity, factors, load, keep, other, top, work):
    work[...] = dot_nt(factors[...], load[...])
    keep[...] = work[pl.ds(pl.multiple_of(parity[0] * SHARE, SHARE), SHARE), :]
    part = work[pl.ds(pl.multiple_of((1 - parity[0]) * SHARE, SHARE), SHARE), :]
    other[...] = part
    top[0] = jnp.broadcast_to(as_row(jnp.max(jnp.abs(part), axis=1, keepdims=True)), (8, SHARE))


def net_flow(parity, factors, load):
    half = pltpu.HBM((PAIRS * SHARE, COLS), F32)
    return pl.pallas_call(
        net_flow_kernel,
        grid=(PAIRS,),
        in_specs=[
            pl.BlockSpec(memory_space=pltpu.SMEM),
            pl.BlockSpec((2 * SHARE, BUSES), lambda j: (j, 0)),
            pl.BlockSpec((COLS, BUSES), lambda j: (0, 0)),
        ],
        out_specs=[pl.BlockSpec((SHARE, COLS), lambda j: (j, 0))] * 2 + [pl.BlockSpec((1, 8, SHARE), lambda j: (j, 0, 0))],
        out_shape=[half, half, pltpu.HBM((PAIRS, 8, SHARE), F32)],
        scratch_shapes=[pltpu.VMEM((2 * SHARE, COLS), F32)],
        compiler_params=pltpu.CompilerParams(vmem_limit_bytes=WIDE),
        name="net_flow",
    )(parity, factors, load)


def hour_levels(level):
    column = lax.broadcasted_iota(jnp.int32, (HOURS, COLS), 1)
    row = lax.broadcasted_iota(jnp.int32, (HOURS, COLS), 0)
    here = jnp.bitwise_and(column, HOURS - 1) == row
    first, second = [jnp.where(here, piece.astype(F32), 0.0) for piece in split2(level)]
    ones = jnp.where(row < 2, 1.0, 0.0)
    return jnp.concatenate([first, second, first, ones], axis=0).astype(BF16)


def capacity_part(factors, capacity):
    half = BUSES // 2
    given = jnp.transpose(dot_nt(factors[:, 0:half], capacity[:, 0:half]) + dot_nt(factors[:, half:], capacity[:, half:]))
    return given[0:8] + given[8:16]


def left_side(given, high, low, value):
    first, second = [piece.astype(F32) for piece in split2(given)]
    row = lax.broadcasted_iota(jnp.int32, (8, SHARE), 0)
    constant = jnp.where(row == 0, high, jnp.where(row == 1, low, 0.0))
    both = jnp.transpose(jnp.concatenate([first, first, second, constant, jnp.broadcast_to(value, (8, SHARE))], axis=0))
    return both[:, 0:32].astype(BF16), both[:, 32:33]


def send_kernel(place, units, factors, level, other, top, capacity_out, send_a, send_b, stage, tops, powers, semaphores):
    loads = (
        pltpu.make_async_copy(other, stage, semaphores.at[0]),
        pltpu.make_async_copy(top, tops, semaphores.at[1]),
    )
    for load in loads:
        load.start()
    parity = jnp.bitwise_and(place[0], 1)
    first = (place[0] * BUSES).astype(F32)
    lows = lax.broadcasted_iota(jnp.int32, (128, 512), 0).astype(F32)
    totals = [jnp.zeros((128, 128), F32), jnp.zeros((128, 128), F32)]
    for src in range(BUS_AXIS):
        values = jnp.concatenate([units[src, 8 * part : 8 * part + 8, :] for part in range(4)], axis=1)
        local = jnp.concatenate([units[src, 32 + part : 33 + part, :] for part in range(4)], axis=1) - first
        high = jnp.floor(local * (1.0 / 128.0))
        low = local - high * 128.0
        pieces = [piece.astype(F32) for piece in split2(values)]
        work = [jnp.where(high == float(block), piece, 0.0) for piece in pieces for block in range(8)]
        match = jnp.where(lows == low, 1.0, 0.0).astype(BF16)
        totals[src % 2] = totals[src % 2] + dot_nt(jnp.concatenate(work, axis=0).astype(BF16), match)
    total = totals[0] + totals[1]
    total = total[0:64] + total[64:128]
    capacity = jnp.concatenate([total[8 * block : 8 * block + 8] for block in range(8)], axis=1)
    capacity = jnp.concatenate(split2(capacity), axis=0)
    capacity_out[...] = capacity.astype(F32)
    right = hour_levels(level[0:1, :])
    most = jnp.max(jnp.abs(level[0:1, :]), axis=1, keepdims=True)
    powers[...] = jnp.zeros_like(powers)
    for load in loads:
        load.wait()
    for pair in range(PAIRS):
        row = pl.multiple_of((2 * pair + 1 - parity) * SHARE, SHARE)
        given = capacity_part(factors[pl.ds(row, SHARE), :], capacity)
        power = power_of(tops[pair, 0:1, :] + jnp.max(jnp.abs(given), axis=0, keepdims=True) * most)
        powers[pair : pair + 1, 0:SHARE] = power
        unit = jnp.exp2(power * -0.125) * CODE
        left, unit = left_side(given * unit, OFFSET - 0.5, 0.5, unit)
        for index, out in enumerate((send_a, send_b)):
            for start in range(0, HALF, 32):
                some = slice(index * HALF + start, index * HALF + start + 32)
                rows = slice(pair * SHARE + some.start, pair * SHARE + some.stop)
                code = wrapped(dot_nn(left[some], right) - stage[rows, :] * unit[some])
                out[pair * HALF + start : pair * HALF + start + 32, :] = code
    for out in (send_a, send_b):
        out[PAIRS * HALF : PAIRS * HALF + 8, :] = powers[...].astype(jnp.int32).astype(jnp.int16)


def sent_flow(place, units, factors, level, other, top):
    whole = pl.BlockSpec(memory_space=pltpu.VMEM)
    anywhere = pl.BlockSpec(memory_space=pltpu.HBM)
    sent = jax.ShapeDtypeStruct((PAIRS * HALF + 8, COLS), jnp.int16)
    return pl.pallas_call(
        send_kernel,
        in_specs=[pl.BlockSpec(memory_space=pltpu.SMEM), whole, whole, whole, anywhere, anywhere],
        out_specs=[whole, whole, whole],
        out_shape=[pltpu.VMEM((2 * HOURS, BUSES), F32), sent, sent],
        scratch_shapes=[
            pltpu.VMEM((PAIRS * SHARE, COLS), F32),
            pltpu.VMEM((PAIRS, 8, SHARE), F32),
            pltpu.VMEM((8, COLS), F32),
            pltpu.SemaphoreType.DMA((2,)),
        ],
        compiler_params=pltpu.CompilerParams(vmem_limit_bytes=VMEM),
        name="sent_flow",
    )(place, near(units), factors, near(level), far(other), far(top))


def kept_kernel(place, capacity, factors, net, level, out, top):
    side = 2 * pl.program_id(0) + jnp.bitwise_and(place[0], 1)
    rows = pl.ds(pl.multiple_of(side * SHARE, SHARE), SHARE)
    given = capacity_part(factors[rows, :], capacity[...].astype(BF16))
    left, _ = left_side(given, 0.0, 0.0, given[0:1])
    part = dot_nn(left, hour_levels(level[0:1, :])) - net[...]
    out[...] = part
    top[0] = jnp.broadcast_to(as_row(jnp.max(jnp.abs(part), axis=1, keepdims=True)), (8, SHARE))


def kept_flow(place, capacity, factors, net, level):
    whole = pl.BlockSpec(memory_space=pltpu.VMEM)
    return pl.pallas_call(
        kept_kernel,
        grid=(PAIRS,),
        in_specs=[
            pl.BlockSpec(memory_space=pltpu.SMEM),
            whole,
            whole,
            pl.BlockSpec((SHARE, COLS), lambda j: (j, 0)),
            whole,
        ],
        out_specs=[pl.BlockSpec((SHARE, COLS), lambda j: (j, 0)), pl.BlockSpec((1, 8, SHARE), lambda j: (j, 0, 0))],
        out_shape=[
            pltpu.VMEM((PAIRS * SHARE, COLS), F32),
            pltpu.VMEM((PAIRS, 8, SHARE), F32),
        ],
        compiler_params=pltpu.CompilerParams(vmem_limit_bytes=MIDDLE),
        name="kept_flow",
    )(place, near(capacity), factors, net, near(level))


def pair_kernel(part, top, code_a, code_b, power_a, power_b, coded):
    here = lax.broadcasted_iota(jnp.int32, (8, 256), 0) == pl.program_id(0)
    lane = lax.broadcasted_iota(jnp.int32, (1, 256), 1)
    rows = [
        jnp.sum(jnp.where(here, from_code(power[:, 0:256]), 0.0), axis=0, keepdims=True) for power in (power_a, power_b)
    ]
    unit = unit_of(jnp.where(lane < HALF, rows[0], rows[1]))[:, 0:SHARE]
    power = power_of(top[0, 0:1, :] + unit * CODE)
    again = jnp.exp2(power * -0.125) * CODE
    scales = [jnp.broadcast_to(scale, (8, SHARE)) for scale in (unit * again, again)]
    scales = jnp.transpose(jnp.concatenate(scales, axis=0))
    for index, code in enumerate((code_a, code_b)):
        for start in range(0, HALF, 32):
            some = slice(index * HALF + start, index * HALF + start + 32)
            value = part[some, :] * scales[some, 8:9] + OFFSET
            coded[0, some, :] = wrapped(value + from_code(code[start : start + 32, :]) * scales[some, 0:1])
    across = jnp.concatenate([jnp.broadcast_to(power, (8, SHARE)), jnp.zeros((8, COLS - SHARE), F32)], axis=1)
    coded[0, SHARE : SHARE + 8, :] = across.astype(jnp.int32).astype(jnp.int16)


def pair_flow(part, top, code_a, code_b):
    lines = pl.BlockSpec((HALF, COLS), lambda j: (j, 0))
    tail = pl.BlockSpec((8, COLS), lambda j: (PAIRS * HALF // 8, 0))
    return pl.pallas_call(
        pair_kernel,
        grid=(PAIRS,),
        in_specs=[
            pl.BlockSpec((SHARE, COLS), lambda j: (j, 0)),
            pl.BlockSpec((1, 8, SHARE), lambda j: (j, 0, 0)),
            lines,
            lines,
            tail,
            tail,
        ],
        out_specs=pl.BlockSpec((1, SHARE + 8, COLS), lambda j: (j, 0, 0)),
        out_shape=pltpu.HBM((PAIRS, SHARE + 8, COLS), jnp.int16),
        compiler_params=pltpu.CompilerParams(vmem_limit_bytes=VMEM),
        name="pair_flow",
    )(part, top, code_a, code_b, code_a, code_b)


def excess_kernel(received, limit, rows, current, target, out, coded, pick, pushes, squares, pushed, semaphores):
    loads = [pltpu.make_async_copy(received.at[src], coded.at[src], semaphores.at[src]) for src in range(PAIRS)]
    for load in loads:
        load.start()
    level = rows[0:1, :]
    weight = rows[1:2, :]
    cluster = rows[2:3, :]
    column = lax.broadcasted_iota(jnp.int32, (1, COLS), 1)
    hour = jnp.bitwise_and(column, HOURS - 1)
    key = cluster * float(HOURS) + hour.astype(F32)
    for owner in range(SCEN_AXIS):
        inner = lax.broadcasted_iota(jnp.int32, (ROWS, COLS), 0)
        mine = (jnp.right_shift(inner, 3) * SCEN_AXIS + owner) * HOURS + jnp.bitwise_and(inner, HOURS - 1)
        pick[owner * ROWS : owner * ROWS + ROWS, :] = jnp.where(mine.astype(F32) == key, 1.0, 0.0).astype(BF16)
    row = lax.broadcasted_iota(jnp.int32, (128, COLS), 0)
    inner = jnp.bitwise_and(row, 15)
    owner = jnp.right_shift(row, 4)
    mine = jnp.where(inner < 8, inner * SCEN_AXIS + owner, owner * OWNED + inner - 8)
    pick[COLS : COLS + 128, :] = jnp.where(mine.astype(F32) == cluster, 1.0, 0.0).astype(BF16)
    scaled = level * weight
    half = 0.5 * weight
    for load in loads:
        load.wait()
    power = jnp.concatenate([from_code(coded[src, SHARE : SHARE + 8, 0:SHARE])[0:1] for src in range(PAIRS)] * 2, axis=0)
    unit = unit_of(jnp.transpose(power))
    for start in range(0, SHARE, 32):
        some = slice(start, start + 32)
        flow = from_code(coded[0, some, :]) * unit[some, 0:1]
        for src in range(1, PAIRS):
            flow = flow + from_code(coded[src, some, :]) * unit[some, src : src + 1]
        edge = limit[some, 0:1]
        excess = flow - jnp.clip(flow, -edge, edge)
        for out_ref, value in ((pushes, excess * scaled), (squares, excess * excess * half)):
            out_ref[some, 0:COLS], out_ref[some, COLS:] = split2(value)
    twice = pick[0:COLS, :]
    pushed[...] = dot_nt(jnp.concatenate([twice, twice], axis=1), pushes[...])
    twice = pick[COLS:, :]
    pooled = dot_nt(jnp.concatenate([twice, twice], axis=1), squares[...])
    lane = lax.broadcasted_iota(jnp.int32, (128, 128), 1)
    last = lax.broadcasted_iota(jnp.int32, (8, SHARE), 0)
    table = jnp.zeros((128, 128), F32)
    blocks = []
    for dest in range(SCEN_AXIS):
        given = jnp.where(last == 0, current[dest : dest + 1, :], jnp.where(last == 1, target[dest : dest + 1, 0:1], 0.0))
        block, power = coded_pool(
            pushed[dest * ROWS : dest * ROWS + ROWS, :],
            jnp.concatenate([pooled[dest * 16 : dest * 16 + 16], given], axis=0),
        )
        table = jnp.where(lane == dest, power, table)
        out[dest, 0:128, :] = block[0:128].astype(jnp.int32).astype(jnp.int16)
        blocks.append(block[128:136])
    table = jnp.transpose(table)
    for dest in range(SCEN_AXIS):
        tail = jnp.broadcast_to(table[dest : dest + 1], (8, 128))
        out[dest, 128:144, :] = jnp.concatenate([blocks[dest], tail], axis=0).astype(jnp.int32).astype(jnp.int16)


def excess_sums(received, limit, rows, current, target):
    return pl.pallas_call(
        excess_kernel,
        in_specs=[pl.BlockSpec(memory_space=pltpu.HBM)] + [pl.BlockSpec(memory_space=pltpu.VMEM)] * 4,
        out_specs=pl.BlockSpec(memory_space=pltpu.VMEM),
        out_shape=pltpu.VMEM((SCEN_AXIS, POOLED, 128), jnp.int16),
        scratch_shapes=[
            pltpu.VMEM((PAIRS, SHARE + 8, COLS), jnp.int16),
            pltpu.VMEM((COLS + 128, COLS), BF16),
            pltpu.VMEM((SHARE, 2 * COLS), BF16),
            pltpu.VMEM((SHARE, 2 * COLS), BF16),
            pltpu.VMEM((COLS, SHARE), F32),
            pltpu.SemaphoreType.DMA((PAIRS,)),
        ],
        compiler_params=pltpu.CompilerParams(vmem_limit_bytes=VMEM),
        name="excess_sums",
    )(received, near(limit), near(rows), near(current), near(target))


def update_kernel(sums, current, target, out):
    tables = jnp.concatenate([from_code(sums[src, POOLED - 16 : POOLED, :])[15:16] for src in range(SCEN_AXIS)], axis=0)
    units = unit_of(jnp.transpose(tables))
    pushed = jnp.zeros((ROWS, SHARE), F32)
    pooled = jnp.zeros((16, SHARE), F32)
    given = []
    for src in range(SCEN_AXIS):
        rough, fine = decoded_pool(from_code(sums[src]), units[:, src : src + 1])
        pushed = pushed + rough
        pooled = pooled + fine[0:16]
        given.append(fine[16:24])
    spread = jnp.concatenate([part[0:1] for part in given], axis=0)
    spread_target = jnp.concatenate([part[1:2, 0:1] for part in given], axis=0)
    chosen = jnp.maximum(spread + STEP * (pooled[0:8] - spread_target), 0.0)
    owned = jnp.maximum(current[...] + STEP * (pooled[8:16] - target[:, 0:1]), 0.0)
    wide = jnp.concatenate([pushed[8 * i : 8 * i + 8] * chosen[i : i + 1] for i in range(OWNED)], axis=0)
    block, power = coded_rows(wide, owned)
    tail = jnp.broadcast_to(as_row(power), (8, 128))
    block = jnp.concatenate([block, tail], axis=0).astype(jnp.int32).astype(jnp.int16)
    for dest in range(BUS_AXIS):
        out[dest] = block


def updated(sums, current, target):
    return pl.pallas_call(
        update_kernel,
        in_specs=[pl.BlockSpec(memory_space=pltpu.VMEM)] * 3,
        out_specs=pl.BlockSpec(memory_space=pltpu.VMEM),
        out_shape=jax.ShapeDtypeStruct((BUS_AXIS, UPDATED, 128), jnp.int16),
        compiler_params=pltpu.CompilerParams(vmem_limit_bytes=VMEM),
        name="update",
    )(near(sums), near(current), near(target))


def slopes_kernel(packed, factors, slopes, duals):
    tables = jnp.concatenate([from_code(packed[src, UPDATED - 16 : UPDATED, :])[15:16] for src in range(BUS_AXIS)], axis=0)
    units = unit_of(jnp.transpose(tables))
    total = jnp.zeros((2 * ROWS, BUSES), F32)
    for src in range(BUS_AXIS):
        wide, duals[src] = decoded_rows(from_code(packed[src]), units[:, src : src + 1], 8)
        pieces = jnp.concatenate(split2(wide), axis=0)
        total = total + dot_nn(pieces, factors[src * SHARE : src * SHARE + SHARE, :])
    slopes[...] = total[0:ROWS] + total[ROWS:]


def slopes_of(packed, factors):
    return pl.pallas_call(
        slopes_kernel,
        in_specs=[pl.BlockSpec(memory_space=pltpu.VMEM)] * 2,
        out_specs=[pl.BlockSpec(memory_space=pltpu.VMEM)] * 2,
        out_shape=[
            jax.ShapeDtypeStruct((ROWS, BUSES), F32),
            jax.ShapeDtypeStruct((BUS_AXIS, 8, SHARE), F32),
        ],
        compiler_params=pltpu.CompilerParams(vmem_limit_bytes=VMEM),
        name="slopes",
    )(near(packed), factors)


NEAR_A = [(i, i ^ 1) for i in range(BUS_AXIS)]
NEAR_B = [(i, (i + 1 if i % 2 else i - 1) % BUS_AXIS) for i in range(BUS_AXIS)]
SAME_PARITY = [list(range(0, BUS_AXIS, 2)), list(range(1, BUS_AXIS, 2))]


def exchange(tiles, axis):
    return lax.all_to_all(tiles, axis, 0, 0, tiled=True)


def far(x):
    return pltpu.with_memory_space_constraint(x, pltpu.HBM)


def near(x):
    return pltpu.with_memory_space_constraint(x, pltpu.VMEM)


def per_device(
    shift_factors,
    net_load,
    dispatch_level,
    scenario_weight,
    cluster_id,
    commitment,
    unit_capacity,
    unit_bus,
    line_limit,
    multipliers,
    penalty_target,
):
    place = lax.axis_index("bus")
    factors = near(shift_factors)
    units = exchange(packed_units(commitment, unit_capacity, unit_bus), "bus")
    parity = jnp.bitwise_and(place, 1)
    keep, other, top = net_flow(parity.reshape(1), shift_factors, net_load.reshape(COLS, BUSES))
    keep, dispatch_level, scenario_weight, cluster_id = lax.optimization_barrier(
        (keep, dispatch_level, scenario_weight, cluster_id)
    )
    rows = jnp.stack(
        [
            dispatch_level.reshape(COLS),
            jnp.repeat(scenario_weight, HOURS),
            jnp.repeat(cluster_id[:, 0].astype(F32), HOURS),
        ],
        axis=0,
    )
    capacity, send_a, send_b = sent_flow(place.reshape(1), units, factors, rows, other, top)
    code_a = lax.ppermute(send_a, "bus", NEAR_A)
    code_b = lax.ppermute(send_b, "bus", NEAR_B)
    part, top = kept_flow(place.reshape(1), capacity, factors, keep, rows)
    coded = pair_flow(part, top, code_a, code_b)
    received = lax.all_to_all(coded, "bus", 0, 0, axis_index_groups=SAME_PARITY, tiled=True)

    limit = lax.dynamic_slice_in_dim(line_limit, place * SHARE, SHARE, 0).reshape(SHARE, 1)
    current = lax.dynamic_slice_in_dim(multipliers, place * SHARE, SHARE, 1)
    target = penalty_target.reshape(OWNED, 1)
    sums = exchange(excess_sums(received, limit, rows, current, target), "scen")
    packed = exchange(updated(sums, current, target), "bus")
    slopes, duals = slopes_of(packed, factors)
    slopes = exchange(slopes.reshape(LINE_AXIS, HOURS, BUSES), "line")
    dual_out = jnp.moveaxis(duals, 0, 1).reshape(OWNED, LINES)
    return dual_out, jnp.sum(slopes, axis=0, keepdims=True)


def solution(mesh):
    placed = (
        P("line", "bus"),
        P("scen", None, "bus"),
        P("scen", None),
        P("scen"),
        P("scen", None),
        P(None, "bus"),
        P("bus"),
        P("bus"),
        P("line"),
        P("scen", "line"),
        P("scen"),
    )

    return jax.shard_map(
        per_device,
        mesh=mesh,
        in_specs=placed,
        out_specs=(P("scen", "line"), P(("line", "scen"), None, "bus")),
        check_vma=False,
    )
```

```python
import jax
import jax.numpy as jnp
from jax import lax
from jax.experimental import pallas as pl
from jax.experimental.pallas import tpu as pltpu
from jax.sharding import PartitionSpec as P


BUS_AXIS = 8
LINE_AXIS = 8
SCEN_AXIS = 8
LINES = 1536
SHARE = LINES // BUS_AXIS
HALF = SHARE // 2
PAIRS = BUS_AXIS // 2
BUSES = 1024
SCEN = 64
HOURS = 8
COLS = SCEN * HOURS
OWNED = 8
ROWS = OWNED * HOURS
STEP = 0.1
CODE = 32000.0
FINE = 60000.0
OFFSET = 65536.5
POOLED = 144
UPDATED = 128
VMEM = 20 * 1024 * 1024
WIDE = 56 * 1024 * 1024
MIDDLE = 50 * 1024 * 1024

F32 = jnp.float32
BF16 = jnp.bfloat16


def dot_nt(a, b):
    return lax.dot_general(a, b, (((1,), (1,)), ((), ())), preferred_element_type=F32)


def dot_nn(a, b):
    return lax.dot_general(a, b, (((1,), (0,)), ((), ())), preferred_element_type=F32)


def split2(x):
    high = x.astype(BF16)
    return high, (x - high.astype(F32)).astype(BF16)


def power_of(top):
    return jnp.ceil(jnp.log2(jnp.maximum(top, 1e-30)) * 8.0)


def powers_of(part):
    return power_of(jnp.max(jnp.abs(part), axis=1, keepdims=True))


def rounded(x):
    return jnp.floor(x + 0.5)


def wrapped(x):
    return x.astype(jnp.int32).astype(jnp.int16)


def from_code(code):
    return code.astype(jnp.int32).astype(F32)


def unit_of(power):
    return jnp.exp2(power * 0.125) * (1.0 / CODE)


def coded_rows(rough, fine):
    rough_power = powers_of(rough)
    fine_power = powers_of(fine)
    rough = rounded(rough * (jnp.exp2(rough_power * -0.125) * CODE))
    fine = fine * (jnp.exp2(fine_power * -0.125) * CODE)
    high = rounded(fine)
    both = jnp.concatenate([rough, high, rounded((fine - high) * FINE)], axis=0)
    half = both.shape[0] // 2
    tail = jnp.concatenate([both[0:half, 128:SHARE], both[half:, 128:SHARE]], axis=1)
    blank = jnp.zeros((128 - rough_power.shape[0] - fine_power.shape[0], 1), F32)
    return jnp.concatenate([both[:, 0:128], tail], axis=0), jnp.concatenate([rough_power, fine_power, blank], axis=0)


def coded_pool(rough, fine):
    rough_power = powers_of(rough)
    fine_power = powers_of(fine)
    scaled = [part * (jnp.exp2(power * -0.125) * CODE) for part, power in ((rough, rough_power), (fine, fine_power))]
    both = rounded(jnp.concatenate(scaled, axis=0))
    right = jnp.concatenate([both[48:88, 128:SHARE], jnp.zeros((8, 64), F32)], axis=0)
    tail = jnp.concatenate([both[0:48, 128:SHARE], right], axis=1)
    power = jnp.concatenate([rough_power, fine_power, jnp.zeros((40, 1), F32)], axis=0)
    return jnp.concatenate([both[:, 0:128], tail], axis=0), power


def decoded_pool(block, unit):
    tail = jnp.concatenate([block[88:136, 0:64], block[88:128, 64:128]], axis=0)
    both = jnp.concatenate([block[0:88], tail], axis=1) * unit[0:88]
    return both[0:ROWS], both[ROWS:88]


def decoded_rows(block, unit, count):
    rows = ROWS + 2 * count
    tail = block[rows : rows + rows // 2]
    tail = jnp.concatenate([tail[:, 0:64], tail[:, 64:128]], axis=0)
    both = jnp.concatenate([block[0:rows], tail], axis=1)
    fine = both[ROWS : ROWS + count] + both[ROWS + count : rows] * (1.0 / FINE)
    return both[0:ROWS] * unit[0:ROWS], fine * unit[ROWS : ROWS + count]


def as_row(column):
    return jnp.transpose(jnp.broadcast_to(column, (column.shape[0], 128)))[0:1]


def units_kernel(commitment, capacity, bus, out):
    values = commitment[...].astype(F32) * capacity[...]
    where = bus[...].astype(F32)
    blank = jnp.zeros((8, 128), F32)
    row = lax.broadcasted_iota(jnp.int32, (8, 128), 0)
    for part in range(4):
        blank = jnp.where(row == part, where[:, 128 * part : 128 * part + 128], blank)
    for dest in range(BUS_AXIS):
        for part in range(4):
            out[dest, 8 * part : 8 * part + 8, :] = values[:, 128 * part : 128 * part + 128]
        out[dest, 32:40, :] = blank


def packed_units(commitment, capacity, bus):
    return pl.pallas_call(
        units_kernel,
        out_shape=jax.ShapeDtypeStruct((BUS_AXIS, 40, 128), F32),
        compiler_params=pltpu.CompilerParams(vmem_limit_bytes=WIDE),
        name="units",
    )(commitment, capacity.reshape(1, 512), bus.reshape(1, 512))


def net_flow_kernel(parity, factors, load, keep, other, top, work):
    work[...] = dot_nt(factors[...], load[...])
    keep[...] = work[pl.ds(pl.multiple_of(parity[0] * SHARE, SHARE), SHARE), :]
    part = work[pl.ds(pl.multiple_of((1 - parity[0]) * SHARE, SHARE), SHARE), :]
    other[...] = part
    top[0] = jnp.broadcast_to(as_row(jnp.max(jnp.abs(part), axis=1, keepdims=True)), (8, SHARE))


def net_flow(parity, factors, load):
    half = pltpu.HBM((PAIRS * SHARE, COLS), F32)
    return pl.pallas_call(
        net_flow_kernel,
        grid=(PAIRS,),
        in_specs=[
            pl.BlockSpec(memory_space=pltpu.SMEM),
            pl.BlockSpec((2 * SHARE, BUSES), lambda j: (j, 0)),
            pl.BlockSpec((COLS, BUSES), lambda j: (0, 0)),
        ],
        out_specs=[pl.BlockSpec((SHARE, COLS), lambda j: (j, 0))] * 2 + [pl.BlockSpec((1, 8, SHARE), lambda j: (j, 0, 0))],
        out_shape=[half, half, pltpu.HBM((PAIRS, 8, SHARE), F32)],
        scratch_shapes=[pltpu.VMEM((2 * SHARE, COLS), F32)],
        compiler_params=pltpu.CompilerParams(vmem_limit_bytes=WIDE),
        name="net_flow",
    )(parity, factors, load)


def hour_levels(level):
    column = lax.broadcasted_iota(jnp.int32, (HOURS, COLS), 1)
    row = lax.broadcasted_iota(jnp.int32, (HOURS, COLS), 0)
    here = jnp.bitwise_and(column, HOURS - 1) == row
    first, second = [jnp.where(here, piece.astype(F32), 0.0) for piece in split2(level)]
    ones = jnp.where(row < 2, 1.0, 0.0)
    return jnp.concatenate([first, second, first, ones], axis=0).astype(BF16)


def capacity_part(factors, capacity):
    half = BUSES // 2
    given = jnp.transpose(dot_nt(factors[:, 0:half], capacity[:, 0:half]) + dot_nt(factors[:, half:], capacity[:, half:]))
    return given[0:8] + given[8:16]


def left_side(given, high, low, value):
    first, second = [piece.astype(F32) for piece in split2(given)]
    row = lax.broadcasted_iota(jnp.int32, (8, SHARE), 0)
    constant = jnp.where(row == 0, high, jnp.where(row == 1, low, 0.0))
    both = jnp.transpose(jnp.concatenate([first, first, second, constant, jnp.broadcast_to(value, (8, SHARE))], axis=0))
    return both[:, 0:32].astype(BF16), both[:, 32:33]


def send_kernel(place, units, factors, level, other, top, capacity_out, send_a, send_b, stage, tops, powers, semaphores):
    loads = (
        pltpu.make_async_copy(other, stage, semaphores.at[0]),
        pltpu.make_async_copy(top, tops, semaphores.at[1]),
    )
    for load in loads:
        load.start()
    parity = jnp.bitwise_and(place[0], 1)
    first = (place[0] * BUSES).astype(F32)
    lows = lax.broadcasted_iota(jnp.int32, (128, 512), 0).astype(F32)
    totals = [jnp.zeros((128, 128), F32), jnp.zeros((128, 128), F32)]
    for src in range(BUS_AXIS):
        values = jnp.concatenate([units[src, 8 * part : 8 * part + 8, :] for part in range(4)], axis=1)
        local = jnp.concatenate([units[src, 32 + part : 33 + part, :] for part in range(4)], axis=1) - first
        high = jnp.floor(local * (1.0 / 128.0))
        low = local - high * 128.0
        pieces = [piece.astype(F32) for piece in split2(values)]
        work = [jnp.where(high == float(block), piece, 0.0) for piece in pieces for block in range(8)]
        match = jnp.where(lows == low, 1.0, 0.0).astype(BF16)
        totals[src % 2] = totals[src % 2] + dot_nt(jnp.concatenate(work, axis=0).astype(BF16), match)
    total = totals[0] + totals[1]
    total = total[0:64] + total[64:128]
    capacity = jnp.concatenate([total[8 * block : 8 * block + 8] for block in range(8)], axis=1)
    capacity = jnp.concatenate(split2(capacity), axis=0)
    capacity_out[...] = capacity.astype(F32)
    right = hour_levels(level[0:1, :])
    most = jnp.max(jnp.abs(level[0:1, :]), axis=1, keepdims=True)
    powers[...] = jnp.zeros_like(powers)
    for load in loads:
        load.wait()
    for pair in range(PAIRS):
        row = pl.multiple_of((2 * pair + 1 - parity) * SHARE, SHARE)
        given = capacity_part(factors[pl.ds(row, SHARE), :], capacity)
        power = power_of(tops[pair, 0:1, :] + jnp.max(jnp.abs(given), axis=0, keepdims=True) * most)
        powers[pair : pair + 1, 0:SHARE] = power
        unit = jnp.exp2(power * -0.125) * CODE
        left, unit = left_side(given * unit, OFFSET - 0.5, 0.5, unit)
        for index, out in enumerate((send_a, send_b)):
            for start in range(0, HALF, 32):
                some = slice(index * HALF + start, index * HALF + start + 32)
                rows = slice(pair * SHARE + some.start, pair * SHARE + some.stop)
                code = wrapped(dot_nn(left[some], right) - stage[rows, :] * unit[some])
                out[pair * HALF + start : pair * HALF + start + 32, :] = code
    for out in (send_a, send_b):
        out[PAIRS * HALF : PAIRS * HALF + 8, :] = powers[...].astype(jnp.int32).astype(jnp.int16)


def sent_flow(place, units, factors, level, other, top):
    whole = pl.BlockSpec(memory_space=pltpu.VMEM)
    anywhere = pl.BlockSpec(memory_space=pltpu.HBM)
    sent = jax.ShapeDtypeStruct((PAIRS * HALF + 8, COLS), jnp.int16)
    return pl.pallas_call(
        send_kernel,
        in_specs=[pl.BlockSpec(memory_space=pltpu.SMEM), whole, whole, whole, anywhere, anywhere],
        out_specs=[whole, whole, whole],
        out_shape=[pltpu.VMEM((2 * HOURS, BUSES), F32), sent, sent],
        scratch_shapes=[
            pltpu.VMEM((PAIRS * SHARE, COLS), F32),
            pltpu.VMEM((PAIRS, 8, SHARE), F32),
            pltpu.VMEM((8, COLS), F32),
            pltpu.SemaphoreType.DMA((2,)),
        ],
        compiler_params=pltpu.CompilerParams(vmem_limit_bytes=VMEM),
        name="sent_flow",
    )(place, near(units), factors, near(level), far(other), far(top))


def kept_kernel(place, capacity, factors, net, level, out, top):
    side = 2 * pl.program_id(0) + jnp.bitwise_and(place[0], 1)
    rows = pl.ds(pl.multiple_of(side * SHARE, SHARE), SHARE)
    given = capacity_part(factors[rows, :], capacity[...].astype(BF16))
    left, _ = left_side(given, 0.0, 0.0, given[0:1])
    part = dot_nn(left, hour_levels(level[0:1, :])) - net[...]
    out[...] = part
    top[0] = jnp.broadcast_to(as_row(jnp.max(jnp.abs(part), axis=1, keepdims=True)), (8, SHARE))


def kept_flow(place, capacity, factors, net, level):
    whole = pl.BlockSpec(memory_space=pltpu.VMEM)
    return pl.pallas_call(
        kept_kernel,
        grid=(PAIRS,),
        in_specs=[
            pl.BlockSpec(memory_space=pltpu.SMEM),
            whole,
            whole,
            pl.BlockSpec((SHARE, COLS), lambda j: (j, 0)),
            whole,
        ],
        out_specs=[pl.BlockSpec((SHARE, COLS), lambda j: (j, 0)), pl.BlockSpec((1, 8, SHARE), lambda j: (j, 0, 0))],
        out_shape=[
            pltpu.VMEM((PAIRS * SHARE, COLS), F32),
            pltpu.VMEM((PAIRS, 8, SHARE), F32),
        ],
        compiler_params=pltpu.CompilerParams(vmem_limit_bytes=MIDDLE),
        name="kept_flow",
    )(place, near(capacity), factors, net, near(level))


def pair_kernel(part, top, code_a, code_b, power_a, power_b, coded):
    lane = lax.broadcasted_iota(jnp.int32, (1, 256), 1)
    for owner in range(2):
        here = lax.broadcasted_iota(jnp.int32, (8, 256), 0) == 2 * pl.program_id(0) + owner
        rows = [
            jnp.sum(jnp.where(here, from_code(power[:, 0:256]), 0.0), axis=0, keepdims=True)
            for power in (power_a, power_b)
        ]
        unit = unit_of(jnp.where(lane < HALF, rows[0], rows[1]))[:, 0:SHARE]
        power = power_of(top[owner, 0:1, :] + unit * CODE)
        again = jnp.exp2(power * -0.125) * CODE
        scales = [jnp.broadcast_to(scale, (8, SHARE)) for scale in (unit * again, again)]
        scales = jnp.transpose(jnp.concatenate(scales, axis=0))
        for index, code in enumerate((code_a, code_b)):
            for start in range(0, HALF, 32):
                some = slice(index * HALF + start, index * HALF + start + 32)
                value = part[owner * SHARE + some.start : owner * SHARE + some.stop, :] * scales[some, 8:9] + OFFSET
                piece = from_code(code[owner * HALF + start : owner * HALF + start + 32, :])
                coded[owner, some, :] = wrapped(value + piece * scales[some, 0:1])
        across = jnp.concatenate([jnp.broadcast_to(power, (8, SHARE)), jnp.zeros((8, COLS - SHARE), F32)], axis=1)
        coded[owner, SHARE : SHARE + 8, :] = across.astype(jnp.int32).astype(jnp.int16)


def pair_flow(part, top, code_a, code_b):
    lines = pl.BlockSpec((2 * HALF, COLS), lambda j: (j, 0))
    tail = pl.BlockSpec((8, COLS), lambda j: (PAIRS * HALF // 8, 0))
    return pl.pallas_call(
        pair_kernel,
        grid=(PAIRS // 2,),
        in_specs=[
            pl.BlockSpec((2 * SHARE, COLS), lambda j: (j, 0)),
            pl.BlockSpec((2, 8, SHARE), lambda j: (j, 0, 0)),
            lines,
            lines,
            tail,
            tail,
        ],
        out_specs=pl.BlockSpec((2, SHARE + 8, COLS), lambda j: (j, 0, 0)),
        out_shape=pltpu.HBM((PAIRS, SHARE + 8, COLS), jnp.int16),
        compiler_params=pltpu.CompilerParams(vmem_limit_bytes=VMEM),
        name="pair_flow",
    )(part, top, code_a, code_b, code_a, code_b)


def excess_kernel(received, limit, rows, current, target, out, coded, pick, pushes, squares, pushed, semaphores):
    loads = [pltpu.make_async_copy(received.at[src], coded.at[src], semaphores.at[src]) for src in range(PAIRS)]
    for load in loads:
        load.start()
    level = rows[0:1, :]
    weight = rows[1:2, :]
    cluster = rows[2:3, :]
    column = lax.broadcasted_iota(jnp.int32, (1, COLS), 1)
    hour = jnp.bitwise_and(column, HOURS - 1)
    key = cluster * float(HOURS) + hour.astype(F32)
    for owner in range(SCEN_AXIS):
        inner = lax.broadcasted_iota(jnp.int32, (ROWS, COLS), 0)
        mine = (jnp.right_shift(inner, 3) * SCEN_AXIS + owner) * HOURS + jnp.bitwise_and(inner, HOURS - 1)
        pick[owner * ROWS : owner * ROWS + ROWS, :] = jnp.where(mine.astype(F32) == key, 1.0, 0.0).astype(BF16)
    row = lax.broadcasted_iota(jnp.int32, (128, COLS), 0)
    inner = jnp.bitwise_and(row, 15)
    owner = jnp.right_shift(row, 4)
    mine = jnp.where(inner < 8, inner * SCEN_AXIS + owner, owner * OWNED + inner - 8)
    pick[COLS : COLS + 128, :] = jnp.where(mine.astype(F32) == cluster, 1.0, 0.0).astype(BF16)
    scaled = level * weight
    half = 0.5 * weight
    for load in loads:
        load.wait()
    power = jnp.concatenate([from_code(coded[src, SHARE : SHARE + 8, 0:SHARE])[0:1] for src in range(PAIRS)] * 2, axis=0)
    unit = unit_of(jnp.transpose(power))
    for start in range(0, SHARE, 32):
        some = slice(start, start + 32)
        flow = from_code(coded[0, some, :]) * unit[some, 0:1]
        for src in range(1, PAIRS):
            flow = flow + from_code(coded[src, some, :]) * unit[some, src : src + 1]
        edge = limit[some, 0:1]
        excess = flow - jnp.clip(flow, -edge, edge)
        for out_ref, value in ((pushes, excess * scaled), (squares, excess * excess * half)):
            out_ref[some, 0:COLS], out_ref[some, COLS:] = split2(value)
    twice = pick[0:COLS, :]
    pushed[...] = dot_nt(jnp.concatenate([twice, twice], axis=1), pushes[...])
    twice = pick[COLS:, :]
    pooled = dot_nt(jnp.concatenate([twice, twice], axis=1), squares[...])
    lane = lax.broadcasted_iota(jnp.int32, (128, 128), 1)
    last = lax.broadcasted_iota(jnp.int32, (8, SHARE), 0)
    table = jnp.zeros((128, 128), F32)
    blocks = []
    for dest in range(SCEN_AXIS):
        given = jnp.where(last == 0, current[dest : dest + 1, :], jnp.where(last == 1, target[dest : dest + 1, 0:1], 0.0))
        block, power = coded_pool(
            pushed[dest * ROWS : dest * ROWS + ROWS, :],
            jnp.concatenate([pooled[dest * 16 : dest * 16 + 16], given], axis=0),
        )
        table = jnp.where(lane == dest, power, table)
        out[dest, 0:128, :] = block[0:128].astype(jnp.int32).astype(jnp.int16)
        blocks.append(block[128:136])
    table = jnp.transpose(table)
    for dest in range(SCEN_AXIS):
        tail = jnp.broadcast_to(table[dest : dest + 1], (8, 128))
        out[dest, 128:144, :] = jnp.concatenate([blocks[dest], tail], axis=0).astype(jnp.int32).astype(jnp.int16)


def excess_sums(received, limit, rows, current, target):
    return pl.pallas_call(
        excess_kernel,
        in_specs=[pl.BlockSpec(memory_space=pltpu.HBM)] + [pl.BlockSpec(memory_space=pltpu.VMEM)] * 4,
        out_specs=pl.BlockSpec(memory_space=pltpu.VMEM),
        out_shape=pltpu.VMEM((SCEN_AXIS, POOLED, 128), jnp.int16),
        scratch_shapes=[
            pltpu.VMEM((PAIRS, SHARE + 8, COLS), jnp.int16),
            pltpu.VMEM((COLS + 128, COLS), BF16),
            pltpu.VMEM((SHARE, 2 * COLS), BF16),
            pltpu.VMEM((SHARE, 2 * COLS), BF16),
            pltpu.VMEM((COLS, SHARE), F32),
            pltpu.SemaphoreType.DMA((PAIRS,)),
        ],
        compiler_params=pltpu.CompilerParams(vmem_limit_bytes=VMEM),
        name="excess_sums",
    )(received, near(limit), near(rows), near(current), near(target))


def update_kernel(sums, current, target, out):
    tables = jnp.concatenate([from_code(sums[src, POOLED - 16 : POOLED, :])[15:16] for src in range(SCEN_AXIS)], axis=0)
    units = unit_of(jnp.transpose(tables))
    pushed = jnp.zeros((ROWS, SHARE), F32)
    pooled = jnp.zeros((16, SHARE), F32)
    given = []
    for src in range(SCEN_AXIS):
        rough, fine = decoded_pool(from_code(sums[src]), units[:, src : src + 1])
        pushed = pushed + rough
        pooled = pooled + fine[0:16]
        given.append(fine[16:24])
    spread = jnp.concatenate([part[0:1] for part in given], axis=0)
    spread_target = jnp.concatenate([part[1:2, 0:1] for part in given], axis=0)
    chosen = jnp.maximum(spread + STEP * (pooled[0:8] - spread_target), 0.0)
    owned = jnp.maximum(current[...] + STEP * (pooled[8:16] - target[:, 0:1]), 0.0)
    wide = jnp.concatenate([pushed[8 * i : 8 * i + 8] * chosen[i : i + 1] for i in range(OWNED)], axis=0)
    block, power = coded_rows(wide, owned)
    tail = jnp.broadcast_to(as_row(power), (8, 128))
    block = jnp.concatenate([block, tail], axis=0).astype(jnp.int32).astype(jnp.int16)
    for dest in range(BUS_AXIS):
        out[dest] = block


def updated(sums, current, target):
    return pl.pallas_call(
        update_kernel,
        in_specs=[pl.BlockSpec(memory_space=pltpu.VMEM)] * 3,
        out_specs=pl.BlockSpec(memory_space=pltpu.VMEM),
        out_shape=jax.ShapeDtypeStruct((BUS_AXIS, UPDATED, 128), jnp.int16),
        compiler_params=pltpu.CompilerParams(vmem_limit_bytes=VMEM),
        name="update",
    )(near(sums), near(current), near(target))


def slopes_kernel(packed, factors, slopes, duals):
    tables = jnp.concatenate([from_code(packed[src, UPDATED - 16 : UPDATED, :])[15:16] for src in range(BUS_AXIS)], axis=0)
    units = unit_of(jnp.transpose(tables))
    total = jnp.zeros((2 * ROWS, BUSES), F32)
    for src in range(BUS_AXIS):
        wide, duals[src] = decoded_rows(from_code(packed[src]), units[:, src : src + 1], 8)
        pieces = jnp.concatenate(split2(wide), axis=0)
        total = total + dot_nn(pieces, factors[src * SHARE : src * SHARE + SHARE, :])
    slopes[...] = total[0:ROWS] + total[ROWS:]


def slopes_of(packed, factors):
    return pl.pallas_call(
        slopes_kernel,
        in_specs=[pl.BlockSpec(memory_space=pltpu.VMEM)] * 2,
        out_specs=[pl.BlockSpec(memory_space=pltpu.VMEM)] * 2,
        out_shape=[
            jax.ShapeDtypeStruct((ROWS, BUSES), F32),
            jax.ShapeDtypeStruct((BUS_AXIS, 8, SHARE), F32),
        ],
        compiler_params=pltpu.CompilerParams(vmem_limit_bytes=VMEM),
        name="slopes",
    )(near(packed), factors)


NEAR_A = [(i, i ^ 1) for i in range(BUS_AXIS)]
NEAR_B = [(i, (i + 1 if i % 2 else i - 1) % BUS_AXIS) for i in range(BUS_AXIS)]
SAME_PARITY = [list(range(0, BUS_AXIS, 2)), list(range(1, BUS_AXIS, 2))]


def exchange(tiles, axis):
    return lax.all_to_all(tiles, axis, 0, 0, tiled=True)


def far(x):
    return pltpu.with_memory_space_constraint(x, pltpu.HBM)


def near(x):
    return pltpu.with_memory_space_constraint(x, pltpu.VMEM)


def per_device(
    shift_factors,
    net_load,
    dispatch_level,
    scenario_weight,
    cluster_id,
    commitment,
    unit_capacity,
    unit_bus,
    line_limit,
    multipliers,
    penalty_target,
):
    place = lax.axis_index("bus")
    factors = near(shift_factors)
    units = exchange(packed_units(commitment, unit_capacity, unit_bus), "bus")
    parity = jnp.bitwise_and(place, 1)
    keep, other, top = net_flow(parity.reshape(1), shift_factors, net_load.reshape(COLS, BUSES))
    keep, dispatch_level, scenario_weight, cluster_id = lax.optimization_barrier(
        (keep, dispatch_level, scenario_weight, cluster_id)
    )
    rows = jnp.stack(
        [
            dispatch_level.reshape(COLS),
            jnp.repeat(scenario_weight, HOURS),
            jnp.repeat(cluster_id[:, 0].astype(F32), HOURS),
        ],
        axis=0,
    )
    capacity, send_a, send_b = sent_flow(place.reshape(1), units, factors, rows, other, top)
    code_a = lax.ppermute(send_a, "bus", NEAR_A)
    code_b = lax.ppermute(send_b, "bus", NEAR_B)
    part, top = kept_flow(place.reshape(1), capacity, factors, keep, rows)
    coded = pair_flow(part, top, code_a, code_b)
    received = lax.all_to_all(coded, "bus", 0, 0, axis_index_groups=SAME_PARITY, tiled=True)

    limit = lax.dynamic_slice_in_dim(line_limit, place * SHARE, SHARE, 0).reshape(SHARE, 1)
    current = lax.dynamic_slice_in_dim(multipliers, place * SHARE, SHARE, 1)
    target = penalty_target.reshape(OWNED, 1)
    sums = exchange(excess_sums(received, limit, rows, current, target), "scen")
    packed = exchange(updated(sums, current, target), "bus")
    slopes, duals = slopes_of(packed, factors)
    slopes = exchange(slopes.reshape(LINE_AXIS, HOURS, BUSES), "line")
    dual_out = jnp.moveaxis(duals, 0, 1).reshape(OWNED, LINES)
    return dual_out, jnp.sum(slopes, axis=0, keepdims=True)


def solution(mesh):
    placed = (
        P("line", "bus"),
        P("scen", None, "bus"),
        P("scen", None),
        P("scen"),
        P("scen", None),
        P(None, "bus"),
        P("bus"),
        P("bus"),
        P("line"),
        P("scen", "line"),
        P("scen"),
    )

    return jax.shard_map(
        per_device,
        mesh=mesh,
        in_specs=placed,
        out_specs=(P("scen", "line"), P(("line", "scen"), None, "bus")),
        check_vma=False,
    )
```
